32 devices in a mesh: section: 8 (over z, x), expert: 4 (over y, core).
Axes of the slice: x: 2, y: 2, z: 4, core: 2. Of those that a mesh axis runs over, the one named last changes fastest.
Arguments:
- entering: bfloat16 [2, 2, 128, 3584], P(None, None, 'expert'), may hold values from -6 to 6
- norm_gain: float32 [8, 3584], P('section'), may hold values from 0.5 to 1.5
- w_gate: bfloat16 [8, 3584, 2048], P('section', None, 'expert'), may hold values from -0.09375 to 0.09375
- w_up: bfloat16 [8, 3584, 2048], P('section', None, 'expert'), may hold values from -0.09375 to 0.09375
- w_down: bfloat16 [8, 2048, 3584], P('section', 'expert'), may hold values from -0.1875 to 0.1875
- route_ids: int32 [2, 2, 8, 128, 8], P(None, None, 'section', 'expert'), may hold values from 0 to 255, as said below
- route_scores: float32 [2, 2, 8, 128, 8], P(None, None, 'section', 'expert'), may hold values from 0.05 to 1
Outputs:
- leaving: bfloat16 [2, 2, 128, 3584], P(None, None, 'expert', 'section')
The draws below stay inside these ranges and needn't reach their ends.
Inputs may be any that keep to these rules, and one draw needn't show every extreme that they name: `route_ids`: A token's 8 ids are distinct. In every block of 32 tokens (one direction, micro-batch and layer), at most 2 tokens name any one expert below 2, and in every such block exactly 2 tokens name one of them.
All inputs are finite; a program needn't handle non-finite values.
Results may differ from the reference program's by a relative error of at most 0.0072.
Values may be sent and summed in bfloat16 or wider, within the bound.
No kernel may reach another device: no remote copies, remote signals or barrier semaphores. Data moves between devices by JAX's collectives and lax.ppermute only.
A program may use at most 64 MiB of HBM per device.

```python
import math
import jax
import jax.numpy as jnp
from jax import lax

D = 3584
EXP_HID = 1024
EXPERTS = 256
TOPK = 8
GROUP = 2
CAP = 2
MICRO = 2
TOK_DEV = 32
LAYERS = 8
EXP_WIN = 2
TOKENS = 128
N_EXPERT = 4


def draw_route_ids(key, part):
    blocks = 2 * MICRO * LAYERS * (TOKENS // TOK_DEV)
    keys = jax.random.split(jax.random.fold_in(key, 7), 5)
    counts = jax.random.randint(keys[0], (blocks, EXP_WIN), 0, CAP + 1)
    forced = jax.random.randint(keys[1], (blocks, 1), 0, EXP_WIN)
    counts = jnp.where(jnp.arange(EXP_WIN)[None, :] == forced, CAP, counts)
    noise = jax.random.randint(keys[2], (blocks, EXP_WIN, TOK_DEV), 0, 65536) * TOK_DEV + jnp.arange(TOK_DEV)
    order = jnp.argsort(noise, axis=-1, stable=True)
    ranks = jnp.argsort(order, axis=-1, stable=True)
    member = ranks < counts[:, :, None]
    others = EXPERTS - EXP_WIN
    scores = jax.random.randint(keys[3], (blocks * TOK_DEV, others), 0, 65536) * others + jnp.arange(others)
    picks = jnp.argsort(scores, axis=-1, stable=True)[:, :TOPK] + EXP_WIN
    rotate = jax.random.randint(keys[4], (blocks * TOK_DEV, 1), 0, TOPK)
    member_rows = jnp.transpose(member, (0, 2, 1)).reshape(blocks * TOK_DEV, EXP_WIN)
    places = jnp.arange(TOPK)[None, :]
    chosen = picks
    for expert in range(EXP_WIN):
        marked = (places == (rotate + expert) % TOPK) & member_rows[:, expert:expert + 1]
        chosen = jnp.where(marked, expert, chosen)
    return chosen.reshape(2, MICRO, LAYERS, TOKENS, TOPK).astype(jnp.int32)


def block_levels(own_key, extent, cuts, smallest, high):
    loudness = 1.0
    for position, blocks in cuts:
        steps = jax.random.uniform(jax.random.fold_in(jax.random.fold_in(own_key, 6), position), (blocks,), jnp.float32, smallest / len(cuts), high / len(cuts))
        loudness = loudness * jnp.repeat(jnp.exp(steps), extent[position] // blocks).reshape((-1,) + (1,) * (len(extent) - 1 - position))
    return loudness


def normal_values(key, dims, scale, limit, pieces=(), kind=jnp.bfloat16):
    level = block_levels(key, dims, pieces, -0.22, 0.18) if pieces else 1.0
    drawn = jax.random.normal(key, dims, jnp.float32) * scale * level
    return jnp.minimum(jnp.maximum(drawn, -limit), limit).astype(kind)


def setup_inputs(seed: int = 0) -> dict:
    key_of = jax.random.split(jax.random.key(seed), 8)
    entering = normal_values(key_of[0], (2, MICRO, TOKENS, D), 1.0, 6.0, ((2, 4),))
    norm_gain = jnp.clip(1.0 + 0.1 * jax.random.normal(key_of[1], (LAYERS, D), jnp.float32), 0.5, 1.5)
    w_gate = normal_values(key_of[2], (LAYERS, D, EXP_WIN * EXP_HID), D ** -0.5, 0.09375, ((0, 8), (2, 4)))
    w_up = normal_values(key_of[3], (LAYERS, D, EXP_WIN * EXP_HID), D ** -0.5, 0.09375, ((0, 8), (2, 4)))
    w_down = normal_values(key_of[4], (LAYERS, EXP_WIN * EXP_HID, D), EXP_HID ** -0.5, 0.1875, ((0, 8), (1, 4)))
    route_ids = draw_route_ids(jax.random.fold_in(key_of[7], 71), 0)
    route_scores = jnp.clip(jnp.exp(math.log(1.0) - 2.9957323 * jax.random.uniform(key_of[6], (2, MICRO, LAYERS, TOKENS, TOPK), jnp.float32) ** block_levels(key_of[6], (2, MICRO, LAYERS, TOKENS, TOPK), ((2, 8), (3, 4)), -0.2, 0.2)), 0.05, 1.0)
    return dict(entering=entering, norm_gain=norm_gain, w_gate=w_gate, w_up=w_up, w_down=w_down, route_ids=route_ids, route_scores=route_scores)


norm_eps = 1e-06
route_scale = 2.5

def slot_tables(ids, weights):
    window = N_EXPERT // GROUP
    hit = (ids[:, :, :, None] == jnp.arange(window, dtype=jnp.int32)).astype(jnp.float32)
    count = lax.optimization_barrier(jnp.sum(hit, axis=2))
    share = lax.optimization_barrier(jnp.sum(weights[:, :, :, None] * hit, axis=2))
    before = jnp.cumsum(count, axis=1) - count
    slots = jnp.arange(CAP, dtype=jnp.float32)
    place = jnp.transpose(count, (0, 2, 1))[:, :, None, :] * (jnp.transpose(before, (0, 2, 1))[:, :, None, :] == slots[None, None, :, None]).astype(jnp.float32)
    comb = place * jnp.transpose(share, (0, 2, 1))[:, :, None, :]
    return (place, comb)

def layer(x, gain, wg, wu, wd, ids, scores):
    window = N_EXPERT // GROUP
    hid = EXP_HID // GROUP
    blocks = N_EXPERT
    xf = x.astype(jnp.float32)
    h = (xf * lax.rsqrt(lax.optimization_barrier(jnp.mean(xf * xf, axis=-1, keepdims=True)) + norm_eps) * gain).astype(jnp.bfloat16)
    weights = route_scale * scores / lax.optimization_barrier(jnp.sum(scores, axis=-1, keepdims=True))
    hb = h.reshape(blocks, TOK_DEV, D)
    place, comb = slot_tables(ids.reshape(blocks, TOK_DEV, TOPK), weights.reshape(blocks, TOK_DEV, TOPK))
    rows = jnp.einsum('bect,btd->becd', place, hb.astype(jnp.float32)).astype(jnp.bfloat16)
    outs = []
    for e in range(window):
        flat = rows[:, e].reshape(blocks * CAP, D)
        total = jnp.zeros((blocks * CAP, D), jnp.float32)
        for j in range(GROUP):
            lo = (e * GROUP + j) * hid
            gate = jnp.dot(flat, wg[:, lo:lo + hid], preferred_element_type=jnp.float32)
            up = jnp.dot(flat, wu[:, lo:lo + hid], preferred_element_type=jnp.float32)
            act = (jax.nn.silu(gate) * up).astype(jnp.bfloat16)
            part = jnp.dot(act, wd[lo:lo + hid, :], preferred_element_type=jnp.float32).astype(jnp.bfloat16)
            total = total + part.astype(jnp.float32)
        outs.append(total.reshape(blocks, CAP, D))
    expert_out = jnp.stack(outs, axis=1)
    added = jnp.einsum('bect,becd->btd', comb, expert_out, precision=lax.Precision.HIGHEST)
    return (xf + added.reshape(TOKENS, D)).astype(jnp.bfloat16)

def run(x, norm_gain, w_gate, w_up, w_down, ids, scores, backward):

    def one(carry, items):
        gain, wg, wu, wd, idl, scl = items
        return (layer(carry, gain, wg, wu, wd, idl, scl), None)
    final, unused = lax.scan(one, x, (norm_gain, w_gate, w_up, w_down, ids, scores), reverse=backward)
    return final

def reference(entering, norm_gain, w_gate, w_up, w_down, route_ids, route_scores):
    results = []
    for direction in range(2):
        row = []
        for micro in range(MICRO):
            row.append(run(entering[direction, micro], norm_gain, w_gate, w_up, w_down, route_ids[direction, micro], route_scores[direction, micro], direction == 1))
        results.append(jnp.stack(row))
    return jnp.stack(results)
```

```python
import functools

import jax
import jax.numpy as jnp
from jax import lax
from jax.experimental import pallas as pl
from jax.experimental.pallas import tpu as pltpu
from jax.sharding import PartitionSpec as P

GROUP = 2
CAP = 2

norm_eps = 1e-06
route_scale = 2.5

F32 = jnp.float32
BF16 = jnp.bfloat16
LANES = 128
AXES = ("section", "expert")

VMEM = pltpu.VMEM
SMEM = pltpu.SMEM


def iota(shape, dim):
    return lax.broadcasted_iota(jnp.int32, shape, dim)


def mm(a, b):
    return jnp.dot(a, b, preferred_element_type=F32)


def route_kernel(me_ref, ids_ref, scores_ref, x_ref, *refs, tokens, window, slots):
    spread = len(refs) - 1
    outs, rows_ref = refs[:spread], refs[spread]
    count, width = x_ref.shape
    ids = ids_ref[...]
    scores = scores_ref[...]
    weights = route_scale * scores / jnp.sum(scores, axis=-1, keepdims=True)
    place_i = iota((count, count), 0)
    place_j = iota((count, count), 1)
    block_of = lambda v: jnp.floor((v.astype(F32) + 0.5) * (1.0 / tokens))
    earlier = ((place_j < place_i) & (block_of(place_i) == block_of(place_j))).astype(BF16)
    lane = iota((count, LANES), 1)
    token_lane = iota((slots, count), 1).astype(F32)
    base = block_of(iota((count, 1), 0)) * CAP
    hits, shares = [], []
    stacked = jnp.zeros((count, LANES), F32)
    for e in range(window):
        same = ids == e
        hit = jnp.sum(jnp.where(same, 1.0, 0.0), axis=-1, keepdims=True)
        hits.append(hit)
        shares.append(jnp.sum(jnp.where(same, weights, 0.0), axis=-1, keepdims=True))
        stacked = jnp.where(lane == e, hit, stacked)
    before = mm(earlier, stacked.astype(BF16))
    x = x_ref[...]
    meta_lane = iota((slots, LANES), 1)
    for e in range(window):
        slot = (base + before[:, e:e + 1]).astype(jnp.int32)
        taken = jnp.where(lane == slot, hits[e], 0.0)
        pick = taken.T[:slots]
        token = jnp.sum(pick * token_lane + pick, axis=-1, keepdims=True) - 1.0
        w = jnp.sum((taken * shares[e]).T[:slots], axis=-1, keepdims=True)
        high = w.astype(BF16).astype(F32)
        mid = (w - high).astype(BF16).astype(F32)
        low = w - high - mid
        meta = jnp.where(meta_lane == 0, token, 0.0)
        meta = jnp.where(meta_lane == 1, high, meta)
        meta = jnp.where(meta_lane == 2, mid, meta)
        meta = jnp.where(meta_lane == 3, low, meta)
        rows_ref[e, :, :width] = mm(pick.astype(BF16), x).astype(BF16)
        rows_ref[e, :, width:] = meta.astype(BF16)
    me = me_ref[0]
    for k in range(spread):
        peer = lax.rem(me + k, spread)
        outs[k][...] = rows_ref[lax.div(peer, GROUP)]


def feed_forward(h, wg_ref, wu_ref, wd_ref):
    gate = mm(h, wg_ref[...])
    up = mm(h, wu_ref[...])
    act = (gate / (1.0 + jnp.exp(-gate)) * up).astype(BF16)
    return mm(act, wd_ref[...])


def first_kernel(me_ref, gain_ref, wg_ref, wu_ref, wd_ref, *refs, sections, feats):
    spread = len(refs) - 1
    ins, out_ref = refs[:spread], refs[spread]
    width = gain_ref.shape[1]
    slots = ins[0].shape[0]
    room = out_ref.shape[2] - feats
    x = jnp.concatenate([r[:, :width].astype(F32) for r in ins], axis=0)
    mean = jnp.mean(x * x, axis=-1, keepdims=True)
    h = (x * lax.rsqrt(mean + norm_eps) * gain_ref[...]).astype(BF16)
    part = feed_forward(h, wg_ref, wu_ref, wd_ref).astype(BF16)
    me = me_ref[0]
    for k in range(spread):
        block = lax.rem(me - k + spread, spread)
        meta = ins[k][:, width:width + room]
        for s in range(sections):
            out_ref[s * spread + block, :, :feats] = part[k * slots:(k + 1) * slots, s * feats:(s + 1) * feats]
            out_ref[s * spread + block, :, feats:] = meta


def round_kernel(gain_ref, wg_ref, wu_ref, wd_ref, in_ref, out_ref, last_ref, *, sections, feats):
    count, slots, padded = in_ref.shape
    spread = count // sections
    rows = spread * slots
    width = sections * feats
    pieces = []
    total = jnp.zeros((rows, 1), F32)
    for s in range(sections):
        piece = in_ref[s * spread:(s + 1) * spread, :, :].astype(F32).reshape(rows, padded)[:, :feats]
        total = total + jnp.sum(piece * piece, axis=-1, keepdims=True)
        pieces.append(piece)
    scale = lax.rsqrt(total * (1.0 / width) + norm_eps)
    gate = jnp.zeros((rows, wg_ref.shape[1]), F32)
    up = jnp.zeros((rows, wg_ref.shape[1]), F32)
    for s in range(sections):
        h = (pieces[s] * scale * gain_ref[s:s + 1, :]).astype(BF16)
        gate = gate + mm(h, wg_ref[s * feats:(s + 1) * feats, :])
        up = up + mm(h, wu_ref[s * feats:(s + 1) * feats, :])
    act = (gate / (1.0 + jnp.exp(-gate)) * up).astype(BF16)
    part = mm(act, wd_ref[...]).astype(BF16)
    for s in range(sections):
        piece = part[:, s * feats:(s + 1) * feats]
        for b in range(spread):
            out_ref[s * spread + b, :, :feats] = piece[b * slots:(b + 1) * slots]
            out_ref[s * spread + b, :, feats:] = jnp.zeros((slots, padded - feats), BF16)
    depth = in_ref[:spread, :, :].astype(F32).reshape(rows, padded)[:, feats:feats + 1]
    last_ref[0] = jnp.max(depth).astype(jnp.int32)


def apply_parts(step, parts, x, cols, rows_tab, feats):
    tokens, padded = x.shape
    count = parts.shape[0]
    chosen = (iota((tokens, count), 0).astype(F32) == rows_tab[0:1, :]) & (rows_tab[4:5, :] == step)
    added = jnp.zeros((tokens, padded), F32)
    for n in (1, 2, 3):
        added = added + mm(jnp.where(chosen, rows_tab[n:n + 1, :], 0.0).astype(BF16), parts)
    lane = iota((tokens, padded), 1)
    x = jnp.where(lane < feats, x.astype(F32) + added, 0.0).astype(BF16)
    pick = (iota((count, tokens), 1).astype(F32) == cols[:, 0:1]).astype(BF16)
    send = jnp.where(iota((count, padded), 1) == feats, cols[:, 5:6], mm(pick, x))
    return x, send.astype(BF16)


def table_kernel(x_ref, in_ref, x_out, send_out, cols_out, rows_out, *, sections, feats):
    count, slots, padded = in_ref.shape
    tokens = x_ref.shape[0]
    total = count * slots
    per = total // sections
    parts = in_ref[...].reshape(total, padded)
    meta = parts[:, feats:feats + 4].astype(F32)
    token = meta[:, 0:1]
    pick = (iota((total, tokens), 1).astype(F32) == token).astype(F32)
    hit = [jnp.minimum(jnp.sum(pick[l * per:(l + 1) * per], axis=0, keepdims=True), 1.0) for l in range(sections)]
    ahead, behind = [None] * sections, [None] * sections
    run_a = run_b = jnp.zeros((1, tokens), F32)
    for l in range(sections):
        ahead[l] = run_a
        run_a = run_a + hit[l]
        m = sections - 1 - l
        behind[m] = run_b
        run_b = run_b + hit[m]
    forward = iota((1, tokens), 1) < tokens // 2
    level = [
        jnp.sum(pick[l * per:(l + 1) * per] * jnp.where(forward, ahead[l], behind[l]), axis=-1, keepdims=True)
        for l in range(sections)
    ]
    level = jnp.concatenate(level, axis=0)
    depth = jnp.max(run_a)
    lane = iota((total, LANES), 1)
    cols = jnp.where(lane == 0, token, 0.0)
    for n in (1, 2, 3):
        cols = jnp.where(lane == n, meta[:, n:n + 1], cols)
    cols = jnp.where(lane == 4, level, cols)
    cols = jnp.where(lane == 5, depth, cols)
    rows_tab = cols.T[:8]
    cols_out[...] = cols
    rows_out[...] = rows_tab
    x, send = apply_parts(0.0, parts, x_ref[...], cols, rows_tab, feats)
    x_out[...] = x
    send_out[...] = send.reshape(count, slots, padded)


def update_kernel(step_ref, x_ref, in_ref, cols_ref, rows_ref, x_out, send_out, *, feats):
    count, slots, padded = in_ref.shape
    step = step_ref[0].astype(F32)
    parts = in_ref[...].reshape(count * slots, padded)
    x, send = apply_parts(step, parts, x_ref[...], cols_ref[...], rows_ref[...], feats)
    x_out[...] = x
    send_out[...] = send.reshape(count, slots, padded)


def call(kernel, out_shape, in_spaces, out_spaces, name, scratch=(), limit=None):
    spec = lambda space: pl.BlockSpec(memory_space=space)
    single = not isinstance(out_shape, (list, tuple))
    return pl.pallas_call(
        kernel,
        out_shape=out_shape,
        in_specs=[spec(s) for s in in_spaces],
        out_specs=spec(out_spaces[0]) if single else [spec(s) for s in out_spaces],
        scratch_shapes=list(scratch),
        compiler_params=pltpu.CompilerParams(vmem_limit_bytes=limit),
        name=name,
    )


def on_device(entering, norm_gain, w_gate, w_up, w_down, route_ids, route_scores):
    sections = lax.axis_size("section")
    spread = lax.axis_size("expert")
    section = lax.axis_index("section")
    peer = lax.axis_index("expert")
    window = spread // GROUP
    ways, micro, tokens, width = entering.shape
    everyone = ways * micro * tokens
    slots = ways * micro * CAP
    feats = width // sections
    padded = (feats // LANES + 1) * LANES
    devices = sections * spread
    topk = route_ids.shape[-1]

    wg, wu, wd = (w_gate[0], w_up[0], w_down[0])
    me = peer.astype(jnp.int32).reshape(1)
    flat = entering.reshape(everyone, width)
    sds = jax.ShapeDtypeStruct

    rows = call(
        functools.partial(route_kernel, tokens=tokens, window=window, slots=slots),
        [sds((slots, width + LANES), BF16)] * spread,
        [SMEM, VMEM, VMEM, VMEM],
        [VMEM] * spread,
        "route",
        scratch=[VMEM((window, slots, width + LANES), BF16)],
    )(me, route_ids.reshape(everyone, topk), route_scores.reshape(everyone, topk), flat)
    received = [rows[0]] + [
        lax.ppermute(rows[k], "expert", [(y, (y + k) % spread) for y in range(spread)]) for k in range(1, spread)
    ]
    message = sds((devices, slots, padded), BF16)
    swap = lambda v: lax.all_to_all(v, AXES, split_axis=0, concat_axis=0, tiled=True)
    parts = call(
        functools.partial(first_kernel, sections=sections, feats=feats),
        message,
        [SMEM] + [VMEM] * (4 + spread),
        [VMEM],
        "first",
    )(me, norm_gain, wg, wu, wd, *received)
    own = lax.dynamic_slice(flat, (0, section * feats), (everyone, feats))
    own = jnp.pad(own, ((0, 0), (0, padded - feats)))
    x, send, cols, rows_tab = call(
        functools.partial(table_kernel, sections=sections, feats=feats),
        [sds((everyone, padded), BF16), message, sds((devices * slots, LANES), F32), sds((8, devices * slots), F32)],
        [VMEM, VMEM],
        [VMEM] * 4,
        "table",
    )(own, swap(parts))
    gain = norm_gain.reshape(sections, feats)

    def more(carry):
        return carry[0] < carry[1]

    def turn(carry):
        step, unused, x, send = carry
        parts, last = call(
            functools.partial(round_kernel, sections=sections, feats=feats),
            [message, sds((1,), jnp.int32)],
            [VMEM] * 5,
            [VMEM, SMEM],
            "round",
        )(gain, wg, wu, wd, swap(send))
        x, send = call(
            functools.partial(update_kernel, feats=feats),
            [sds((everyone, padded), BF16), message],
            [SMEM] + [VMEM] * 4,
            [VMEM] * 2,
            "update",
        )(step.reshape(1), x, swap(parts), cols, rows_tab)
        return (step + 1, last[0], x, send)

    carry = (jnp.int32(1), jnp.int32(2), x, send)
    x = lax.while_loop(more, turn, carry)[2]
    return x[:, :feats].reshape(ways, micro, tokens, feats)


def solution(mesh):
    return jax.shard_map(
        on_device,
        mesh=mesh,
        in_specs=(
            P(None, None, "expert", None),
            P("section", None),
            P("section", None, "expert"),
            P("section", None, "expert"),
            P("section", "expert", None),
            P(None, None, "section", "expert", None),
            P(None, None, "section", "expert", None),
        ),
        out_specs=P(None, None, "expert", "section"),
        check_vma=False,
    )
```

```python
import functools

import jax
import jax.numpy as jnp
from jax import lax
from jax.experimental import pallas as pl
from jax.experimental.pallas import tpu as pltpu
from jax.sharding import PartitionSpec as P

GROUP = 2
CAP = 2

norm_eps = 1e-06
route_scale = 2.5

F32 = jnp.float32
BF16 = jnp.bfloat16
LANES = 128
AXES = ("section", "expert")

VMEM = pltpu.VMEM
SMEM = pltpu.SMEM


def iota(shape, dim):
    return lax.broadcasted_iota(jnp.int32, shape, dim)


def mm(a, b):
    return jnp.dot(a, b, preferred_element_type=F32)


def route_kernel(me_ref, ids_ref, scores_ref, x_ref, *refs, window, slots):
    spread = len(refs) - 1
    outs, rows_ref = refs[:spread], refs[spread]
    groups, topk, tokens = ids_ref.shape
    count, width = x_ref.shape
    across = lambda ref: jnp.concatenate([ref[g] for g in range(groups)], axis=1)
    ids = across(ids_ref)
    scores = across(scores_ref)
    weights = route_scale * scores / jnp.sum(scores, axis=0, keepdims=True)
    block_of = lambda v: jnp.floor((v.astype(F32) + 0.5) * (1.0 / tokens))
    place_i = iota((count, count), 0)
    place_j = iota((count, count), 1)
    earlier = ((place_i < place_j) & (block_of(place_i) == block_of(place_j))).astype(BF16)
    token_lane = iota((slots, count), 1).astype(F32)
    slot_row = iota((slots, count), 0).astype(F32)
    base = block_of(iota((1, count), 1)) * CAP
    same = [ids == e for e in range(window)]
    hits = jnp.concatenate([jnp.sum(jnp.where(m, 1.0, 0.0), axis=0, keepdims=True) for m in same], axis=0)
    before = mm(hits.astype(BF16), earlier)
    x = x_ref[...]
    meta_lane = iota((slots, LANES), 1)
    for e in range(window):
        share = jnp.sum(jnp.where(same[e], weights, 0.0), axis=0, keepdims=True)
        pick = jnp.where(base + before[e:e + 1] == slot_row, hits[e:e + 1], 0.0)
        token = jnp.sum(pick * token_lane + pick, axis=-1, keepdims=True) - 1.0
        w = jnp.sum(pick * share, axis=-1, keepdims=True)
        high = w.astype(BF16).astype(F32)
        mid = (w - high).astype(BF16).astype(F32)
        low = w - high - mid
        meta = jnp.where(meta_lane == 0, token, 0.0)
        meta = jnp.where(meta_lane == 1, high, meta)
        meta = jnp.where(meta_lane == 2, mid, meta)
        meta = jnp.where(meta_lane == 3, low, meta)
        rows_ref[e, :, :width] = mm(pick.astype(BF16), x).astype(BF16)
        rows_ref[e, :, width:] = meta.astype(BF16)
    me = me_ref[0]
    for k in range(spread):
        peer = lax.rem(me + k, spread)
        outs[k][...] = rows_ref[lax.div(peer, GROUP)]


def load_kernel(*refs):
    half = (len(refs) - 1) // 2
    sems = refs[-1]
    copies = [pltpu.make_async_copy(refs[n], refs[half + n], sems.at[n]) for n in range(half)]
    for copy in copies:
        copy.start()
    for copy in copies:
        copy.wait()


def feed_forward(h, wg_ref, wu_ref, wd_ref):
    gate = mm(h, wg_ref[...])
    up = mm(h, wu_ref[...])
    act = (gate / (1.0 + jnp.exp(-gate)) * up).astype(BF16)
    return mm(act, wd_ref[...])


def first_kernel(me_ref, gain_ref, wg_ref, wu_ref, wd_ref, *refs, sections, feats):
    spread = len(refs) - 1
    ins, out_ref = refs[:spread], refs[spread]
    width = gain_ref.shape[1]
    slots = ins[0].shape[0]
    room = out_ref.shape[2] - feats
    x = jnp.concatenate([r[:, :width].astype(F32) for r in ins], axis=0)
    mean = jnp.mean(x * x, axis=-1, keepdims=True)
    h = (x * lax.rsqrt(mean + norm_eps) * gain_ref[...]).astype(BF16)
    part = feed_forward(h, wg_ref, wu_ref, wd_ref).astype(BF16)
    me = me_ref[0]
    for k in range(spread):
        block = lax.rem(me - k + spread, spread)
        meta = ins[k][:, width:width + room]
        for s in range(sections):
            out_ref[s * spread + block, :, :feats] = part[k * slots:(k + 1) * slots, s * feats:(s + 1) * feats]
            out_ref[s * spread + block, :, feats:] = meta


def round_kernel(gain_ref, wg_ref, wu_ref, wd_ref, in_ref, out_ref, last_ref, *, sections, feats):
    count, slots, padded = in_ref.shape
    spread = count // sections
    rows = spread * slots
    width = sections * feats
    pieces = []
    total = jnp.zeros((rows, 1), F32)
    for s in range(sections):
        piece = in_ref[s * spread:(s + 1) * spread, :, :].astype(F32).reshape(rows, padded)[:, :feats]
        total = total + jnp.sum(piece * piece, axis=-1, keepdims=True)
        pieces.append(piece)
    scale = lax.rsqrt(total * (1.0 / width) + norm_eps)
    gate = jnp.zeros((rows, wg_ref.shape[1]), F32)
    up = jnp.zeros((rows, wg_ref.shape[1]), F32)
    for s in range(sections):
        h = (pieces[s] * scale * gain_ref[:, s * feats:(s + 1) * feats]).astype(BF16)
        gate = gate + mm(h, wg_ref[s * feats:(s + 1) * feats, :])
        up = up + mm(h, wu_ref[s * feats:(s + 1) * feats, :])
    act = (gate / (1.0 + jnp.exp(-gate)) * up).astype(BF16)
    part = mm(act, wd_ref[...]).astype(BF16)
    for s in range(sections):
        piece = part[:, s * feats:(s + 1) * feats]
        for b in range(spread):
            out_ref[s * spread + b, :, :feats] = piece[b * slots:(b + 1) * slots]
            out_ref[s * spread + b, :, feats:] = jnp.zeros((slots, padded - feats), BF16)
    depth = in_ref[:spread, :, :].astype(F32).reshape(rows, padded)[:, feats:feats + 1]
    last_ref[0] = jnp.max(depth).astype(jnp.int32)


def apply_parts(step, parts, x, cols, rows_tab, feats):
    tokens, padded = x.shape
    count = parts.shape[0]
    chosen = (iota((tokens, count), 0).astype(F32) == rows_tab[0:1, :]) & (rows_tab[4:5, :] == step)
    added = jnp.zeros((tokens, padded), F32)
    for n in (1, 2, 3):
        added = added + mm(jnp.where(chosen, rows_tab[n:n + 1, :], 0.0).astype(BF16), parts)
    lane = iota((tokens, padded), 1)
    x = jnp.where(lane < feats, x.astype(F32) + added, 0.0).astype(BF16)
    pick = (iota((count, tokens), 1).astype(F32) == cols[:, 0:1]).astype(BF16)
    send = jnp.where(iota((count, padded), 1) == feats, cols[:, 5:6], mm(pick, x))
    return x, send.astype(BF16)


def table_kernel(x_ref, in_ref, x_out, send_out, cols_out, rows_out, step_out, last_out, *, sections, feats):
    count, slots, padded = in_ref.shape
    tokens = x_ref.shape[0]
    total = count * slots
    per = total // sections
    parts = in_ref[...].reshape(total, padded)
    meta = parts[:, feats:feats + 4].astype(F32)
    token = meta[:, 0:1]
    pick = (iota((total, tokens), 1).astype(F32) == token).astype(F32)
    hit = [jnp.minimum(jnp.sum(pick[l * per:(l + 1) * per], axis=0, keepdims=True), 1.0) for l in range(sections)]
    ahead, behind = [None] * sections, [None] * sections
    run_a = run_b = jnp.zeros((1, tokens), F32)
    for l in range(sections):
        ahead[l] = run_a
        run_a = run_a + hit[l]
        m = sections - 1 - l
        behind[m] = run_b
        run_b = run_b + hit[m]
    forward = iota((1, tokens), 1) < tokens // 2
    level = [
        jnp.sum(pick[l * per:(l + 1) * per] * jnp.where(forward, ahead[l], behind[l]), axis=-1, keepdims=True)
        for l in range(sections)
    ]
    level = jnp.concatenate(level, axis=0)
    depth = jnp.max(run_a)
    lane = iota((total, LANES), 1)
    cols = jnp.where(lane == 0, token, 0.0)
    for n in (1, 2, 3):
        cols = jnp.where(lane == n, meta[:, n:n + 1], cols)
    cols = jnp.where(lane == 4, level, cols)
    cols = jnp.where(lane == 5, depth, cols)
    rows_tab = cols.T[:8]
    cols_out[...] = cols
    step_out[0] = 1
    last_out[0] = 2
    rows_out[...] = rows_tab
    x, send = apply_parts(0.0, parts, x_ref[...], cols, rows_tab, feats)
    x_out[...] = x
    send_out[...] = send.reshape(count, slots, padded)


def update_kernel(step_ref, x_ref, in_ref, cols_ref, rows_ref, x_out, send_out, step_out, *, feats):
    count, slots, padded = in_ref.shape
    step = step_ref[0].astype(F32)
    step_out[0] = step_ref[0] + 1
    parts = in_ref[...].reshape(count * slots, padded)
    x, send = apply_parts(step, parts, x_ref[...], cols_ref[...], rows_ref[...], feats)
    x_out[...] = x
    send_out[...] = send.reshape(count, slots, padded)


def call(kernel, out_shape, in_spaces, out_spaces, name, scratch=(), limit=24 * 2**20, aliases={}):
    spec = lambda space: pl.BlockSpec(memory_space=space)
    single = not isinstance(out_shape, (list, tuple))
    return pl.pallas_call(
        kernel,
        out_shape=out_shape,
        in_specs=[spec(s) for s in in_spaces],
        out_specs=spec(out_spaces[0]) if single else [spec(s) for s in out_spaces],
        scratch_shapes=list(scratch),
        input_output_aliases=aliases,
        compiler_params=pltpu.CompilerParams(vmem_limit_bytes=limit),
        name=name,
    )


def on_device(entering, norm_gain, w_gate, w_up, w_down, route_ids, route_scores):
    sections = lax.axis_size("section")
    spread = lax.axis_size("expert")
    section = lax.axis_index("section")
    peer = lax.axis_index("expert")
    window = spread // GROUP
    ways, micro, tokens, width = entering.shape
    everyone = ways * micro * tokens
    slots = ways * micro * CAP
    feats = width // sections
    padded = (feats // LANES + 1) * LANES
    devices = sections * spread
    by_token = lambda v: jnp.swapaxes(v[:, :, 0], 2, 3).reshape(ways * micro, v.shape[-1], tokens)

    stored = [pltpu.with_memory_space_constraint(v[0], pltpu.HBM) for v in (w_gate, w_up, w_down)]
    weights = call(
        load_kernel,
        [VMEM(v.shape, v.dtype) for v in stored],
        [pltpu.HBM] * 3,
        [VMEM] * 3,
        "load",
        scratch=[pltpu.SemaphoreType.DMA((3,))],
    )(*stored)
    wg, wu, wd = [pltpu.with_memory_space_constraint(v, VMEM) for v in weights]
    me = peer.astype(jnp.int32).reshape(1)
    flat = entering.reshape(everyone, width)
    sds = jax.ShapeDtypeStruct

    rows = call(
        functools.partial(route_kernel, window=window, slots=slots),
        [sds((slots, width + LANES), BF16)] * spread,
        [SMEM, VMEM, VMEM, VMEM],
        [VMEM] * spread,
        "route",
        scratch=[VMEM((window, slots, width + LANES), BF16)],
    )(me, by_token(route_ids), by_token(route_scores), flat)
    received = [rows[0]] + [
        lax.ppermute(rows[k], "expert", [(y, (y + k) % spread) for y in range(spread)]) for k in range(1, spread)
    ]
    message = sds((devices, slots, padded), BF16)
    swap = lambda v: lax.all_to_all(v, AXES, split_axis=0, concat_axis=0, tiled=True)
    parts = call(
        functools.partial(first_kernel, sections=sections, feats=feats),
        message,
        [SMEM] + [VMEM] * (4 + spread),
        [VMEM],
        "first",
    )(me, norm_gain, wg, wu, wd, *received)
    own = lax.dynamic_slice(flat, (0, section * feats), (everyone, feats))
    own = jnp.pad(own, ((0, 0), (0, padded - feats)))
    parts, own = lax.optimization_barrier((parts, own))
    number = sds((1,), jnp.int32)
    state = sds((everyone, padded), BF16)
    x, send, cols, rows_tab, step, last = call(
        functools.partial(table_kernel, sections=sections, feats=feats),
        [state, message, sds((devices * slots, LANES), F32), sds((8, devices * slots), F32), number, number],
        [VMEM, VMEM],
        [VMEM] * 4 + [SMEM] * 2,
        "table",
    )(own, swap(parts))

    def more(carry):
        return carry[0][0] < carry[1][0]

    def turn(carry):
        step, unused, x, send = lax.optimization_barrier(carry)
        parts, last = call(
            functools.partial(round_kernel, sections=sections, feats=feats),
            [message, number],
            [VMEM] * 5,
            [VMEM, SMEM],
            "round",
        )(norm_gain, wg, wu, wd, swap(send))
        x, send, step = call(
            functools.partial(update_kernel, feats=feats),
            [state, message, number],
            [SMEM] + [VMEM] * 4,
            [VMEM] * 2 + [SMEM],
            "update",
            aliases={1: 0},
        )(step, x, swap(parts), cols, rows_tab)
        return (step, last, x, send)

    x = lax.while_loop(more, turn, (step, last, x, send))[2]
    return x[:, :feats].reshape(ways, micro, tokens, feats)


def solution(mesh):
    return jax.shard_map(
        on_device,
        mesh=mesh,
        in_specs=(
            P(None, None, "expert", None),
            P("section", None),
            P("section", None, "expert"),
            P("section", None, "expert"),
            P("section", "expert", None),
            P(None, None, "section", "expert", None),
            P(None, None, "section", "expert", None),
        ),
        out_specs=P(None, None, "expert", "section"),
        check_vma=False,
    )
```

```python
import functools

import jax
import jax.numpy as jnp
from jax import lax
from jax.experimental import pallas as pl
from jax.experimental.pallas import tpu as pltpu
from jax.sharding import PartitionSpec as P

GROUP = 2
CAP = 2

norm_eps = 1e-06
route_scale = 2.5

F32 = jnp.float32
BF16 = jnp.bfloat16
LANES = 128
AXES = ("section", "expert")

VMEM = pltpu.VMEM
HBM = pltpu.HBM
SMEM = pltpu.SMEM


def iota(shape, dim):
    return lax.broadcasted_iota(jnp.int32, shape, dim)


def start(*copies):
    for copy in copies:
        copy.start()
    return copies


def mm(a, b):
    return jnp.dot(a, b, preferred_element_type=F32)


def route_kernel(me_ref, ids_hbm, scores_hbm, x_hbm, w_hbm, *refs, window, slots):
    spread = len(refs) - 6
    outs, w_ref = refs[:spread], refs[spread]
    ids_ref, scores_ref, x_ref, rows_ref, sems = refs[spread + 1:]
    pairs = ((ids_hbm, ids_ref), (scores_hbm, scores_ref), (x_hbm, x_ref), (w_hbm, w_ref))
    copies = start(*[pltpu.make_async_copy(a, b, sems.at[n]) for n, (a, b) in enumerate(pairs)])
    groups, topk, tokens = ids_ref.shape
    count, width = x_ref.shape
    block_of = lambda v: jnp.floor((v.astype(F32) + 0.5) * (1.0 / tokens))
    place_i = iota((count, count), 0)
    place_j = iota((count, count), 1)
    earlier = ((place_i < place_j) & (block_of(place_i) == block_of(place_j))).astype(BF16)
    token_lane = iota((slots, count), 1).astype(F32)
    slot_row = iota((slots, count), 0).astype(F32)
    base = block_of(iota((1, count), 1)) * CAP
    meta_lane = iota((slots, LANES), 1)
    copies[0].wait()
    copies[1].wait()
    across = lambda ref: jnp.concatenate([ref[g] for g in range(groups)], axis=1)
    ids = across(ids_ref)
    scores = across(scores_ref)
    weights = route_scale * scores / jnp.sum(scores, axis=0, keepdims=True)
    same = [ids == e for e in range(window)]
    hits = jnp.concatenate([jnp.sum(jnp.where(m, 1.0, 0.0), axis=0, keepdims=True) for m in same], axis=0)
    before = mm(hits.astype(BF16), earlier)
    picks = []
    for e in range(window):
        share = jnp.sum(jnp.where(same[e], weights, 0.0), axis=0, keepdims=True)
        pick = jnp.where(base + before[e:e + 1] == slot_row, hits[e:e + 1], 0.0)
        picks.append(pick.astype(BF16))
        token = jnp.sum(pick * token_lane + pick, axis=-1, keepdims=True) - 1.0
        w = jnp.sum(pick * share, axis=-1, keepdims=True)
        high = w.astype(BF16).astype(F32)
        mid = (w - high).astype(BF16).astype(F32)
        low = w - high - mid
        meta = jnp.where(meta_lane == 0, token, 0.0)
        meta = jnp.where(meta_lane == 1, high, meta)
        meta = jnp.where(meta_lane == 2, mid, meta)
        meta = jnp.where(meta_lane == 3, low, meta)
        rows_ref[e, :, width:] = meta.astype(BF16)
    copies[2].wait()
    x = x_ref[...]
    for e in range(window):
        rows_ref[e, :, :width] = mm(picks[e], x).astype(BF16)
    me = me_ref[0]
    for k in range(spread):
        peer = lax.rem(me + k, spread)
        outs[k][...] = rows_ref[lax.div(peer, GROUP)]
    copies[3].wait()


def load_kernel(section_ref, x_hbm, w_hbm, own_ref, w_ref, piece_ref, sems, *, feats):
    section = section_ref[0]
    tokens, padded = own_ref.shape
    span = piece_ref.shape[1]
    width = x_hbm.shape[1]
    first = jnp.minimum(lax.div(section * feats, LANES), (width - span) // LANES) * LANES
    piece, weight = start(
        pltpu.make_async_copy(x_hbm.at[:, pl.ds(pl.multiple_of(first, LANES), span)], piece_ref, sems.at[0]),
        pltpu.make_async_copy(w_hbm, w_ref, sems.at[1]),
    )
    piece.wait()
    moved = pltpu.roll(piece_ref[...].astype(F32), lax.rem(span - (section * feats - first), span), 1)[:, :padded]
    own_ref[...] = jnp.where(iota((tokens, padded), 1) < feats, moved, 0.0).astype(BF16)
    weight.wait()


def silu_times(gate, up):
    return (gate / (1.0 + jnp.exp(-gate)) * up).astype(BF16)


def first_kernel(me_ref, gain_ref, wg_ref, wu_ref, wd_hbm, *refs, sections, feats):
    spread = len(refs) - 3
    ins, out_ref, wd_ref, sems = refs[:spread], refs[spread], refs[spread + 1], refs[spread + 2]
    copy, = start(pltpu.make_async_copy(wd_hbm, wd_ref, sems.at[0]))
    width = gain_ref.shape[1]
    slots = ins[0].shape[0]
    room = out_ref.shape[2] - feats
    x = jnp.concatenate([r[:, :width].astype(F32) for r in ins], axis=0)
    mean = jnp.mean(x * x, axis=-1, keepdims=True)
    h = (x * lax.rsqrt(mean + norm_eps) * gain_ref[...]).astype(BF16)
    act = silu_times(mm(h, wg_ref[...]), mm(h, wu_ref[...]))
    copy.wait()
    part = mm(act, wd_ref[...]).astype(BF16)
    me = me_ref[0]
    for k in range(spread):
        block = lax.rem(me - k + spread, spread)
        meta = ins[k][:, width:width + room]
        for s in range(sections):
            out_ref[s * spread + block, :, :feats] = part[k * slots:(k + 1) * slots, s * feats:(s + 1) * feats]
            out_ref[s * spread + block, :, feats:] = meta


def all_layers(pieces, gain_ref, wg_ref, wu_ref, wd_ref):
    rows, feats = pieces[0].shape
    total = jnp.zeros((rows, 1), F32)
    for piece in pieces:
        total = total + jnp.sum(piece * piece, axis=-1, keepdims=True)
    scale = lax.rsqrt(total * (1.0 / (feats * len(pieces))) + norm_eps)
    gate = jnp.zeros((rows, wg_ref.shape[1]), F32)
    up = jnp.zeros((rows, wg_ref.shape[1]), F32)
    for s, piece in enumerate(pieces):
        here = slice(s * feats, (s + 1) * feats)
        h = (piece * scale * gain_ref[:, here]).astype(BF16)
        gate = gate + mm(h, wg_ref[here, :])
        up = up + mm(h, wu_ref[here, :])
    return mm(silu_times(gate, up), wd_ref[...])


def write_flags(flags_ref, notes):
    top = jnp.max(notes, axis=0, keepdims=True)
    following = top[:, 1:2] + 1.0
    flags_ref[0] = jnp.max(jnp.where(following < top[:, 2:3], 1.0, 0.0)).astype(jnp.int32)
    flags_ref[1] = jnp.max(jnp.where(following < top[:, 0:1], 1.0, 0.0)).astype(jnp.int32)


def round_kernel(gain_ref, wg_ref, wu_ref, wd_ref, in_ref, out_ref, flags_ref, *, sections, feats):
    count, slots, padded = in_ref.shape
    spread = count // sections
    rows = spread * slots
    block = lambda s: in_ref[s * spread:(s + 1) * spread, :, :].astype(F32).reshape(rows, padded)
    write_flags(flags_ref, block(0)[:, feats:feats + 3])
    pieces = [block(s)[:, :feats] for s in range(sections)]
    part = all_layers(pieces, gain_ref, wg_ref, wu_ref, wd_ref).astype(BF16)
    for s in range(sections):
        piece = part[:, s * feats:(s + 1) * feats]
        for b in range(spread):
            out_ref[s * spread + b, :, :feats] = piece[b * slots:(b + 1) * slots]
            out_ref[s * spread + b, :, feats:] = jnp.zeros((slots, padded - feats), BF16)


def compact_round_kernel(gain_ref, wg_ref, wu_ref, wd_ref, in_ref, out_ref, flags_ref, wide_ref, *, sections, feats, tiles):
    count, sub, lanes = in_ref.shape
    spread = count // sections
    rows = spread * (sub // tiles)
    span = spread * sub
    wide_ref[...] = in_ref[...].astype(F32).reshape(count * sub, lanes)
    at = lambda s, k: pl.ds(s * span + k, rows, stride=tiles)
    spare = feats - (tiles - 1) * lanes
    write_flags(flags_ref, wide_ref[at(0, tiles - 1), :][:, spare:spare + 3])
    pieces = []
    for s in range(sections):
        pieces.append(jnp.concatenate([wide_ref[at(s, k), :] for k in range(tiles)], axis=1)[:, :feats])
    part = all_layers(pieces, gain_ref, wg_ref, wu_ref, wd_ref)
    for s in range(sections):
        piece = part[:, s * feats:(s + 1) * feats]
        piece = jnp.concatenate([piece, jnp.zeros((rows, tiles * lanes - feats), F32)], axis=1)
        for k in range(tiles):
            wide_ref[at(s, k), :] = piece[:, k * lanes:(k + 1) * lanes]
    out_ref[...] = wide_ref[...].reshape(count, sub, lanes).astype(BF16)


def add_parts(chosen, weights, parts, x, step, feats):
    tokens, padded = x.shape
    added = jnp.zeros((tokens, padded), F32)
    for w in weights:
        added = added + mm(jnp.where(chosen, w, 0.0).astype(BF16), parts)
    lane = iota((tokens, padded), 1)
    x = x.astype(F32)
    kept = jnp.where(lane == feats + 1, step + 1.0, x)
    return jnp.where(lane < feats, x + added, kept).astype(BF16)


def with_notes(rows, x, feats):
    return jnp.where(iota(rows.shape, 1) < feats, rows, x[0:1].astype(F32))


def gather_full(cols, x, send_ref, feats):
    count, slots, padded = send_ref.shape
    pick = (iota((count * slots, x.shape[0]), 1).astype(F32) == cols[:, 0:1]).astype(BF16)
    send_ref[...] = with_notes(mm(pick, x), x, feats).reshape(count, slots, padded).astype(BF16)


def gather_compact(cols, x, step, send_ref, table_ref, wide_ref, slots, feats, tiles):
    count, sub, lanes = send_ref.shape
    kept = sub // tiles
    lane = iota(cols.shape, 1)
    live = (cols[:, 4:5] == step) & (cols[:, 0:1] >= 0.0)
    values = jnp.where(lane == 0, cols + 1.0, cols)
    tables = []
    for c in range(kept):
        mine = jnp.where(live & (cols[:, 5:6] == c), values, 0.0)
        tables.append(jnp.sum(mine.reshape(count, slots, LANES), axis=1))
    table = jnp.concatenate(tables, axis=0)
    pick = (iota((kept * count, x.shape[0]), 1).astype(F32) + 1.0 == table[:, 0:1]).astype(BF16)
    rows = with_notes(mm(pick, x), x, feats)
    for c in range(kept):
        for k in range(tiles):
            wide_ref[pl.ds(c * tiles + k, count, stride=sub), :] = rows[c * count:(c + 1) * count, k * lanes:(k + 1) * lanes]
    send_ref[...] = wide_ref[...].reshape(count, sub, lanes).astype(BF16)
    table_ref[...] = table


def table_kernel(x_ref, in_ref, x_out, send_out, cols_out, rows_out, *, sections, feats, kept):
    count, slots, padded = in_ref.shape
    tokens = x_ref.shape[0]
    total = count * slots
    per = total // sections
    parts = in_ref[...].reshape(total, padded)
    meta = parts[:, feats:feats + 4].astype(F32)
    token = meta[:, 0:1]
    pick = (iota((total, tokens), 1).astype(F32) == token).astype(F32)
    hit = [jnp.minimum(jnp.sum(pick[l * per:(l + 1) * per], axis=0, keepdims=True), 1.0) for l in range(sections)]
    ahead, behind = [None] * sections, [None] * sections
    run_a = run_b = jnp.zeros((1, tokens), F32)
    for l in range(sections):
        ahead[l] = run_a
        run_a = run_a + hit[l]
        m = sections - 1 - l
        behind[m] = run_b
        run_b = run_b + hit[m]
    forward = iota((1, tokens), 1) < tokens // 2
    level = [
        jnp.sum(pick[l * per:(l + 1) * per] * jnp.where(forward, ahead[l], behind[l]), axis=-1, keepdims=True)
        for l in range(sections)
    ]
    level = jnp.concatenate(level, axis=0)
    depth = jnp.max(run_a, axis=-1, keepdims=True)
    lane = iota((total, LANES), 1)
    row = iota((total, LANES), 0)
    mine = jnp.where((lane.astype(F32) == level) & (token >= 0.0), 1.0, 0.0)
    seen = mine
    shift = 1
    slot = lax.rem(row, slots)
    while shift < slots:
        seen = seen + jnp.where(slot >= shift, pltpu.roll(seen, shift, 0), 0.0)
        shift *= 2
    seen = seen * mine
    rank = jnp.sum(seen, axis=-1, keepdims=True) - 1.0
    most = jnp.max(seen, axis=0, keepdims=True)
    level_lane = iota((1, LANES), 1).astype(F32)
    full = jnp.max(jnp.where(most > kept, level_lane + 1.0, 0.0), axis=-1, keepdims=True)
    cols = jnp.where(lane == 0, token, 0.0)
    for n in (1, 2, 3):
        cols = jnp.where(lane == n, meta[:, n:n + 1], cols)
    cols = jnp.where(lane == 4, level, cols)
    cols = jnp.where(lane == 5, rank, cols)
    rows_tab = cols.T[:8]
    cols_out[...] = cols
    rows_out[...] = rows_tab
    x_lane = iota((tokens, padded), 1)
    x = jnp.where(x_lane == feats, depth, x_ref[...].astype(F32))
    x = jnp.where(x_lane == feats + 2, full, x).astype(BF16)
    chosen = chosen_full(rows_tab, 0.0, tokens)
    x = add_parts(chosen, [rows_tab[n:n + 1] for n in (1, 2, 3)], parts, x, jnp.zeros((1, 1), F32), feats)
    x_out[...] = x
    gather_full(cols, x, send_out, feats)


def chosen_full(rows_tab, step, tokens):
    same = iota((tokens, rows_tab.shape[1]), 0).astype(F32) == rows_tab[0:1]
    return same & (rows_tab[4:5] == step)


def update_kernel(x_ref, in_ref, cols_ref, rows_ref, x_out, send_out, compact_out, table_out, wide_ref, *, feats, tiles):
    count, slots, padded = in_ref.shape
    x = x_ref[...]
    step = x[0:1, feats + 1:feats + 2].astype(F32)
    rows_tab = rows_ref[...]
    parts = in_ref[...].reshape(count * slots, padded)
    chosen = chosen_full(rows_tab, step, x.shape[0])
    x = add_parts(chosen, [rows_tab[n:n + 1] for n in (1, 2, 3)], parts, x, step, feats)
    x_out[...] = x
    cols = cols_ref[...]
    gather_full(cols, x, send_out, feats)
    gather_compact(cols, x, step + 1.0, compact_out, table_out, wide_ref, slots, feats, tiles)


def compact_update_kernel(x_ref, in_ref, cols_ref, tab_ref, x_out, send_out, table_out, wide_ref, *, slots, feats, tiles):
    count, sub, lanes = in_ref.shape
    kept = sub // tiles
    x = x_ref[...]
    step = x[0:1, feats + 1:feats + 2].astype(F32)
    wide_ref[...] = in_ref[...].astype(F32).reshape(count * sub, lanes)
    at = lambda c, k: pl.ds(c * tiles + k, count, stride=sub)
    parts = jnp.concatenate(
        [jnp.concatenate([wide_ref[at(c, k), :] for k in range(tiles)], axis=1) for c in range(kept)], axis=0
    ).astype(BF16)
    table = tab_ref[...].T[:8]
    chosen = iota((x.shape[0], table.shape[1]), 0).astype(F32) + 1.0 == table[0:1]
    x = add_parts(chosen, [table[n:n + 1] for n in (1, 2, 3)], parts, x, step, feats)
    x_out[...] = x
    gather_compact(cols_ref[...], x, step + 1.0, send_out, table_out, wide_ref, slots, feats, tiles)


def call(kernel, out_shape, in_spaces, out_spaces, name, scratch=(), limit=24 * 2**20, aliases={}):
    spec = lambda space: pl.BlockSpec(memory_space=space)
    single = not isinstance(out_shape, (list, tuple))
    return pl.pallas_call(
        kernel,
        out_shape=out_shape,
        in_specs=[spec(s) for s in in_spaces],
        out_specs=spec(out_spaces[0]) if single else [spec(s) for s in out_spaces],
        scratch_shapes=list(scratch),
        input_output_aliases=aliases,
        compiler_params=pltpu.CompilerParams(vmem_limit_bytes=limit),
        name=name,
    )


def on_device(entering, norm_gain, w_gate, w_up, w_down, route_ids, route_scores):
    sections = lax.axis_size("section")
    spread = lax.axis_size("expert")
    window = spread // GROUP
    ways, micro, tokens, width = entering.shape
    everyone = ways * micro * tokens
    slots = ways * micro * CAP
    feats = width // sections
    tiles = feats // LANES + 1
    padded = tiles * LANES
    devices = sections * spread
    kept = max(1, 8 // tiles)
    sub = kept * tiles
    by_token = lambda v: jnp.swapaxes(v[:, :, 0], 2, 3).reshape(ways * micro, v.shape[-1], tokens)
    scalar = lambda name: lax.axis_index(name).astype(jnp.int32).reshape(1)
    in_hbm = lambda v: pltpu.with_memory_space_constraint(v, HBM)
    in_vmem = lambda v: pltpu.with_memory_space_constraint(v, VMEM)
    sds = jax.ShapeDtypeStruct
    dma = pltpu.SemaphoreType.DMA

    me, section = scalar("expert"), scalar("section")
    flat = in_hbm(entering.reshape(everyone, width))
    ids, scores = in_hbm(by_token(route_ids)), in_hbm(by_token(route_scores))
    wg, wu, wd = [in_hbm(v[0]) for v in (w_gate, w_up, w_down)]
    resident = lambda v: VMEM(v.shape, v.dtype)

    *rows, wg = call(
        functools.partial(route_kernel, window=window, slots=slots),
        [sds((slots, width + LANES), BF16)] * spread + [resident(wg)],
        [SMEM] + [HBM] * 4,
        [VMEM] * (spread + 1),
        "route",
        scratch=[
            VMEM(ids.shape, ids.dtype),
            VMEM(scores.shape, scores.dtype),
            VMEM((everyone, width), BF16),
            VMEM((window, slots, width + LANES), BF16),
            dma((4,)),
        ],
    )(me, ids, scores, flat, wg)
    received = [rows[0]] + [
        lax.ppermute(rows[k], "expert", [(y, (y + k) % spread) for y in range(spread)]) for k in range(1, spread)
    ]
    reach = max(s * feats % LANES for s in range(sections)) + feats
    span = -(-reach // LANES) * LANES
    state = sds((everyone, padded), BF16)
    own, wu = call(
        functools.partial(load_kernel, feats=feats),
        [state, resident(wu)],
        [SMEM, HBM, HBM],
        [VMEM] * 2,
        "load",
        scratch=[VMEM((everyone, span), BF16), dma((2,))],
    )(section, flat, wu)
    wg, wu = in_vmem(wg), in_vmem(wu)
    message = sds((devices, slots, padded), BF16)
    compact = sds((devices, sub, LANES), BF16)
    swap = lambda v: lax.all_to_all(v, AXES, split_axis=0, concat_axis=0, tiled=True)
    parts, wd = call(
        functools.partial(first_kernel, sections=sections, feats=feats),
        [message, resident(wd)],
        [SMEM] + [VMEM] * 3 + [HBM] + [VMEM] * spread,
        [VMEM] * 2,
        "first",
        scratch=[dma((1,))],
    )(me, norm_gain, wg, wu, wd, *received)
    experts = (norm_gain, wg, wu, in_vmem(wd))
    parts, own = lax.optimization_barrier((parts, own))
    x, send, cols, rows_tab = call(
        functools.partial(table_kernel, sections=sections, feats=feats, kept=kept),
        [state, message, sds((devices * slots, LANES), F32), sds((8, devices * slots), F32)],
        [VMEM, VMEM],
        [VMEM] * 4,
        "table",
    )(own, swap(parts))
    flags_of = sds((2,), jnp.int32)
    table_of = sds((devices * kept, LANES), F32)
    wide = VMEM((devices * sub, LANES), F32)

    def full_turn(x, send):
        parts, flags = call(
            functools.partial(round_kernel, sections=sections, feats=feats),
            [message, flags_of],
            [VMEM] * 5,
            [VMEM, SMEM],
            "round",
        )(*experts, swap(send))
        x, send, packed, table = call(
            functools.partial(update_kernel, feats=feats, tiles=tiles),
            [state, message, compact, table_of],
            [VMEM] * 4,
            [VMEM] * 4,
            "update",
            aliases={0: 0},
            scratch=[wide],
        )(x, swap(parts), cols, rows_tab)
        return flags, x, send, packed, table

    def full_body(carry):
        carry = lax.optimization_barrier(carry)
        return full_turn(carry[1], carry[2])

    def compact_body(carry):
        unused, x, packed, table = lax.optimization_barrier(carry)
        parts, flags = call(
            functools.partial(compact_round_kernel, sections=sections, feats=feats, tiles=tiles),
            [compact, flags_of],
            [VMEM] * 5,
            [VMEM, SMEM],
            "compact_round",
            scratch=[wide],
        )(*experts, swap(packed))
        x, packed, table = call(
            functools.partial(compact_update_kernel, slots=slots, feats=feats, tiles=tiles),
            [state, compact, table_of],
            [VMEM] * 4,
            [VMEM] * 3,
            "compact_update",
            aliases={0: 0, 3: 2},
            scratch=[wide],
        )(x, swap(parts), cols, table)
        return flags, x, packed, table

    carry = full_turn(x, send)
    carry = lax.while_loop(lambda c: c[0][0] > 0, full_body, carry)
    flags, x, send, packed, table = carry
    x = lax.while_loop(lambda c: c[0][1] > 0, compact_body, (flags, x, packed, table))[1]
    return x[:, :feats].reshape(ways, micro, tokens, feats)


def solution(mesh):
    return jax.shard_map(
        on_device,
        mesh=mesh,
        in_specs=(
            P(None, None, "expert", None),
            P("section", None),
            P("section", None, "expert"),
            P("section", None, "expert"),
            P("section", "expert", None),
            P(None, None, "section", "expert", None),
            P(None, None, "section", "expert", None),
        ),
        out_specs=P(None, None, "expert", "section"),
        check_vma=False,
    )
```

```python
import functools

import jax
import jax.numpy as jnp
from jax import lax
from jax.experimental import pallas as pl
from jax.experimental.pallas import tpu as pltpu
from jax.sharding import PartitionSpec as P

GROUP = 2
CAP = 2

norm_eps = 1e-06
route_scale = 2.5

F32 = jnp.float32
BF16 = jnp.bfloat16
LANES = 128
AXES = ("section", "expert")

VMEM = pltpu.VMEM
HBM = pltpu.HBM
SMEM = pltpu.SMEM


def iota(shape, dim):
    return lax.broadcasted_iota(jnp.int32, shape, dim)


def start(*copies):
    for copy in copies:
        copy.start()
    return copies


def mm(a, b):
    return jnp.dot(a, b, preferred_element_type=F32)


def route_kernel(me_ref, ids_hbm, scores_hbm, x_hbm, *refs, window, slots):
    spread = len(refs) - 5
    outs = refs[:spread]
    ids_ref, scores_ref, x_ref, rows_ref, sems = refs[spread:]
    pairs = ((ids_hbm, ids_ref), (scores_hbm, scores_ref), (x_hbm, x_ref))
    copies = start(*[pltpu.make_async_copy(a, b, sems.at[n]) for n, (a, b) in enumerate(pairs)])
    groups, topk, tokens = ids_ref.shape
    count, width = x_ref.shape
    block_of = lambda v: jnp.floor((v.astype(F32) + 0.5) * (1.0 / tokens))
    place_i = iota((count, count), 0)
    place_j = iota((count, count), 1)
    earlier = ((place_i < place_j) & (block_of(place_i) == block_of(place_j))).astype(BF16)
    token_lane = iota((slots, count), 1).astype(F32)
    slot_row = iota((slots, count), 0).astype(F32)
    base = block_of(iota((1, count), 1)) * CAP
    meta_lane = iota((slots, LANES), 1)
    copies[0].wait()
    copies[1].wait()
    across = lambda ref: jnp.concatenate([ref[g] for g in range(groups)], axis=1)
    ids = across(ids_ref)
    scores = across(scores_ref)
    weights = route_scale * scores / jnp.sum(scores, axis=0, keepdims=True)
    same = [ids == e for e in range(window)]
    hits = jnp.concatenate([jnp.sum(jnp.where(m, 1.0, 0.0), axis=0, keepdims=True) for m in same], axis=0)
    before = mm(hits.astype(BF16), earlier)
    picks = []
    for e in range(window):
        share = jnp.sum(jnp.where(same[e], weights, 0.0), axis=0, keepdims=True)
        pick = jnp.where(base + before[e:e + 1] == slot_row, hits[e:e + 1], 0.0)
        picks.append(pick.astype(BF16))
        token = jnp.sum(pick * token_lane + pick, axis=-1, keepdims=True) - 1.0
        w = jnp.sum(pick * share, axis=-1, keepdims=True)
        high = w.astype(BF16).astype(F32)
        mid = (w - high).astype(BF16).astype(F32)
        low = w - high - mid
        meta = jnp.where(meta_lane == 0, token, 0.0)
        meta = jnp.where(meta_lane == 1, high, meta)
        meta = jnp.where(meta_lane == 2, mid, meta)
        meta = jnp.where(meta_lane == 3, low, meta)
        rows_ref[e, :, width:] = meta.astype(BF16)
    copies[2].wait()
    x = x_ref[...]
    for e in range(window):
        rows_ref[e, :, :width] = mm(picks[e], x).astype(BF16)
    me = me_ref[0]
    for k in range(spread):
        peer = lax.rem(me + k, spread)
        outs[k][...] = rows_ref[lax.div(peer, GROUP)]


def load_kernel(section_ref, x_hbm, wg_hbm, wu_hbm, own_ref, wg_ref, wu_ref, piece_ref, sems, *, feats):
    section = section_ref[0]
    tokens, padded = own_ref.shape
    span = piece_ref.shape[1]
    width = x_hbm.shape[1]
    first = jnp.minimum(lax.div(section * feats, LANES), (width - span) // LANES) * LANES
    piece, *weights = start(
        pltpu.make_async_copy(x_hbm.at[:, pl.ds(pl.multiple_of(first, LANES), span)], piece_ref, sems.at[0]),
        pltpu.make_async_copy(wg_hbm, wg_ref, sems.at[1]),
        pltpu.make_async_copy(wu_hbm, wu_ref, sems.at[2]),
    )
    piece.wait()
    moved = pltpu.roll(piece_ref[...].astype(F32), lax.rem(span - (section * feats - first), span), 1)[:, :padded]
    own_ref[...] = jnp.where(iota((tokens, padded), 1) < feats, moved, 0.0).astype(BF16)
    for weight in weights:
        weight.wait()


def silu_times(gate, up):
    return (gate / (1.0 + jnp.exp(-gate)) * up).astype(BF16)


def first_kernel(me_ref, gain_ref, wg_ref, wu_ref, wd_hbm, *refs, sections, feats):
    spread = len(refs) - 3
    ins, out_ref, wd_ref, sems = refs[:spread], refs[spread], refs[spread + 1], refs[spread + 2]
    copy, = start(pltpu.make_async_copy(wd_hbm, wd_ref, sems.at[0]))
    width = gain_ref.shape[1]
    slots = ins[0].shape[0]
    room = out_ref.shape[2] - feats
    x = jnp.concatenate([r[:, :width].astype(F32) for r in ins], axis=0)
    mean = jnp.mean(x * x, axis=-1, keepdims=True)
    h = (x * lax.rsqrt(mean + norm_eps) * gain_ref[...]).astype(BF16)
    act = silu_times(mm(h, wg_ref[...]), mm(h, wu_ref[...]))
    copy.wait()
    part = mm(act, wd_ref[...]).astype(BF16)
    me = me_ref[0]
    for k in range(spread):
        block = lax.rem(me - k + spread, spread)
        meta = ins[k][:, width:width + room]
        for s in range(sections):
            out_ref[s * spread + block, :, :feats] = part[k * slots:(k + 1) * slots, s * feats:(s + 1) * feats]
            out_ref[s * spread + block, :, feats:] = meta


def all_layers(pieces, gain_ref, wg_ref, wu_ref, wd_ref):
    rows, feats = pieces[0].shape
    total = jnp.zeros((rows, 1), F32)
    for piece in pieces:
        total = total + jnp.sum(piece * piece, axis=-1, keepdims=True)
    scale = lax.rsqrt(total * (1.0 / (feats * len(pieces))) + norm_eps)
    gate = jnp.zeros((rows, wg_ref.shape[1]), F32)
    up = jnp.zeros((rows, wg_ref.shape[1]), F32)
    for s, piece in enumerate(pieces):
        here = slice(s * feats, (s + 1) * feats)
        h = (piece * scale * gain_ref[:, here]).astype(BF16)
        gate = gate + mm(h, wg_ref[here, :])
        up = up + mm(h, wu_ref[here, :])
    return mm(silu_times(gate, up), wd_ref[...])


def write_flags(more_full, more, notes):
    top = jnp.max(notes, axis=0, keepdims=True)
    following = top[:, 1:2] + 1.0
    more_full[0] = jnp.max(jnp.where(following < top[:, 2:3], 1.0, 0.0)).astype(jnp.int32)
    more[0] = jnp.max(jnp.where(following < top[:, 0:1], 1.0, 0.0)).astype(jnp.int32)


def round_kernel(gain_ref, wg_ref, wu_ref, wd_ref, in_ref, out_ref, more_full, more, *, sections, feats):
    count, slots, padded = in_ref.shape
    spread = count // sections
    rows = spread * slots
    block = lambda s: in_ref[s * spread:(s + 1) * spread, :, :].astype(F32).reshape(rows, padded)
    write_flags(more_full, more, block(0)[:, feats:feats + 3])
    pieces = [block(s)[:, :feats] for s in range(sections)]
    part = all_layers(pieces, gain_ref, wg_ref, wu_ref, wd_ref).astype(BF16)
    for s in range(sections):
        piece = part[:, s * feats:(s + 1) * feats]
        for b in range(spread):
            out_ref[s * spread + b, :, :feats] = piece[b * slots:(b + 1) * slots]
            out_ref[s * spread + b, :, feats:] = jnp.zeros((slots, padded - feats), BF16)


def compact_round_kernel(gain_ref, wg_ref, wu_ref, wd_ref, in_ref, out_ref, more_full, more, wide_ref, *, sections, feats, tiles):
    count, sub, lanes = in_ref.shape
    spread = count // sections
    rows = spread * (sub // tiles)
    span = spread * sub
    wide_ref[...] = in_ref[...].astype(F32).reshape(count * sub, lanes)
    at = lambda s, k: pl.ds(s * span + k, rows, stride=tiles)
    spare = feats - (tiles - 1) * lanes
    write_flags(more_full, more, wide_ref[at(0, tiles - 1), :][:, spare:spare + 3])
    pieces = []
    for s in range(sections):
        pieces.append(jnp.concatenate([wide_ref[at(s, k), :] for k in range(tiles)], axis=1)[:, :feats])
    part = all_layers(pieces, gain_ref, wg_ref, wu_ref, wd_ref)
    for s in range(sections):
        piece = part[:, s * feats:(s + 1) * feats]
        piece = jnp.concatenate([piece, jnp.zeros((rows, tiles * lanes - feats), F32)], axis=1)
        for k in range(tiles):
            wide_ref[at(s, k), :] = piece[:, k * lanes:(k + 1) * lanes]
    out_ref[...] = wide_ref[...].reshape(count, sub, lanes).astype(BF16)


def add_parts(chosen, weights, parts, x, step, feats):
    tokens, padded = x.shape
    added = jnp.zeros((tokens, padded), F32)
    for w in weights:
        added = added + mm(jnp.where(chosen, w, 0.0).astype(BF16), parts)
    lane = iota((tokens, padded), 1)
    x = x.astype(F32)
    kept = jnp.where(lane == feats + 1, step + 1.0, x)
    return jnp.where(lane < feats, x + added, kept).astype(BF16)


def with_notes(rows, x, feats):
    return jnp.where(iota(rows.shape, 1) < feats, rows, x[0:1].astype(F32))


def gather_full(cols, x, send_ref, feats):
    count, slots, padded = send_ref.shape
    pick = (iota((count * slots, x.shape[0]), 1).astype(F32) == cols[:, 0:1]).astype(BF16)
    send_ref[...] = with_notes(mm(pick, x), x, feats).reshape(count, slots, padded).astype(BF16)


def gather_compact(cols, x, step, send_ref, table_ref, wide_ref, slots, feats, tiles):
    count, sub, lanes = send_ref.shape
    kept = sub // tiles
    lane = iota(cols.shape, 1)
    live = (cols[:, 4:5] == step) & (cols[:, 0:1] >= 0.0)
    values = jnp.where(lane == 0, cols + 1.0, cols)
    tables = []
    for c in range(kept):
        mine = jnp.where(live & (cols[:, 5:6] == c), values, 0.0)
        tables.append(jnp.sum(mine.reshape(count, slots, LANES), axis=1))
    table = jnp.concatenate(tables, axis=0)
    pick = (iota((kept * count, x.shape[0]), 1).astype(F32) + 1.0 == table[:, 0:1]).astype(BF16)
    rows = with_notes(mm(pick, x), x, feats)
    for c in range(kept):
        for k in range(tiles):
            wide_ref[pl.ds(c * tiles + k, count, stride=sub), :] = rows[c * count:(c + 1) * count, k * lanes:(k + 1) * lanes]
    send_ref[...] = wide_ref[...].reshape(count, sub, lanes).astype(BF16)
    table_ref[...] = table


def table_kernel(x_ref, in_ref, x_out, send_out, cols_out, rows_out, *, sections, feats, kept):
    count, slots, padded = in_ref.shape
    tokens = x_ref.shape[0]
    total = count * slots
    per = total // sections
    parts = in_ref[...].reshape(total, padded)
    meta = parts[:, feats:feats + 4].astype(F32)
    token = meta[:, 0:1]
    pick = (iota((total, tokens), 1).astype(F32) == token).astype(F32)
    hit = [jnp.minimum(jnp.sum(pick[l * per:(l + 1) * per], axis=0, keepdims=True), 1.0) for l in range(sections)]
    ahead, behind = [None] * sections, [None] * sections
    run_a = run_b = jnp.zeros((1, tokens), F32)
    for l in range(sections):
        ahead[l] = run_a
        run_a = run_a + hit[l]
        m = sections - 1 - l
        behind[m] = run_b
        run_b = run_b + hit[m]
    forward = iota((1, tokens), 1) < tokens // 2
    level = [
        jnp.sum(pick[l * per:(l + 1) * per] * jnp.where(forward, ahead[l], behind[l]), axis=-1, keepdims=True)
        for l in range(sections)
    ]
    level = jnp.concatenate(level, axis=0)
    depth = jnp.max(run_a, axis=-1, keepdims=True)
    lane = iota((total, LANES), 1)
    row = iota((total, LANES), 0)
    mine = jnp.where((lane.astype(F32) == level) & (token >= 0.0), 1.0, 0.0)
    seen = mine
    shift = 1
    slot = lax.rem(row, slots)
    while shift < slots:
        seen = seen + jnp.where(slot >= shift, pltpu.roll(seen, shift, 0), 0.0)
        shift *= 2
    seen = seen * mine
    rank = jnp.sum(seen, axis=-1, keepdims=True) - 1.0
    most = jnp.max(seen, axis=0, keepdims=True)
    level_lane = iota((1, LANES), 1).astype(F32)
    full = jnp.max(jnp.where(most > kept, level_lane + 1.0, 0.0), axis=-1, keepdims=True)
    cols = jnp.where(lane == 0, token, 0.0)
    for n in (1, 2, 3):
        cols = jnp.where(lane == n, meta[:, n:n + 1], cols)
    cols = jnp.where(lane == 4, level, cols)
    cols = jnp.where(lane == 5, rank, cols)
    rows_tab = cols.T[:8]
    cols_out[...] = cols
    rows_out[...] = rows_tab
    x_lane = iota((tokens, padded), 1)
    x = jnp.where(x_lane == feats, depth, x_ref[...].astype(F32))
    x = jnp.where(x_lane == feats + 2, full, x).astype(BF16)
    chosen = chosen_full(rows_tab, 0.0, tokens)
    x = add_parts(chosen, [rows_tab[n:n + 1] for n in (1, 2, 3)], parts, x, jnp.zeros((1, 1), F32), feats)
    x_out[...] = x
    gather_full(cols, x, send_out, feats)


def chosen_full(rows_tab, step, tokens):
    same = iota((tokens, rows_tab.shape[1]), 0).astype(F32) == rows_tab[0:1]
    return same & (rows_tab[4:5] == step)


def update_kernel(x_ref, in_ref, cols_ref, rows_ref, x_out, send_out, compact_out, table_out, wide_ref, *, feats, tiles):
    count, slots, padded = in_ref.shape
    x = x_ref[...]
    step = x[0:1, feats + 1:feats + 2].astype(F32)
    rows_tab = rows_ref[...]
    parts = in_ref[...].reshape(count * slots, padded)
    chosen = chosen_full(rows_tab, step, x.shape[0])
    x = add_parts(chosen, [rows_tab[n:n + 1] for n in (1, 2, 3)], parts, x, step, feats)
    x_out[...] = x
    cols = cols_ref[...]
    gather_full(cols, x, send_out, feats)
    gather_compact(cols, x, step + 1.0, compact_out, table_out, wide_ref, slots, feats, tiles)


def compact_update_kernel(x_ref, in_ref, cols_ref, tab_ref, x_out, send_out, table_out, wide_ref, *, slots, feats, tiles):
    count, sub, lanes = in_ref.shape
    kept = sub // tiles
    x = x_ref[...]
    step = x[0:1, feats + 1:feats + 2].astype(F32)
    wide_ref[...] = in_ref[...].astype(F32).reshape(count * sub, lanes)
    at = lambda c, k: pl.ds(c * tiles + k, count, stride=sub)
    parts = jnp.concatenate(
        [jnp.concatenate([wide_ref[at(c, k), :] for k in range(tiles)], axis=1) for c in range(kept)], axis=0
    ).astype(BF16)
    table = tab_ref[...].T[:8]
    chosen = iota((x.shape[0], table.shape[1]), 0).astype(F32) + 1.0 == table[0:1]
    x = add_parts(chosen, [table[n:n + 1] for n in (1, 2, 3)], parts, x, step, feats)
    x_out[...] = x
    gather_compact(cols_ref[...], x, step + 1.0, send_out, table_out, wide_ref, slots, feats, tiles)


def call(kernel, out_shape, in_spaces, out_spaces, name, scratch=(), limit=24 * 2**20, aliases={}):
    spec = lambda space: pl.BlockSpec(memory_space=space)
    single = not isinstance(out_shape, (list, tuple))
    return pl.pallas_call(
        kernel,
        out_shape=out_shape,
        in_specs=[spec(s) for s in in_spaces],
        out_specs=spec(out_spaces[0]) if single else [spec(s) for s in out_spaces],
        scratch_shapes=list(scratch),
        input_output_aliases=aliases,
        compiler_params=pltpu.CompilerParams(vmem_limit_bytes=limit),
        name=name,
    )


def on_device(entering, norm_gain, w_gate, w_up, w_down, route_ids, route_scores):
    sections = lax.axis_size("section")
    spread = lax.axis_size("expert")
    window = spread // GROUP
    ways, micro, tokens, width = entering.shape
    everyone = ways * micro * tokens
    slots = ways * micro * CAP
    feats = width // sections
    tiles = feats // LANES + 1
    padded = tiles * LANES
    devices = sections * spread
    kept = max(1, 8 // tiles)
    sub = kept * tiles
    by_token = lambda v: jnp.swapaxes(v[:, :, 0], 2, 3).reshape(ways * micro, v.shape[-1], tokens)
    scalar = lambda name: lax.axis_index(name).astype(jnp.int32).reshape(1)
    in_hbm = lambda v: pltpu.with_memory_space_constraint(v, HBM)
    in_vmem = lambda v: pltpu.with_memory_space_constraint(v, VMEM)
    sds = jax.ShapeDtypeStruct
    dma = pltpu.SemaphoreType.DMA

    me, section = scalar("expert"), scalar("section")
    flat = in_hbm(entering.reshape(everyone, width))
    ids, scores = in_hbm(by_token(route_ids)), in_hbm(by_token(route_scores))
    wg, wu, wd = [in_hbm(v[0]) for v in (w_gate, w_up, w_down)]
    resident = lambda v: VMEM(v.shape, v.dtype)

    rows = call(
        functools.partial(route_kernel, window=window, slots=slots),
        [sds((slots, width + LANES), BF16)] * spread,
        [SMEM] + [HBM] * 3,
        [VMEM] * spread,
        "route",
        scratch=[
            VMEM(ids.shape, ids.dtype),
            VMEM(scores.shape, scores.dtype),
            VMEM((everyone, width), BF16),
            VMEM((window, slots, width + LANES), BF16),
            dma((3,)),
        ],
    )(me, ids, scores, flat)
    received = [rows[0]] + [
        lax.ppermute(rows[k], "expert", [(y, (y + k) % spread) for y in range(spread)]) for k in range(1, spread)
    ]
    reach = max(s * feats % LANES for s in range(sections)) + feats
    span = -(-reach // LANES) * LANES
    state = sds((everyone, padded), BF16)
    own, wg, wu = call(
        functools.partial(load_kernel, feats=feats),
        [state, resident(wg), resident(wu)],
        [SMEM] + [HBM] * 3,
        [VMEM] * 3,
        "load",
        scratch=[VMEM((everyone, span), BF16), dma((3,))],
    )(section, flat, wg, wu)
    wg, wu = in_vmem(wg), in_vmem(wu)
    message = sds((devices, slots, padded), BF16)
    compact = sds((devices, sub, LANES), BF16)
    swap = lambda v: lax.all_to_all(v, AXES, split_axis=0, concat_axis=0, tiled=True)
    parts, wd = call(
        functools.partial(first_kernel, sections=sections, feats=feats),
        [message, resident(wd)],
        [SMEM] + [VMEM] * 3 + [HBM] + [VMEM] * spread,
        [VMEM] * 2,
        "first",
        scratch=[dma((1,))],
    )(me, norm_gain, wg, wu, wd, *received)
    experts = (norm_gain, wg, wu, in_vmem(wd))
    parts, own = lax.optimization_barrier((parts, own))
    x, send, cols, rows_tab = call(
        functools.partial(table_kernel, sections=sections, feats=feats, kept=kept),
        [state, message, sds((devices * slots, LANES), F32), sds((8, devices * slots), F32)],
        [VMEM, VMEM],
        [VMEM] * 4,
        "table",
    )(own, swap(parts))
    flag = SMEM((1,), jnp.int32)
    table_of = VMEM((devices * kept, LANES), F32)
    wide = VMEM((devices * sub, LANES), F32)

    def full_turn(x, send):
        parts, *flags = call(
            functools.partial(round_kernel, sections=sections, feats=feats),
            [message, flag, flag],
            [VMEM] * 5,
            [VMEM, SMEM, SMEM],
            "round",
        )(*experts, swap(send))
        x, send, packed, table = call(
            functools.partial(update_kernel, feats=feats, tiles=tiles),
            [state, message, compact, table_of],
            [VMEM] * 4,
            [VMEM] * 4,
            "update",
            aliases={0: 0},
            scratch=[wide],
        )(x, swap(parts), cols, rows_tab)
        return tuple(flags), x, send, packed, table

    def full_body(carry):
        carry = lax.optimization_barrier(carry)
        return full_turn(carry[1], carry[2])

    def compact_body(carry):
        unused, x, packed, table = lax.optimization_barrier(carry)
        parts, *flags = call(
            functools.partial(compact_round_kernel, sections=sections, feats=feats, tiles=tiles),
            [compact, flag, flag],
            [VMEM] * 5,
            [VMEM, SMEM, SMEM],
            "compact_round",
            scratch=[wide],
        )(*experts, swap(packed))
        x, packed, table = call(
            functools.partial(compact_update_kernel, slots=slots, feats=feats, tiles=tiles),
            [state, compact, table_of],
            [VMEM] * 4,
            [VMEM] * 3,
            "compact_update",
            aliases={0: 0, 3: 2},
            scratch=[wide],
        )(x, swap(parts), cols, in_vmem(table))
        return flags[1], x, packed, table

    carry = full_turn(x, send)
    carry = lax.while_loop(lambda c: c[0][0][0] > 0, full_body, carry)
    flags, x, send, packed, table = carry
    x = lax.while_loop(lambda c: c[0][0] > 0, compact_body, (flags[1], x, packed, table))[1]
    return x[:, :feats].reshape(ways, micro, tokens, feats)


def solution(mesh):
    return jax.shard_map(
        on_device,
        mesh=mesh,
        in_specs=(
            P(None, None, "expert", None),
            P("section", None),
            P("section", None, "expert"),
            P("section", None, "expert"),
            P("section", "expert", None),
            P(None, None, "section", "expert", None),
            P(None, None, "section", "expert", None),
        ),
        out_specs=P(None, None, "expert", "section"),
        check_vma=False,
    )
```

```python
import functools

import jax
import jax.numpy as jnp
from jax import lax
from jax.experimental import pallas as pl
from jax.experimental.pallas import tpu as pltpu
from jax.sharding import PartitionSpec as P

GROUP = 2
CAP = 2

norm_eps = 1e-06
route_scale = 2.5

F32 = jnp.float32
BF16 = jnp.bfloat16
LANES = 128
AXES = ("section", "expert")

VMEM = pltpu.VMEM
HBM = pltpu.HBM
SMEM = pltpu.SMEM


def iota(shape, dim):
    return lax.broadcasted_iota(jnp.int32, shape, dim)


def start(*copies):
    for copy in copies:
        copy.start()
    return copies


def mm(a, b):
    return jnp.dot(a, b, preferred_element_type=F32)


def route_kernel(me_ref, ids_hbm, scores_hbm, x_hbm, *refs, window, slots):
    spread = len(refs) - 5
    outs = refs[:spread]
    ids_ref, scores_ref, x_ref, rows_ref, sems = refs[spread:]
    pairs = ((ids_hbm, ids_ref), (scores_hbm, scores_ref), (x_hbm, x_ref))
    copies = start(*[pltpu.make_async_copy(a, b, sems.at[n]) for n, (a, b) in enumerate(pairs)])
    groups, topk, tokens = ids_ref.shape
    count, width = x_ref.shape
    block_of = lambda v: jnp.floor((v.astype(F32) + 0.5) * (1.0 / tokens))
    place_i = iota((count, count), 0)
    place_j = iota((count, count), 1)
    earlier = ((place_i < place_j) & (block_of(place_i) == block_of(place_j))).astype(BF16)
    token_lane = iota((slots, count), 1).astype(F32)
    slot_row = iota((slots, count), 0).astype(F32)
    base = block_of(iota((1, count), 1)) * CAP
    meta_lane = iota((slots, LANES), 1)
    copies[0].wait()
    copies[1].wait()
    across = lambda ref: jnp.concatenate([ref[g] for g in range(groups)], axis=1)
    ids = across(ids_ref)
    scores = across(scores_ref)
    weights = route_scale * scores / jnp.sum(scores, axis=0, keepdims=True)
    same = [ids == e for e in range(window)]
    hits = jnp.concatenate([jnp.sum(jnp.where(m, 1.0, 0.0), axis=0, keepdims=True) for m in same], axis=0)
    before = mm(hits.astype(BF16), earlier)
    picks = []
    for e in range(window):
        share = jnp.sum(jnp.where(same[e], weights, 0.0), axis=0, keepdims=True)
        pick = jnp.where(base + before[e:e + 1] == slot_row, hits[e:e + 1], 0.0)
        picks.append(pick.astype(BF16))
        token = jnp.sum(pick * token_lane + pick, axis=-1, keepdims=True) - 1.0
        w = jnp.sum(pick * share, axis=-1, keepdims=True)
        high = w.astype(BF16).astype(F32)
        mid = (w - high).astype(BF16).astype(F32)
        low = w - high - mid
        meta = jnp.where(meta_lane == 0, token, 0.0)
        meta = jnp.where(meta_lane == 1, high, meta)
        meta = jnp.where(meta_lane == 2, mid, meta)
        meta = jnp.where(meta_lane == 3, low, meta)
        rows_ref[e, :, width:] = meta.astype(BF16)
    copies[2].wait()
    x = x_ref[...]
    for e in range(window):
        rows_ref[e, :, :width] = mm(picks[e], x).astype(BF16)
    me = me_ref[0]
    for k in range(spread):
        peer = lax.rem(me + k, spread)
        outs[k][...] = rows_ref[lax.div(peer, GROUP)]


def load_kernel(section_ref, x_hbm, wg_hbm, wu_hbm, own_ref, wg_ref, wu_ref, piece_ref, sems, *, feats):
    section = section_ref[0]
    tokens, padded = own_ref.shape
    span = piece_ref.shape[1]
    width = x_hbm.shape[1]
    first = jnp.minimum(lax.div(section * feats, LANES), (width - span) // LANES) * LANES
    piece, *weights = start(
        pltpu.make_async_copy(x_hbm.at[:, pl.ds(pl.multiple_of(first, LANES), span)], piece_ref, sems.at[0]),
        pltpu.make_async_copy(wg_hbm, wg_ref, sems.at[1]),
        pltpu.make_async_copy(wu_hbm, wu_ref, sems.at[2]),
    )
    piece.wait()
    moved = pltpu.roll(piece_ref[...].astype(F32), lax.rem(span - (section * feats - first), span), 1)[:, :padded]
    own_ref[...] = jnp.where(iota((tokens, padded), 1) < feats, moved, 0.0).astype(BF16)
    for weight in weights:
        weight.wait()


def silu_times(gate, up):
    return (gate / (1.0 + jnp.exp(-gate)) * up).astype(BF16)


def first_kernel(me_ref, gain_ref, wg_ref, wu_ref, wd_hbm, *refs, sections, feats):
    spread = len(refs) - 3
    ins, out_ref, wd_ref, sems = refs[:spread], refs[spread], refs[spread + 1], refs[spread + 2]
    copy, = start(pltpu.make_async_copy(wd_hbm, wd_ref, sems.at[0]))
    width = gain_ref.shape[1]
    slots = ins[0].shape[0]
    room = out_ref.shape[2] - feats
    x = jnp.concatenate([r[:, :width].astype(F32) for r in ins], axis=0)
    mean = jnp.mean(x * x, axis=-1, keepdims=True)
    h = (x * lax.rsqrt(mean + norm_eps) * gain_ref[...]).astype(BF16)
    act = silu_times(mm(h, wg_ref[...]), mm(h, wu_ref[...]))
    copy.wait()
    part = mm(act, wd_ref[...]).astype(BF16)
    me = me_ref[0]
    for k in range(spread):
        block = lax.rem(me - k + spread, spread)
        meta = ins[k][:, width:width + room]
        for s in range(sections):
            out_ref[s * spread + block, :, :feats] = part[k * slots:(k + 1) * slots, s * feats:(s + 1) * feats]
            out_ref[s * spread + block, :, feats:] = meta


def all_layers(pieces, gain_ref, wg_ref, wu_ref, wd_ref):
    rows, feats = pieces[0].shape
    total = jnp.zeros((rows, 1), F32)
    for piece in pieces:
        total = total + jnp.sum(piece * piece, axis=-1, keepdims=True)
    scale = lax.rsqrt(total * (1.0 / (feats * len(pieces))) + norm_eps)
    gate = jnp.zeros((rows, wg_ref.shape[1]), F32)
    up = jnp.zeros((rows, wg_ref.shape[1]), F32)
    for s, piece in enumerate(pieces):
        here = slice(s * feats, (s + 1) * feats)
        h = (piece * scale * gain_ref[:, here]).astype(BF16)
        gate = gate + mm(h, wg_ref[here, :])
        up = up + mm(h, wu_ref[here, :])
    return mm(silu_times(gate, up), wd_ref[...])


def round_kernel(gain_ref, wg_ref, wu_ref, wd_ref, in_ref, out_ref, more, wide_ref, *, sections, feats, tiles):
    count, sub, lanes = in_ref.shape
    spread = count // sections
    rows = spread * (sub // tiles)
    span = spread * sub
    wide_ref[...] = in_ref[...].astype(F32).reshape(count * sub, lanes)
    at = lambda s, k: pl.ds(s * span + k, rows, stride=tiles)
    spare = feats - (tiles - 1) * lanes
    more[0] = jnp.max(wide_ref[at(0, tiles - 1), :][:, spare:spare + 1]).astype(jnp.int32)
    pieces = []
    for s in range(sections):
        pieces.append(jnp.concatenate([wide_ref[at(s, k), :] for k in range(tiles)], axis=1)[:, :feats])
    part = all_layers(pieces, gain_ref, wg_ref, wu_ref, wd_ref)
    for s in range(sections):
        piece = part[:, s * feats:(s + 1) * feats]
        piece = jnp.concatenate([piece, jnp.zeros((rows, tiles * lanes - feats), F32)], axis=1)
        for k in range(tiles):
            wide_ref[at(s, k), :] = piece[:, k * lanes:(k + 1) * lanes]
    out_ref[...] = wide_ref[...].reshape(count, sub, lanes).astype(BF16)


def add_parts(table, parts, x, feats):
    tokens, padded = x.shape
    across = table.T[:8]
    chosen = iota((tokens, across.shape[1]), 0).astype(F32) + 1.0 == across[0:1]
    added = jnp.zeros((tokens, padded), F32)
    for n in (1, 2, 3):
        added = added + mm(jnp.where(chosen, across[n:n + 1], 0.0).astype(BF16), parts)
    return jnp.where(iota((tokens, padded), 1) < feats, x.astype(F32) + added, 0.0).astype(BF16)


def find_ready(cols, tokens, sections):
    per = cols.shape[0] // sections
    pick = (iota((cols.shape[0], tokens), 1).astype(F32) == cols[:, 0:1]).astype(F32)
    pending = cols[:, 4:5]
    layer = lambda v, l: v[l * per:(l + 1) * per]
    waits = [jnp.minimum(jnp.sum(layer(pick, l) * layer(pending, l), axis=0, keepdims=True), 1.0) for l in range(sections)]
    ahead, behind = [None] * sections, [None] * sections
    run_a = run_b = jnp.zeros((1, tokens), F32)
    for l in range(sections):
        ahead[l] = run_a
        run_a = run_a + waits[l]
        m = sections - 1 - l
        behind[m] = run_b
        run_b = run_b + waits[m]
    forward = iota((1, tokens), 1) < tokens // 2
    ready = []
    for l in range(sections):
        free = jnp.where(jnp.where(forward, ahead[l], behind[l]) == 0.0, waits[l], 0.0)
        ready.append(jnp.sum(layer(pick, l) * free, axis=-1, keepdims=True))
    return jnp.concatenate(ready, axis=0), pick


def values_of(cols, taken):
    lane = iota(cols.shape, 1)
    return jnp.where(taken & (lane < 4), jnp.where(lane == 0, cols + 1.0, cols), 0.0)


def take_next(cols, x, cols_ref, send_ref, table_ref, wide_ref, sections, slots, feats, tiles):
    count, sub, lanes = send_ref.shape
    kept = sub // tiles
    tokens, padded = x.shape
    total = cols.shape[0]
    per = total // sections
    ready, pick = find_ready(cols, tokens, sections)
    slot = lax.rem(iota((total, LANES), 0), slots)
    seen = jnp.broadcast_to(ready, (total, LANES))
    shift = 1
    while shift < slots:
        seen = seen + jnp.where(slot >= shift, pltpu.roll(seen, shift, 0), 0.0)
        shift *= 2
    late = jnp.where(seen[:, 0:1] > kept, ready, 0.0)
    held = []
    for l in range(sections):
        here = slice(l * per, (l + 1) * per)
        wait = jnp.sum(pick[here] * late[here], axis=0, keepdims=True)
        held.append(jnp.sum(pick[here] * wait, axis=-1, keepdims=True))
    taken = jnp.where(jnp.concatenate(held, axis=0) == 0.0, ready, 0.0)
    cols = jnp.where(iota((total, LANES), 1) == 4, cols - taken, cols)
    cols_ref[...] = cols
    left = jnp.max(cols[:, 4:5], axis=0, keepdims=True)
    group_of = lambda v, size: jnp.floor((v.astype(F32) + 0.5) * (1.0 / size))
    owner = (group_of(iota((count, total), 0), GROUP) == group_of(iota((count, total), 1), slots)).astype(BF16)
    tables = []
    for c in range(kept):
        mine = values_of(cols, (taken > 0.0) & (seen == c + 1.0))
        tables.append(mm(owner, mine.astype(BF16)))
    table = jnp.concatenate(tables, axis=0)
    table_ref[...] = table
    chosen = (iota((kept * count, tokens), 1).astype(F32) + 1.0 == table[:, 0:1]).astype(BF16)
    rows = jnp.where(iota((kept * count, padded), 1) == feats, left, mm(chosen, x))
    for c in range(kept):
        for k in range(tiles):
            wide_ref[pl.ds(c * tiles + k, count, stride=sub), :] = rows[c * count:(c + 1) * count, k * lanes:(k + 1) * lanes]
    send_ref[...] = wide_ref[...].reshape(count, sub, lanes).astype(BF16)


def table_kernel(x_ref, in_ref, x_out, cols_out, send_out, table_out, wide_ref, *, sections, feats, tiles):
    count, slots, padded = in_ref.shape
    tokens = x_ref.shape[0]
    groups = count // GROUP
    parts = in_ref[...].reshape(count * slots, padded)
    meta = [parts[g * GROUP * slots:(g * GROUP + 1) * slots, feats:feats + 4].astype(F32) for g in range(groups)]
    meta = jnp.concatenate(meta, axis=0)
    lane = iota((groups * slots, LANES), 1)
    cols = jnp.where(lane == 0, meta[:, 0:1], 0.0)
    for n in (1, 2, 3):
        cols = jnp.where(lane == n, meta[:, n:n + 1], cols)
    cols = jnp.where((lane == 4) & (meta[:, 0:1] >= 0.0), 1.0, cols)
    ready, unused = find_ready(cols, tokens, sections)
    mine = values_of(cols, ready > 0.0)
    table = jnp.concatenate([mine[g * slots:(g + 1) * slots] for g in range(groups) for n in range(GROUP)], axis=0)
    x = add_parts(table, parts, x_ref[...], feats)
    x_out[...] = x
    cols = jnp.where(lane == 4, cols - ready, cols)
    take_next(cols, x, cols_out, send_out, table_out, wide_ref, sections, slots, feats, tiles)


def update_kernel(x_ref, cols_ref, in_ref, tab_ref, x_out, cols_out, send_out, table_out, in_wide, out_wide, *, sections, slots, feats, tiles):
    count, sub, lanes = in_ref.shape
    in_wide[...] = in_ref[...].astype(F32).reshape(count * sub, lanes)
    at = lambda c, k: pl.ds(c * tiles + k, count, stride=sub)
    parts = jnp.concatenate(
        [jnp.concatenate([in_wide[at(c, k), :] for k in range(tiles)], axis=1) for c in range(sub // tiles)], axis=0
    ).astype(BF16)
    x = add_parts(tab_ref[...], parts, x_ref[...], feats)
    x_out[...] = x
    take_next(cols_ref[...], x, cols_out, send_out, table_out, out_wide, sections, slots, feats, tiles)


def call(kernel, out_shape, in_spaces, out_spaces, name, scratch=(), limit=24 * 2**20, aliases={}):
    spec = lambda space: pl.BlockSpec(memory_space=space)
    single = not isinstance(out_shape, (list, tuple))
    return pl.pallas_call(
        kernel,
        out_shape=out_shape,
        in_specs=[spec(s) for s in in_spaces],
        out_specs=spec(out_spaces[0]) if single else [spec(s) for s in out_spaces],
        scratch_shapes=list(scratch),
        input_output_aliases=aliases,
        compiler_params=pltpu.CompilerParams(vmem_limit_bytes=limit),
        name=name,
    )


def on_device(entering, norm_gain, w_gate, w_up, w_down, route_ids, route_scores):
    sections = lax.axis_size("section")
    spread = lax.axis_size("expert")
    window = spread // GROUP
    ways, micro, tokens, width = entering.shape
    everyone = ways * micro * tokens
    slots = ways * micro * CAP
    feats = width // sections
    tiles = feats // LANES + 1
    padded = tiles * LANES
    devices = sections * spread
    later_kept = max(1, 8 // tiles)
    early_kept = min(slots, 2 * later_kept)
    by_token = lambda v: jnp.swapaxes(v[:, :, 0], 2, 3).reshape(ways * micro, v.shape[-1], tokens)
    scalar = lambda name: lax.axis_index(name).astype(jnp.int32).reshape(1)
    in_hbm = lambda v: pltpu.with_memory_space_constraint(v, HBM)
    in_vmem = lambda v: pltpu.with_memory_space_constraint(v, VMEM)
    sds = jax.ShapeDtypeStruct
    dma = pltpu.SemaphoreType.DMA

    me, section = scalar("expert"), scalar("section")
    flat = in_hbm(entering.reshape(everyone, width))
    ids, scores = in_hbm(by_token(route_ids)), in_hbm(by_token(route_scores))
    wg, wu, wd = [in_hbm(v[0]) for v in (w_gate, w_up, w_down)]
    resident = lambda v: VMEM(v.shape, v.dtype)

    rows = call(
        functools.partial(route_kernel, window=window, slots=slots),
        [sds((slots, width + LANES), BF16)] * spread,
        [SMEM] + [HBM] * 3,
        [VMEM] * spread,
        "route",
        scratch=[
            VMEM(ids.shape, ids.dtype),
            VMEM(scores.shape, scores.dtype),
            VMEM((everyone, width), BF16),
            VMEM((window, slots, width + LANES), BF16),
            dma((3,)),
        ],
    )(me, ids, scores, flat)
    received = [rows[0]] + [
        lax.ppermute(rows[k], "expert", [(y, (y + k) % spread) for y in range(spread)]) for k in range(1, spread)
    ]
    reach = max(s * feats % LANES for s in range(sections)) + feats
    span = -(-reach // LANES) * LANES
    state = sds((everyone, padded), BF16)
    own, wg, wu = call(
        functools.partial(load_kernel, feats=feats),
        [state, resident(wg), resident(wu)],
        [SMEM] + [HBM] * 3,
        [VMEM] * 3,
        "load",
        scratch=[VMEM((everyone, span), BF16), dma((3,))],
    )(section, flat, wg, wu)
    wg, wu = in_vmem(wg), in_vmem(wu)
    message = sds((devices, slots, padded), BF16)
    compact = lambda kept: sds((devices, kept * tiles, LANES), BF16)
    swap = lambda v: lax.all_to_all(v, AXES, split_axis=0, concat_axis=0, tiled=True)
    parts, wd = call(
        functools.partial(first_kernel, sections=sections, feats=feats),
        [message, resident(wd)],
        [SMEM] + [VMEM] * 3 + [HBM] + [VMEM] * spread,
        [VMEM] * 2,
        "first",
        scratch=[dma((1,))],
    )(me, norm_gain, wg, wu, wd, *received)
    experts = (norm_gain, wg, wu, in_vmem(wd))
    parts, own = lax.optimization_barrier((parts, own))
    flag = SMEM((1,), jnp.int32)
    table_of = lambda kept: VMEM((devices * kept, LANES), F32)
    wide = lambda kept: VMEM((devices * kept * tiles, LANES), F32)
    cols_of = VMEM((devices // GROUP * slots, LANES), F32)
    sizes = dict(sections=sections, feats=feats, tiles=tiles)
    carry = call(
        functools.partial(table_kernel, **sizes),
        [state, cols_of, compact(early_kept), table_of(early_kept)],
        [VMEM] * 2,
        [VMEM] * 4,
        "table",
        scratch=[wide(early_kept)],
    )(own, swap(parts))

    def turn(x, cols, packed, table, kept):
        parts, more = call(
            functools.partial(round_kernel, **sizes),
            [compact(kept), flag],
            [VMEM] * 5,
            [VMEM, SMEM],
            "round",
            scratch=[wide(kept)],
        )(*experts, swap(packed))
        return more, *call(
            functools.partial(update_kernel, slots=slots, **sizes),
            [state, cols_of, compact(later_kept), table_of(later_kept)],
            [VMEM] * 4,
            [VMEM] * 4,
            "update",
            aliases={0: 0, 1: 1, 3: 3} if kept == later_kept else {0: 0, 1: 1},
            scratch=[wide(kept), wide(later_kept)],
        )(x, in_vmem(cols), swap(parts), in_vmem(table))

    def body(carry):
        return turn(*lax.optimization_barrier(carry)[1:], later_kept)

    carry = lax.while_loop(lambda c: c[0][0] > 0, body, turn(*carry, early_kept))
    x = carry[1]
    return x[:, :feats].reshape(ways, micro, tokens, feats)


def solution(mesh):
    return jax.shard_map(
        on_device,
        mesh=mesh,
        in_specs=(
            P(None, None, "expert", None),
            P("section", None),
            P("section", None, "expert"),
            P("section", None, "expert"),
            P("section", "expert", None),
            P(None, None, "section", "expert", None),
            P(None, None, "section", "expert", None),
        ),
        out_specs=P(None, None, "expert", "section"),
        check_vma=False,
    )
```

```python
import functools

import jax
import jax.numpy as jnp
from jax import lax
from jax.experimental import pallas as pl
from jax.experimental.pallas import tpu as pltpu
from jax.sharding import PartitionSpec as P

GROUP = 2
CAP = 2
EARLY = 2

norm_eps = 1e-06
route_scale = 2.5

F32 = jnp.float32
BF16 = jnp.bfloat16
LANES = 128
AXES = ("section", "expert")

VMEM = pltpu.VMEM
HBM = pltpu.HBM
SMEM = pltpu.SMEM


def iota(shape, dim):
    return lax.broadcasted_iota(jnp.int32, shape, dim)


def start(*copies):
    for copy in copies:
        copy.start()
    return copies


def mm(a, b):
    return jnp.dot(a, b, preferred_element_type=F32)


def route_kernel(place_ref, ids_hbm, scores_hbm, x_hbm, w_hbm, *refs, window, slots, early):
    spread = len(refs) - 6
    outs, w_ref = refs[:spread], refs[spread]
    ids_ref, scores_ref, x_ref, rows_ref, sems = refs[spread + 1:]
    pairs = ((ids_hbm, ids_ref), (scores_hbm, scores_ref), (x_hbm, x_ref))
    copies = start(*[pltpu.make_async_copy(a, b, sems.at[n]) for n, (a, b) in enumerate(pairs)])
    ahead, = start(pltpu.make_async_copy(w_hbm.at[:early], w_ref.at[:early], sems.at[3]))
    groups, topk, tokens = ids_ref.shape
    count, width = x_ref.shape
    block_of = lambda v: jnp.floor((v.astype(F32) + 0.5) * (1.0 / tokens))
    place_i = iota((count, count), 0)
    place_j = iota((count, count), 1)
    earlier = ((place_i < place_j) & (block_of(place_i) == block_of(place_j))).astype(BF16)
    token_lane = iota((slots, count), 1).astype(F32)
    slot_row = iota((slots, count), 0).astype(F32)
    base = block_of(iota((1, count), 1)) * CAP
    meta_lane = iota((slots, LANES), 1)
    copies[0].wait()
    copies[1].wait()
    across = lambda ref: jnp.concatenate([ref[g] for g in range(groups)], axis=1)
    ids = across(ids_ref)
    scores = across(scores_ref)
    weights = route_scale * scores / jnp.sum(scores, axis=0, keepdims=True)
    same = [ids == e for e in range(window)]
    hits = jnp.concatenate([jnp.sum(jnp.where(m, 1.0, 0.0), axis=0, keepdims=True) for m in same], axis=0)
    before = mm(hits.astype(BF16), earlier)
    picks = []
    for e in range(window):
        share = jnp.sum(jnp.where(same[e], weights, 0.0), axis=0, keepdims=True)
        pick = jnp.where(base + before[e:e + 1] == slot_row, hits[e:e + 1], 0.0)
        picks.append(pick.astype(BF16))
        token = jnp.sum(pick * token_lane + pick, axis=-1, keepdims=True) - 1.0
        w = jnp.sum(pick * share, axis=-1, keepdims=True)
        high = w.astype(BF16).astype(F32)
        mid = (w - high).astype(BF16).astype(F32)
        low = w - high - mid
        meta = jnp.where(meta_lane == 0, token, 0.0)
        meta = jnp.where(meta_lane == 1, high, meta)
        meta = jnp.where(meta_lane == 2, mid, meta)
        meta = jnp.where(meta_lane == 3, low, meta)
        rows_ref[e, :, width:] = meta.astype(BF16)
    copies[2].wait()
    x = x_ref[...]
    for e in range(window):
        rows_ref[e, :, :width] = mm(picks[e], x).astype(BF16)
    me = lax.rem(place_ref[0], spread)
    for k in range(spread):
        peer = lax.rem(me + k, spread)
        outs[k][...] = rows_ref[lax.div(peer, GROUP)]
    ahead.wait()


def load_kernel(place_ref, x_hbm, wg_hbm, wu_hbm, own_ref, wg_ref, wu_ref, piece_ref, sems, *, spread, feats):
    section = lax.div(place_ref[0], spread)
    tokens, padded = own_ref.shape
    span = piece_ref.shape[1]
    width = x_hbm.shape[1]
    first = jnp.minimum(lax.div(section * feats, LANES), (width - span) // LANES) * LANES
    piece, *weights = start(
        pltpu.make_async_copy(x_hbm.at[:, pl.ds(pl.multiple_of(first, LANES), span)], piece_ref, sems.at[0]),
        pltpu.make_async_copy(wg_hbm, wg_ref, sems.at[1]),
        pltpu.make_async_copy(wu_hbm, wu_ref, sems.at[2]),
    )
    piece.wait()
    moved = pltpu.roll(piece_ref[...].astype(F32), lax.rem(span - (section * feats - first), span), 1)[:, :padded]
    own_ref[...] = jnp.where(iota((tokens, padded), 1) < feats, moved, 0.0).astype(BF16)
    for weight in weights:
        weight.wait()


def silu_times(gate, up):
    return (gate / (1.0 + jnp.exp(-gate)) * up).astype(BF16)


def first_kernel(place_ref, gain_ref, wg_ref, wu_ref, wd_hbm, begun_ref, *refs, sections, feats, early):
    spread = len(refs) - 3
    ins, out_ref, wd_ref, sems = refs[:spread], refs[spread], refs[spread + 1], refs[spread + 2]
    copy, = start(pltpu.make_async_copy(wd_hbm.at[early:], wd_ref.at[early:], sems.at[0]))
    width = gain_ref.shape[1]
    slots = ins[0].shape[0]
    room = out_ref.shape[2] - feats
    x = jnp.concatenate([r[:, :width].astype(F32) for r in ins], axis=0)
    mean = jnp.mean(x * x, axis=-1, keepdims=True)
    h = (x * lax.rsqrt(mean + norm_eps) * gain_ref[...]).astype(BF16)
    act = silu_times(mm(h, wg_ref[...]), mm(h, wu_ref[...]))
    copy.wait()
    part = mm(act, wd_ref[...]).astype(BF16)
    me = lax.rem(place_ref[0], spread)
    for k in range(spread):
        block = lax.rem(me - k + spread, spread)
        meta = ins[k][:, width:width + room]
        for s in range(sections):
            out_ref[s * spread + block, :, :feats] = part[k * slots:(k + 1) * slots, s * feats:(s + 1) * feats]
            out_ref[s * spread + block, :, feats:] = meta


def all_layers(pieces, gain_ref, wg_ref, wu_ref, wd_ref, beside=None):
    rows, feats = pieces[0].shape
    total = jnp.zeros((rows, 1), F32)
    for piece in pieces:
        total = total + jnp.sum(piece * piece, axis=-1, keepdims=True)
    scale = lax.rsqrt(total * (1.0 / (feats * len(pieces))) + norm_eps)
    gate = jnp.zeros((rows, wg_ref.shape[1]), F32)
    up = jnp.zeros((rows, wg_ref.shape[1]), F32)
    for s, piece in enumerate(pieces):
        here = slice(s * feats, (s + 1) * feats)
        h = (piece * scale * gain_ref[:, here]).astype(BF16)
        gate = gate + mm(h, wg_ref[here, :])
        up = up + mm(h, wu_ref[here, :])
        if beside is not None:
            next(beside, None)
    return mm(silu_times(gate, up), wd_ref[...])


def round_kernel(
    gain_ref, wg_ref, wu_ref, wd_ref, in_ref, cols_ref, out_ref, more, cols_out, table_out, wide_ref, *,
    sections, feats, tiles, tokens, slots
):
    count, sub, lanes = in_ref.shape
    spread = count // sections
    rows = spread * (sub // tiles)
    span = spread * sub
    wide_ref[...] = in_ref[...].astype(F32).reshape(count * sub, lanes)
    at = lambda s, k: pl.ds(s * span + k, rows, stride=tiles)
    spare = feats - (tiles - 1) * lanes
    more[0] = jnp.max(wide_ref[at(0, tiles - 1), :][:, spare:spare + 1]).astype(jnp.int32)
    pieces = []
    for s in range(sections):
        pieces.append(jnp.concatenate([wide_ref[at(s, k), :] for k in range(tiles)], axis=1)[:, :feats])
    chosen = []
    steps = select_steps(chosen, cols_ref[...], tokens, table_out.shape[0] // count, count, sections, slots)
    part = all_layers(pieces, gain_ref, wg_ref, wu_ref, wd_ref, steps)
    for unused in steps:
        pass
    cols, table = chosen
    cols_out[...] = cols
    table_out[...] = table
    for s in range(sections):
        piece = part[:, s * feats:(s + 1) * feats]
        piece = jnp.concatenate([piece, jnp.zeros((rows, tiles * lanes - feats), F32)], axis=1)
        for k in range(tiles):
            wide_ref[at(s, k), :] = piece[:, k * lanes:(k + 1) * lanes]
    out_ref[...] = wide_ref[...].reshape(count, sub, lanes).astype(BF16)


def add_parts(table, parts, x, feats):
    tokens, padded = x.shape
    across = table.T[:8]
    chosen = iota((tokens, across.shape[1]), 0).astype(F32) + 1.0 == across[0:1]
    terms = jnp.concatenate([jnp.where(chosen, across[n:n + 1], 0.0) for n in (1, 2, 3)], axis=0)
    added = mm(terms.astype(BF16), parts)
    added = added[:tokens] + added[tokens:2 * tokens] + added[2 * tokens:]
    return jnp.where(iota((tokens, padded), 1) < feats, x.astype(F32) + added, 0.0).astype(BF16)


def find_ready(cols, tokens, sections):
    per = cols.shape[0] // sections
    pick = (iota((cols.shape[0], tokens), 1).astype(F32) == cols[:, 0:1]).astype(F32)
    pending = cols[:, 4:5]
    layer = lambda v, l: v[l * per:(l + 1) * per]
    waits = [jnp.minimum(jnp.sum(layer(pick, l) * layer(pending, l), axis=0, keepdims=True), 1.0) for l in range(sections)]
    ahead, behind = [None] * sections, [None] * sections
    run_a = run_b = jnp.zeros((1, tokens), F32)
    for l in range(sections):
        ahead[l] = run_a
        run_a = run_a + waits[l]
        m = sections - 1 - l
        behind[m] = run_b
        run_b = run_b + waits[m]
    forward = iota((1, tokens), 1) < tokens // 2
    ready = []
    for l in range(sections):
        free = jnp.where(jnp.where(forward, ahead[l], behind[l]) == 0.0, waits[l], 0.0)
        ready.append(jnp.sum(layer(pick, l) * free, axis=-1, keepdims=True))
    return jnp.concatenate(ready, axis=0), pick


def values_of(cols, taken):
    lane = iota(cols.shape, 1)
    return jnp.where(taken & (lane < 4), jnp.where(lane == 0, cols + 1.0, cols), 0.0)


def select_steps(result, cols, tokens, kept, count, sections, slots):
    total = cols.shape[0]
    per = total // sections
    ready, pick = find_ready(cols, tokens, sections)
    yield
    slot = lax.rem(iota((total, LANES), 0), slots)
    seen = jnp.broadcast_to(ready, (total, LANES))
    shift = 1
    while shift < slots:
        seen = seen + jnp.where(slot >= shift, pltpu.roll(seen, shift, 0), 0.0)
        shift *= 2
    yield
    late = jnp.where(seen[:, 0:1] > kept, ready, 0.0)
    held = []
    for l in range(sections):
        here = slice(l * per, (l + 1) * per)
        wait = jnp.sum(pick[here] * late[here], axis=0, keepdims=True)
        held.append(jnp.sum(pick[here] * wait, axis=-1, keepdims=True))
    yield
    taken = jnp.where(jnp.concatenate(held, axis=0) == 0.0, ready, 0.0)
    cols = jnp.where(iota((total, LANES), 1) == 4, cols - taken, cols)
    left = jnp.max(cols[:, 4:5], axis=0, keepdims=True)
    group_of = lambda v, size: jnp.floor((v.astype(F32) + 0.5) * (1.0 / size))
    owner = (group_of(iota((count, total), 0), GROUP) == group_of(iota((count, total), 1), slots)).astype(BF16)
    tables = []
    yield
    for c in range(kept):
        mine = values_of(cols, (taken > 0.0) & (seen == c + 1.0))
        tables.append(mm(owner, mine.astype(BF16)))
    table = jnp.concatenate(tables, axis=0)
    result[:] = cols, jnp.where(iota(table.shape, 1) == 4, left, table)


def select(*args):
    result = []
    for unused in select_steps(result, *args):
        pass
    return result


def pack_rows(table, x, send_ref, wide_ref, feats, tiles):
    count, sub, lanes = send_ref.shape
    kept = sub // tiles
    tokens, padded = x.shape
    chosen = (iota((kept * count, tokens), 1).astype(F32) + 1.0 == table[:, 0:1]).astype(BF16)
    rows = jnp.where(iota((kept * count, padded), 1) == feats, table[:, 4:5], mm(chosen, x))
    for c in range(kept):
        for k in range(tiles):
            wide_ref[pl.ds(c * tiles + k, count, stride=sub), :] = rows[c * count:(c + 1) * count, k * lanes:(k + 1) * lanes]
    send_ref[...] = wide_ref[...].reshape(count, sub, lanes).astype(BF16)


def table_kernel(x_ref, in_ref, x_out, cols_out, send_out, table_out, wide_ref, *, sections, feats, tiles):
    count, slots, padded = in_ref.shape
    tokens = x_ref.shape[0]
    groups = count // GROUP
    parts = in_ref[...].reshape(count * slots, padded)
    meta = [parts[g * GROUP * slots:(g * GROUP + 1) * slots, feats:feats + 4].astype(F32) for g in range(groups)]
    meta = jnp.concatenate(meta, axis=0)
    lane = iota((groups * slots, LANES), 1)
    cols = jnp.where(lane == 0, meta[:, 0:1], 0.0)
    for n in (1, 2, 3):
        cols = jnp.where(lane == n, meta[:, n:n + 1], cols)
    cols = jnp.where((lane == 4) & (meta[:, 0:1] >= 0.0), 1.0, cols)
    ready, unused = find_ready(cols, tokens, sections)
    mine = values_of(cols, ready > 0.0)
    table = jnp.concatenate([mine[g * slots:(g + 1) * slots] for g in range(groups) for n in range(GROUP)], axis=0)
    x = add_parts(table, parts, x_ref[...], feats)
    x_out[...] = x
    cols = jnp.where(lane == 4, cols - ready, cols)
    cols, table = select(cols, tokens, table_out.shape[0] // count, count, sections, slots)
    cols_out[...] = cols
    table_out[...] = table
    pack_rows(table, x, send_out, wide_ref, feats, tiles)


def update_kernel(
    more, x_ref, in_ref, tab_ref, next_ref, *refs, feats, tiles
):
    x_out, send_out, table_out, done_hbm, in_wide, out_wide, done_ref, sems = refs[-8:]
    count, sub, lanes = in_ref.shape
    in_wide[...] = in_ref[...].astype(F32).reshape(count * sub, lanes)
    at = lambda c, k: pl.ds(c * tiles + k, count, stride=sub)
    parts = jnp.concatenate(
        [jnp.concatenate([in_wide[at(c, k), :] for k in range(tiles)], axis=1) for c in range(sub // tiles)], axis=0
    ).astype(BF16)
    x = add_parts(tab_ref[...], parts, x_ref[...], feats)
    x_out[...] = x
    table = next_ref[...]
    table_out[...] = table

    @pl.when(more[0] > 0)
    def forward():
        pack_rows(table, x, send_out, out_wide, feats, tiles)

    @pl.when(more[0] <= 0)
    def finish():
        done_ref[...] = x[:, :feats]
        done, = start(pltpu.make_async_copy(done_ref, done_hbm, sems.at[0]))
        done.wait()


def call(kernel, out_shape, in_spaces, out_spaces, name, scratch=(), limit=24 * 2**20, aliases={}):
    spec = lambda space: pl.BlockSpec(memory_space=space)
    single = not isinstance(out_shape, (list, tuple))
    return pl.pallas_call(
        kernel,
        out_shape=out_shape,
        in_specs=[spec(s) for s in in_spaces],
        out_specs=spec(out_spaces[0]) if single else [spec(s) for s in out_spaces],
        scratch_shapes=list(scratch),
        input_output_aliases=aliases,
        compiler_params=pltpu.CompilerParams(vmem_limit_bytes=limit),
        name=name,
    )


def on_device(entering, norm_gain, w_gate, w_up, w_down, route_ids, route_scores):
    sections = lax.axis_size("section")
    spread = lax.axis_size("expert")
    window = spread // GROUP
    ways, micro, tokens, width = entering.shape
    everyone = ways * micro * tokens
    slots = ways * micro * CAP
    feats = width // sections
    tiles = feats // LANES + 1
    padded = tiles * LANES
    devices = sections * spread
    later_kept = max(1, 8 // tiles)
    early_kept = min(slots, 2 * later_kept)
    by_token = lambda v: jnp.swapaxes(v[:, :, 0], 2, 3).reshape(ways * micro, v.shape[-1], tokens)
    in_hbm = lambda v: pltpu.with_memory_space_constraint(v, HBM)
    in_vmem = lambda v: pltpu.with_memory_space_constraint(v, VMEM)
    sds = jax.ShapeDtypeStruct
    dma = pltpu.SemaphoreType.DMA

    place = lax.axis_index(AXES).astype(jnp.int32).reshape(1)
    flat = in_hbm(entering.reshape(everyone, width))
    ids, scores = in_hbm(by_token(route_ids)), in_hbm(by_token(route_scores))
    wg, wu, wd = [in_hbm(v[0]) for v in (w_gate, w_up, w_down)]
    resident = lambda v: VMEM(v.shape, v.dtype)

    early = wd.shape[0] // EARLY
    *rows, begun = call(
        functools.partial(route_kernel, window=window, slots=slots, early=early),
        [sds((slots, width + LANES), BF16)] * spread + [resident(wd)],
        [SMEM] + [HBM] * 4,
        [VMEM] * (spread + 1),
        "route",
        scratch=[
            VMEM(ids.shape, ids.dtype),
            VMEM(scores.shape, scores.dtype),
            VMEM((everyone, width), BF16),
            VMEM((window, slots, width + LANES), BF16),
            dma((4,)),
        ],
    )(place, ids, scores, flat, wd)
    received = [rows[0]] + [
        lax.ppermute(rows[k], "expert", [(y, (y + k) % spread) for y in range(spread)]) for k in range(1, spread)
    ]
    reach = max(s * feats % LANES for s in range(sections)) + feats
    span = -(-reach // LANES) * LANES
    state = sds((everyone, padded), BF16)
    own, wg, wu = call(
        functools.partial(load_kernel, spread=spread, feats=feats),
        [state, resident(wg), resident(wu)],
        [SMEM] + [HBM] * 3,
        [VMEM] * 3,
        "load",
        scratch=[VMEM((everyone, span), BF16), dma((3,))],
    )(place, flat, wg, wu)
    wg, wu = in_vmem(wg), in_vmem(wu)
    message = sds((devices, slots, padded), BF16)
    compact = lambda kept: sds((devices, kept * tiles, LANES), BF16)
    swap = lambda v: lax.all_to_all(v, AXES, split_axis=0, concat_axis=0, tiled=True)
    parts, wd = call(
        functools.partial(first_kernel, sections=sections, feats=feats, early=early),
        [message, resident(wd)],
        [SMEM] + [VMEM] * 3 + [HBM] + [VMEM] * (1 + spread),
        [VMEM] * 2,
        "first",
        aliases={5: 1},
        scratch=[dma((1,))],
    )(place, norm_gain, wg, wu, wd, in_vmem(begun), *received)
    experts = (norm_gain, wg, wu, in_vmem(wd))
    parts, own = lax.optimization_barrier((parts, own))
    flag = SMEM((1,), jnp.int32)
    table_of = lambda kept: VMEM((devices * kept, LANES), F32)
    wide = lambda kept: VMEM((devices * kept * tiles, LANES), F32)
    cols_of = VMEM((devices // GROUP * slots, LANES), F32)
    sizes = dict(sections=sections, feats=feats, tiles=tiles)
    carry = call(
        functools.partial(table_kernel, **sizes),
        [state, cols_of, compact(early_kept), table_of(early_kept)],
        [VMEM] * 2,
        [VMEM] * 4,
        "table",
        scratch=[wide(early_kept)],
    )(own, swap(parts))

    whole = HBM((everyone, feats), BF16)

    def turn(x, cols, packed, table, kept, *done):
        parts, more, cols, following = call(
            functools.partial(round_kernel, tokens=everyone, slots=slots, **sizes),
            [compact(kept), flag, cols_of, table_of(later_kept)],
            [VMEM] * 6,
            [VMEM, SMEM, VMEM, VMEM],
            "round",
            aliases={5: 2},
            scratch=[wide(kept)],
        )(*experts, swap(packed), in_vmem(cols))
        x, packed, table, done = call(
            functools.partial(update_kernel, feats=feats, tiles=tiles),
            [state, compact(later_kept), table_of(later_kept), whole],
            [SMEM] + [VMEM] * 4 + [HBM] * len(done),
            [VMEM] * 3 + [HBM],
            "update",
            aliases={1: 0, 3: 2, 5: 3} if done else {1: 0},
            scratch=[wide(kept), wide(later_kept), VMEM((everyone, feats), BF16), dma((1,))],
        )(more, x, swap(parts), in_vmem(table), in_vmem(following), *[in_hbm(v) for v in done])
        return more, x, cols, packed, table, done

    def body(carry):
        unused, x, cols, packed, table, done = lax.optimization_barrier(carry)
        return turn(x, cols, packed, table, later_kept, done)

    carry = lax.while_loop(lambda c: c[0][0] > 0, body, turn(*carry, early_kept))
    return carry[5].reshape(ways, micro, tokens, feats)


def solution(mesh):
    return jax.shard_map(
        on_device,
        mesh=mesh,
        in_specs=(
            P(None, None, "expert", None),
            P("section", None),
            P("section", None, "expert"),
            P("section", None, "expert"),
            P("section", "expert", None),
            P(None, None, "section", "expert", None),
            P(None, None, "section", "expert", None),
        ),
        out_specs=P(None, None, "expert", "section"),
        check_vma=False,
    )
```

```python
import functools

import jax
import jax.numpy as jnp
from jax import lax
from jax.experimental import pallas as pl
from jax.experimental.pallas import tpu as pltpu
from jax.sharding import PartitionSpec as P

GROUP = 2
CAP = 2
EARLY = 2

norm_eps = 1e-06
route_scale = 2.5

F32 = jnp.float32
BF16 = jnp.bfloat16
LANES = 128
AXES = ("section", "expert")

VMEM = pltpu.VMEM
HBM = pltpu.HBM
SMEM = pltpu.SMEM


def iota(shape, dim):
    return lax.broadcasted_iota(jnp.int32, shape, dim)


def start(*copies):
    for copy in copies:
        copy.start()
    return copies


def mm(a, b):
    return jnp.dot(a, b, preferred_element_type=F32)


def route_kernel(place_ref, ids_hbm, scores_hbm, x_hbm, w_hbm, *refs, window, slots, early):
    spread = len(refs) - 6
    outs, w_ref = refs[:spread], refs[spread]
    ids_ref, scores_ref, x_ref, rows_ref, sems = refs[spread + 1:]
    pairs = ((ids_hbm, ids_ref), (scores_hbm, scores_ref), (x_hbm, x_ref))
    copies = start(*[pltpu.make_async_copy(a, b, sems.at[n]) for n, (a, b) in enumerate(pairs)])
    ahead, = start(pltpu.make_async_copy(w_hbm.at[:early], w_ref.at[:early], sems.at[3]))
    groups, topk, tokens = ids_ref.shape
    count, width = x_ref.shape
    block_of = lambda v: jnp.floor((v.astype(F32) + 0.5) * (1.0 / tokens))
    place_i = iota((count, count), 0)
    place_j = iota((count, count), 1)
    earlier = ((place_i < place_j) & (block_of(place_i) == block_of(place_j))).astype(BF16)
    token_lane = iota((slots, count), 1).astype(F32)
    slot_row = iota((slots, count), 0).astype(F32)
    base = block_of(iota((1, count), 1)) * CAP
    meta_lane = iota((slots, LANES), 1)
    copies[0].wait()
    copies[1].wait()
    across = lambda ref: jnp.concatenate([ref[g] for g in range(groups)], axis=1)
    ids = across(ids_ref)
    scores = across(scores_ref)
    weights = route_scale * scores / jnp.sum(scores, axis=0, keepdims=True)
    same = [ids == e for e in range(window)]
    hits = jnp.concatenate([jnp.sum(jnp.where(m, 1.0, 0.0), axis=0, keepdims=True) for m in same], axis=0)
    before = mm(hits.astype(BF16), earlier)
    picks = []
    for e in range(window):
        share = jnp.sum(jnp.where(same[e], weights, 0.0), axis=0, keepdims=True)
        pick = jnp.where(base + before[e:e + 1] == slot_row, hits[e:e + 1], 0.0)
        picks.append(pick.astype(BF16))
        token = jnp.sum(pick * token_lane + pick, axis=-1, keepdims=True) - 1.0
        w = jnp.sum(pick * share, axis=-1, keepdims=True)
        high = w.astype(BF16).astype(F32)
        mid = (w - high).astype(BF16).astype(F32)
        low = w - high - mid
        meta = jnp.where(meta_lane == 0, token, 0.0)
        meta = jnp.where(meta_lane == 1, high, meta)
        meta = jnp.where(meta_lane == 2, mid, meta)
        meta = jnp.where(meta_lane == 3, low, meta)
        rows_ref[e, :, width:] = meta.astype(BF16)
    copies[2].wait()
    x = x_ref[...]
    for e in range(window):
        rows_ref[e, :, :width] = mm(picks[e], x).astype(BF16)
    me = lax.rem(place_ref[0], spread)
    for k in range(spread):
        peer = lax.rem(me + k, spread)
        outs[k][...] = rows_ref[lax.div(peer, GROUP)]
    ahead.wait()


def load_kernel(place_ref, x_hbm, wg_hbm, wu_hbm, own_ref, wg_ref, wu_ref, piece_ref, sems, *, spread, feats):
    section = lax.div(place_ref[0], spread)
    tokens, padded = own_ref.shape
    span = piece_ref.shape[1]
    width = x_hbm.shape[1]
    first = jnp.minimum(lax.div(section * feats, LANES), (width - span) // LANES) * LANES
    piece, *weights = start(
        pltpu.make_async_copy(x_hbm.at[:, pl.ds(pl.multiple_of(first, LANES), span)], piece_ref, sems.at[0]),
        pltpu.make_async_copy(wg_hbm, wg_ref, sems.at[1]),
        pltpu.make_async_copy(wu_hbm, wu_ref, sems.at[2]),
    )
    piece.wait()
    moved = pltpu.roll(piece_ref[...].astype(F32), lax.rem(span - (section * feats - first), span), 1)[:, :padded]
    own_ref[...] = jnp.where(iota((tokens, padded), 1) < feats, moved, 0.0).astype(BF16)
    for weight in weights:
        weight.wait()


def silu_times(gate, up):
    return (gate / (1.0 + jnp.exp(-gate)) * up).astype(BF16)


def first_kernel(place_ref, gain_ref, wg_ref, wu_ref, wd_hbm, begun_ref, *refs, sections, feats, early):
    spread = len(refs) - 3
    ins, out_ref, wd_ref, sems = refs[:spread], refs[spread], refs[spread + 1], refs[spread + 2]
    copy, = start(pltpu.make_async_copy(wd_hbm.at[early:], wd_ref.at[early:], sems.at[0]))
    width = gain_ref.shape[1]
    slots = ins[0].shape[0]
    room = out_ref.shape[2] - feats
    x = jnp.concatenate([r[:, :width].astype(F32) for r in ins], axis=0)
    mean = jnp.mean(x * x, axis=-1, keepdims=True)
    h = (x * lax.rsqrt(mean + norm_eps) * gain_ref[...]).astype(BF16)
    act = silu_times(mm(h, wg_ref[...]), mm(h, wu_ref[...]))
    copy.wait()
    part = mm(act, wd_ref[...]).astype(BF16)
    me = lax.rem(place_ref[0], spread)
    for k in range(spread):
        block = lax.rem(me - k + spread, spread)
        meta = ins[k][:, width:width + room]
        for s in range(sections):
            out_ref[s * spread + block, :, :feats] = part[k * slots:(k + 1) * slots, s * feats:(s + 1) * feats]
            out_ref[s * spread + block, :, feats:] = meta


def all_layers(pieces, gain_ref, wg_ref, wu_ref, wd_ref, beside=None):
    rows, feats = pieces[0].shape
    total = jnp.zeros((rows, 1), F32)
    for piece in pieces:
        total = total + jnp.sum(piece * piece, axis=-1, keepdims=True)
    scale = lax.rsqrt(total * (1.0 / (feats * len(pieces))) + norm_eps)
    gate = jnp.zeros((rows, wg_ref.shape[1]), F32)
    up = jnp.zeros((rows, wg_ref.shape[1]), F32)
    for s, piece in enumerate(pieces):
        here = slice(s * feats, (s + 1) * feats)
        h = (piece * scale * gain_ref[:, here]).astype(BF16)
        gate = gate + mm(h, wg_ref[here, :])
        up = up + mm(h, wu_ref[here, :])
        if beside is not None:
            next(beside, None)
    return mm(silu_times(gate, up), wd_ref[...])


def round_kernel(
    gain_ref, wg_ref, wu_ref, wd_ref, in_ref, cols_ref, out_ref, more, cols_out, table_out, wide_ref, *,
    sections, feats, tiles, tokens, slots
):
    count, sub, lanes = in_ref.shape
    spread = count // sections
    rows = spread * (sub // tiles)
    span = spread * sub
    wide_ref[...] = in_ref[...].astype(F32).reshape(count * sub, lanes)
    at = lambda s, k: pl.ds(s * span + k, rows, stride=tiles)
    spare = feats - (tiles - 1) * lanes
    more[0] = jnp.max(wide_ref[at(0, tiles - 1), :][:, spare:spare + 1]).astype(jnp.int32)
    pieces = []
    for s in range(sections):
        pieces.append(jnp.concatenate([wide_ref[at(s, k), :] for k in range(tiles)], axis=1)[:, :feats])
    chosen = []
    steps = select_steps(chosen, cols_ref[...], tokens, table_out.shape[0] // count, count, sections, slots)
    part = all_layers(pieces, gain_ref, wg_ref, wu_ref, wd_ref, steps)
    for unused in steps:
        pass
    cols, table = chosen
    cols_out[...] = cols
    table_out[...] = table
    for s in range(sections):
        piece = part[:, s * feats:(s + 1) * feats]
        piece = jnp.concatenate([piece, jnp.zeros((rows, tiles * lanes - feats), F32)], axis=1)
        for k in range(tiles):
            wide_ref[at(s, k), :] = piece[:, k * lanes:(k + 1) * lanes]
    out_ref[...] = wide_ref[...].reshape(count, sub, lanes).astype(BF16)


def add_parts(table, parts, x, feats):
    tokens, padded = x.shape
    across = table.T[:8]
    chosen = iota((tokens, across.shape[1]), 0).astype(F32) + 1.0 == across[0:1]
    terms = jnp.concatenate([jnp.where(chosen, across[n:n + 1], 0.0) for n in (1, 2, 3)], axis=0)
    added = mm(terms.astype(BF16), parts)
    added = added[:tokens] + added[tokens:2 * tokens] + added[2 * tokens:]
    return jnp.where(iota((tokens, padded), 1) < feats, x.astype(F32) + added, 0.0).astype(BF16)


def find_ready(cols, tokens, sections):
    per = cols.shape[0] // sections
    pick = (iota((cols.shape[0], tokens), 1).astype(F32) == cols[:, 0:1]).astype(F32)
    pending = cols[:, 4:5]
    layer = lambda v, l: v[l * per:(l + 1) * per]
    waits = [jnp.minimum(jnp.sum(layer(pick, l) * layer(pending, l), axis=0, keepdims=True), 1.0) for l in range(sections)]
    ahead, behind = [None] * sections, [None] * sections
    run_a = run_b = jnp.zeros((1, tokens), F32)
    for l in range(sections):
        ahead[l] = run_a
        run_a = run_a + waits[l]
        m = sections - 1 - l
        behind[m] = run_b
        run_b = run_b + waits[m]
    forward = iota((1, tokens), 1) < tokens // 2
    ready = []
    for l in range(sections):
        free = jnp.where(jnp.where(forward, ahead[l], behind[l]) == 0.0, waits[l], 0.0)
        ready.append(jnp.sum(layer(pick, l) * free, axis=-1, keepdims=True))
    return jnp.concatenate(ready, axis=0), pick, run_a


def values_of(cols, taken):
    lane = iota(cols.shape, 1)
    return jnp.where(taken & (lane < 4), jnp.where(lane == 0, cols + 1.0, cols), 0.0)


def select_steps(result, cols, tokens, kept, count, sections, slots):
    total = cols.shape[0]
    per = total // sections
    ready, pick, waits = find_ready(cols, tokens, sections)
    yield
    group_of = lambda v, size: jnp.floor((v.astype(F32) + 0.5) * (1.0 / size))
    row = iota((total, 1), 0)
    urgent = jnp.sum(pick * waits, axis=-1, keepdims=True) * slots + (slots - lax.rem(row, slots)).astype(F32)
    apart = 4.0 * slots * sections
    key = jnp.where(ready > 0.0, urgent, 0.0) + group_of(row, slots) * apart
    yield
    ahead = jnp.broadcast_to(key, (total, LANES)).T[0:1] - key
    rank = jnp.sum(jnp.where((ahead > 0.0) & (ahead < 0.5 * apart), 1.0, 0.0), axis=-1, keepdims=True)
    late = jnp.where(rank >= kept, ready, 0.0)
    yield
    held = []
    for l in range(sections):
        here = slice(l * per, (l + 1) * per)
        wait = jnp.sum(pick[here] * late[here], axis=0, keepdims=True)
        held.append(jnp.sum(pick[here] * wait, axis=-1, keepdims=True))
    yield
    taken = jnp.where(jnp.concatenate(held, axis=0) == 0.0, ready, 0.0)
    cols = jnp.where(iota((total, LANES), 1) == 4, cols - taken, cols)
    left = jnp.max(cols[:, 4:5], axis=0, keepdims=True)
    owner = (group_of(iota((count, total), 0), GROUP) == group_of(iota((count, total), 1), slots)).astype(BF16)
    yield
    tables = []
    for c in range(kept):
        mine = values_of(cols, (taken > 0.0) & (rank == c))
        tables.append(mm(owner, mine.astype(BF16)))
    table = jnp.concatenate(tables, axis=0)
    result[:] = cols, jnp.where(iota(table.shape, 1) == 4, left, table)


def select(*args):
    result = []
    for unused in select_steps(result, *args):
        pass
    return result


def pack_rows(table, x, send_ref, wide_ref, feats, tiles):
    count, sub, lanes = send_ref.shape
    kept = sub // tiles
    tokens, padded = x.shape
    chosen = (iota((kept * count, tokens), 1).astype(F32) + 1.0 == table[:, 0:1]).astype(BF16)
    rows = jnp.where(iota((kept * count, padded), 1) == feats, table[:, 4:5], mm(chosen, x))
    for c in range(kept):
        for k in range(tiles):
            wide_ref[pl.ds(c * tiles + k, count, stride=sub), :] = rows[c * count:(c + 1) * count, k * lanes:(k + 1) * lanes]
    send_ref[...] = wide_ref[...].reshape(count, sub, lanes).astype(BF16)


def table_kernel(x_ref, in_ref, more, x_out, cols_out, send_out, table_out, done_hbm, wide_ref, *, sections, feats, tiles):
    more[0] = 1
    count, slots, padded = in_ref.shape
    tokens = x_ref.shape[0]
    groups = count // GROUP
    parts = in_ref[...].reshape(count * slots, padded)
    meta = [parts[g * GROUP * slots:(g * GROUP + 1) * slots, feats:feats + 4].astype(F32) for g in range(groups)]
    meta = jnp.concatenate(meta, axis=0)
    lane = iota((groups * slots, LANES), 1)
    cols = jnp.where(lane == 0, meta[:, 0:1], 0.0)
    for n in (1, 2, 3):
        cols = jnp.where(lane == n, meta[:, n:n + 1], cols)
    cols = jnp.where((lane == 4) & (meta[:, 0:1] >= 0.0), 1.0, cols)
    ready, *unused = find_ready(cols, tokens, sections)
    mine = values_of(cols, ready > 0.0)
    table = jnp.concatenate([mine[g * slots:(g + 1) * slots] for g in range(groups) for n in range(GROUP)], axis=0)
    x = add_parts(table, parts, x_ref[...], feats)
    x_out[...] = x
    cols = jnp.where(lane == 4, cols - ready, cols)
    cols, table = select(cols, tokens, table_out.shape[0] // count, count, sections, slots)
    cols_out[...] = cols
    table_out[...] = table
    pack_rows(table, x, send_out, wide_ref, feats, tiles)


def update_kernel(
    more, x_ref, in_ref, tab_ref, next_ref, *refs, feats, tiles
):
    x_out, send_out, table_out, done_hbm, in_wide, out_wide, done_ref, sems = refs[-8:]
    count, sub, lanes = in_ref.shape
    in_wide[...] = in_ref[...].astype(F32).reshape(count * sub, lanes)
    at = lambda c, k: pl.ds(c * tiles + k, count, stride=sub)
    parts = jnp.concatenate(
        [jnp.concatenate([in_wide[at(c, k), :] for k in range(tiles)], axis=1) for c in range(sub // tiles)], axis=0
    ).astype(BF16)
    x = add_parts(tab_ref[...], parts, x_ref[...], feats)
    x_out[...] = x
    table = next_ref[...]
    table_out[...] = table

    @pl.when(more[0] > 0)
    def forward():
        pack_rows(table, x, send_out, out_wide, feats, tiles)

    @pl.when(more[0] <= 0)
    def finish():
        done_ref[...] = x[:, :feats]
        done, = start(pltpu.make_async_copy(done_ref, done_hbm, sems.at[0]))
        done.wait()


def call(kernel, out_shape, in_spaces, out_spaces, name, scratch=(), limit=24 * 2**20, aliases={}):
    spec = lambda space: pl.BlockSpec(memory_space=space)
    single = not isinstance(out_shape, (list, tuple))
    return pl.pallas_call(
        kernel,
        out_shape=out_shape,
        in_specs=[spec(s) for s in in_spaces],
        out_specs=spec(out_spaces[0]) if single else [spec(s) for s in out_spaces],
        scratch_shapes=list(scratch),
        input_output_aliases=aliases,
        compiler_params=pltpu.CompilerParams(vmem_limit_bytes=limit),
        name=name,
    )


def on_device(entering, norm_gain, w_gate, w_up, w_down, route_ids, route_scores):
    sections = lax.axis_size("section")
    spread = lax.axis_size("expert")
    window = spread // GROUP
    ways, micro, tokens, width = entering.shape
    everyone = ways * micro * tokens
    slots = ways * micro * CAP
    feats = width // sections
    tiles = feats // LANES + 1
    padded = tiles * LANES
    devices = sections * spread
    kept = max(1, 8 // tiles)
    by_token = lambda v: jnp.swapaxes(v[:, :, 0], 2, 3).reshape(ways * micro, v.shape[-1], tokens)
    in_hbm = lambda v: pltpu.with_memory_space_constraint(v, HBM)
    in_vmem = lambda v: pltpu.with_memory_space_constraint(v, VMEM)
    sds = jax.ShapeDtypeStruct
    dma = pltpu.SemaphoreType.DMA

    place = lax.axis_index(AXES).astype(jnp.int32).reshape(1)
    flat = in_hbm(entering.reshape(everyone, width))
    ids, scores = in_hbm(by_token(route_ids)), in_hbm(by_token(route_scores))
    wg, wu, wd = [in_hbm(v[0]) for v in (w_gate, w_up, w_down)]
    resident = lambda v: VMEM(v.shape, v.dtype)

    early = wd.shape[0] // EARLY
    *rows, begun = call(
        functools.partial(route_kernel, window=window, slots=slots, early=early),
        [sds((slots, width + LANES), BF16)] * spread + [resident(wd)],
        [SMEM] + [HBM] * 4,
        [VMEM] * (spread + 1),
        "route",
        scratch=[
            VMEM(ids.shape, ids.dtype),
            VMEM(scores.shape, scores.dtype),
            VMEM((everyone, width), BF16),
            VMEM((window, slots, width + LANES), BF16),
            dma((4,)),
        ],
    )(place, ids, scores, flat, wd)
    received = [rows[0]] + [
        lax.ppermute(rows[k], "expert", [(y, (y + k) % spread) for y in range(spread)]) for k in range(1, spread)
    ]
    reach = max(s * feats % LANES for s in range(sections)) + feats
    span = -(-reach // LANES) * LANES
    state = sds((everyone, padded), BF16)
    own, wg, wu = call(
        functools.partial(load_kernel, spread=spread, feats=feats),
        [state, resident(wg), resident(wu)],
        [SMEM] + [HBM] * 3,
        [VMEM] * 3,
        "load",
        scratch=[VMEM((everyone, span), BF16), dma((3,))],
    )(place, flat, wg, wu)
    wg, wu = in_vmem(wg), in_vmem(wu)
    message = sds((devices, slots, padded), BF16)
    compact = sds((devices, kept * tiles, LANES), BF16)
    swap = lambda v: lax.all_to_all(v, AXES, split_axis=0, concat_axis=0, tiled=True)
    parts, wd = call(
        functools.partial(first_kernel, sections=sections, feats=feats, early=early),
        [message, resident(wd)],
        [SMEM] + [VMEM] * 3 + [HBM] + [VMEM] * (1 + spread),
        [VMEM] * 2,
        "first",
        aliases={5: 1},
        scratch=[dma((1,))],
    )(place, norm_gain, wg, wu, wd, in_vmem(begun), *received)
    experts = (norm_gain, wg, wu, in_vmem(wd))
    parts, own = lax.optimization_barrier((parts, own))
    flag = SMEM((1,), jnp.int32)
    table_of = VMEM((devices * kept, LANES), F32)
    wide = VMEM((devices * kept * tiles, LANES), F32)
    cols_of = VMEM((devices // GROUP * slots, LANES), F32)
    whole = HBM((everyone, feats), BF16)
    sizes = dict(sections=sections, feats=feats, tiles=tiles)
    carry = call(
        functools.partial(table_kernel, **sizes),
        [flag, state, cols_of, compact, table_of, whole],
        [VMEM] * 2,
        [SMEM] + [VMEM] * 4 + [HBM],
        "table",
        scratch=[wide],
    )(own, swap(parts))

    def turn(carry):
        unused, x, cols, packed, table, done = lax.optimization_barrier(carry)
        parts, more, cols, following = call(
            functools.partial(round_kernel, tokens=everyone, slots=slots, **sizes),
            [compact, flag, cols_of, table_of],
            [VMEM] * 6,
            [VMEM, SMEM, VMEM, VMEM],
            "round",
            aliases={5: 2},
            scratch=[wide],
        )(*experts, swap(packed), in_vmem(cols))
        x, packed, table, done = call(
            functools.partial(update_kernel, feats=feats, tiles=tiles),
            [state, compact, table_of, whole],
            [SMEM] + [VMEM] * 4 + [HBM],
            [VMEM] * 3 + [HBM],
            "update",
            aliases={1: 0, 3: 2, 5: 3},
            scratch=[wide, wide, VMEM((everyone, feats), BF16), dma((1,))],
        )(more, x, swap(parts), in_vmem(table), in_vmem(following), in_hbm(done))
        return more, x, cols, packed, table, done

    done = lax.while_loop(lambda c: c[0][0] > 0, turn, tuple(carry))[5]
    return done.reshape(ways, micro, tokens, feats)


def solution(mesh):
    return jax.shard_map(
        on_device,
        mesh=mesh,
        in_specs=(
            P(None, None, "expert", None),
            P("section", None),
            P("section", None, "expert"),
            P("section", None, "expert"),
            P("section", "expert", None),
            P(None, None, "section", "expert", None),
            P(None, None, "section", "expert", None),
        ),
        out_specs=P(None, None, "expert", "section"),
        check_vma=False,
    )
```

```python
import functools

import jax
import jax.numpy as jnp
from jax import lax
from jax.experimental import pallas as pl
from jax.experimental.pallas import tpu as pltpu
from jax.sharding import PartitionSpec as P

GROUP = 2
CAP = 2
EARLY = 2

norm_eps = 1e-06
route_scale = 2.5

F32 = jnp.float32
BF16 = jnp.bfloat16
LANES = 128
AXES = ("section", "expert")

VMEM = pltpu.VMEM
HBM = pltpu.HBM
SMEM = pltpu.SMEM


def iota(shape, dim):
    return lax.broadcasted_iota(jnp.int32, shape, dim)


def start(*copies):
    for copy in copies:
        copy.start()
    return copies


def mm(a, b):
    return jnp.dot(a, b, preferred_element_type=F32)


def route_kernel(place_ref, ids_hbm, scores_hbm, x_hbm, w_hbm, *refs, window, slots, early):
    spread = len(refs) - 6
    outs, w_ref = refs[:spread], refs[spread]
    ids_ref, scores_ref, x_ref, rows_ref, sems = refs[spread + 1:]
    pairs = ((ids_hbm, ids_ref), (scores_hbm, scores_ref), (x_hbm, x_ref))
    copies = start(*[pltpu.make_async_copy(a, b, sems.at[n]) for n, (a, b) in enumerate(pairs)])
    ahead, = start(pltpu.make_async_copy(w_hbm.at[:early], w_ref.at[:early], sems.at[3]))
    groups, topk, tokens = ids_ref.shape
    count, width = x_ref.shape
    block_of = lambda v: jnp.floor((v.astype(F32) + 0.5) * (1.0 / tokens))
    place_i = iota((count, count), 0)
    place_j = iota((count, count), 1)
    earlier = ((place_i < place_j) & (block_of(place_i) == block_of(place_j))).astype(BF16)
    token_lane = iota((slots, count), 1).astype(F32)
    slot_row = iota((slots, count), 0).astype(F32)
    base = block_of(iota((1, count), 1)) * CAP
    meta_lane = iota((slots, LANES), 1)
    copies[0].wait()
    copies[1].wait()
    across = lambda ref: jnp.concatenate([ref[g] for g in range(groups)], axis=1)
    ids = across(ids_ref)
    scores = across(scores_ref)
    weights = route_scale * scores / jnp.sum(scores, axis=0, keepdims=True)
    same = [ids == e for e in range(window)]
    hits = jnp.concatenate([jnp.sum(jnp.where(m, 1.0, 0.0), axis=0, keepdims=True) for m in same], axis=0)
    before = mm(hits.astype(BF16), earlier)
    picks = []
    for e in range(window):
        share = jnp.sum(jnp.where(same[e], weights, 0.0), axis=0, keepdims=True)
        pick = jnp.where(base + before[e:e + 1] == slot_row, hits[e:e + 1], 0.0)
        picks.append(pick.astype(BF16))
        token = jnp.sum(pick * token_lane + pick, axis=-1, keepdims=True) - 1.0
        w = jnp.sum(pick * share, axis=-1, keepdims=True)
        high = w.astype(BF16).astype(F32)
        mid = (w - high).astype(BF16).astype(F32)
        low = w - high - mid
        meta = jnp.where(meta_lane == 0, token, 0.0)
        meta = jnp.where(meta_lane == 1, high, meta)
        meta = jnp.where(meta_lane == 2, mid, meta)
        meta = jnp.where(meta_lane == 3, low, meta)
        rows_ref[e, :, width:] = meta.astype(BF16)
    copies[2].wait()
    x = x_ref[...]
    for e in range(window):
        rows_ref[e, :, :width] = mm(picks[e], x).astype(BF16)
    me = lax.rem(place_ref[0], spread)
    for k in range(spread):
        peer = lax.rem(me + k, spread)
        outs[k][...] = rows_ref[lax.div(peer, GROUP)]
    ahead.wait()


def load_kernel(place_ref, x_hbm, wg_hbm, wu_hbm, own_ref, wg_ref, wu_ref, piece_ref, sems, *, spread, feats):
    section = lax.div(place_ref[0], spread)
    tokens, padded = own_ref.shape
    span = piece_ref.shape[1]
    width = x_hbm.shape[1]
    first = jnp.minimum(lax.div(section * feats, LANES), (width - span) // LANES) * LANES
    piece, *weights = start(
        pltpu.make_async_copy(x_hbm.at[:, pl.ds(pl.multiple_of(first, LANES), span)], piece_ref, sems.at[0]),
        pltpu.make_async_copy(wg_hbm, wg_ref, sems.at[1]),
        pltpu.make_async_copy(wu_hbm, wu_ref, sems.at[2]),
    )
    piece.wait()
    moved = pltpu.roll(piece_ref[...].astype(F32), lax.rem(span - (section * feats - first), span), 1)[:, :padded]
    own_ref[...] = jnp.where(iota((tokens, padded), 1) < feats, moved, 0.0).astype(BF16)
    for weight in weights:
        weight.wait()


def silu_times(gate, up):
    return (gate / (1.0 + jnp.exp(-gate)) * up).astype(BF16)


def first_kernel(place_ref, gain_ref, wg_ref, wu_ref, wd_hbm, begun_ref, *refs, sections, feats, early):
    spread = len(refs) - 3
    ins, out_ref, wd_ref, sems = refs[:spread], refs[spread], refs[spread + 1], refs[spread + 2]
    copy, = start(pltpu.make_async_copy(wd_hbm.at[early:], wd_ref.at[early:], sems.at[0]))
    width = gain_ref.shape[1]
    slots = ins[0].shape[0]
    room = out_ref.shape[2] - feats
    x = jnp.concatenate([r[:, :width].astype(F32) for r in ins], axis=0)
    mean = jnp.mean(x * x, axis=-1, keepdims=True)
    h = (x * lax.rsqrt(mean + norm_eps) * gain_ref[...]).astype(BF16)
    act = silu_times(mm(h, wg_ref[...]), mm(h, wu_ref[...]))
    copy.wait()
    part = mm(act, wd_ref[...]).astype(BF16)
    me = lax.rem(place_ref[0], spread)
    for k in range(spread):
        block = lax.rem(me - k + spread, spread)
        meta = ins[k][:, width:width + room]
        for s in range(sections):
            out_ref[s * spread + block, :, :feats] = part[k * slots:(k + 1) * slots, s * feats:(s + 1) * feats]
            out_ref[s * spread + block, :, feats:] = meta


def all_layers(pieces, gain_ref, wg_ref, wu_ref, wd_ref, beside=None):
    rows, feats = pieces[0].shape
    total = jnp.zeros((rows, 1), F32)
    for piece in pieces:
        total = total + jnp.sum(piece * piece, axis=-1, keepdims=True)
    scale = lax.rsqrt(total * (1.0 / (feats * len(pieces))) + norm_eps)
    gate = jnp.zeros((rows, wg_ref.shape[1]), F32)
    up = jnp.zeros((rows, wg_ref.shape[1]), F32)
    for s, piece in enumerate(pieces):
        here = slice(s * feats, (s + 1) * feats)
        h = (piece * scale * gain_ref[:, here]).astype(BF16)
        gate = gate + mm(h, wg_ref[here, :])
        up = up + mm(h, wu_ref[here, :])
        if beside is not None:
            next(beside, None)
    return mm(silu_times(gate, up), wd_ref[...])


def round_kernel(
    gain_ref, wg_ref, wu_ref, wd_ref, in_ref, cols_ref, tab_ref,
    out_ref, more, cols_out, table_out, terms_out, picks_out, wide_ref, *,
    sections, feats, tiles, tokens, slots
):
    count, sub, lanes = in_ref.shape
    spread = count // sections
    rows = spread * (sub // tiles)
    span = spread * sub
    wide_ref[...] = in_ref[...].astype(F32).reshape(count * sub, lanes)
    at = lambda s, k: pl.ds(s * span + k, rows, stride=tiles)
    spare = feats - (tiles - 1) * lanes
    more[0] = jnp.max(wide_ref[at(0, tiles - 1), :][:, spare:spare + 1]).astype(jnp.int32)
    pieces = []
    for s in range(sections):
        pieces.append(jnp.concatenate([wide_ref[at(s, k), :] for k in range(tiles)], axis=1)[:, :feats])
    chosen = []
    steps = select_steps(chosen, cols_ref[...], tokens, table_out.shape[0] // count, count, sections, slots)
    terms = part_terms(tab_ref[...], tokens)
    part = all_layers(pieces, gain_ref, wg_ref, wu_ref, wd_ref, steps)
    for unused in steps:
        pass
    cols, table = chosen
    terms_out[...] = terms
    picks_out[...] = row_picks(table, tokens)
    cols_out[...] = cols
    table_out[...] = table
    for s in range(sections):
        piece = part[:, s * feats:(s + 1) * feats]
        piece = jnp.concatenate([piece, jnp.zeros((rows, tiles * lanes - feats), F32)], axis=1)
        for k in range(tiles):
            wide_ref[at(s, k), :] = piece[:, k * lanes:(k + 1) * lanes]
    out_ref[...] = wide_ref[...].reshape(count, sub, lanes).astype(BF16)


def part_terms(table, tokens):
    across = table.T[:8]
    chosen = iota((tokens, across.shape[1]), 0).astype(F32) + 1.0 == across[0:1]
    return jnp.concatenate([jnp.where(chosen, across[n:n + 1], 0.0) for n in (1, 2, 3)], axis=0).astype(BF16)


def add_parts(terms, parts, x, feats):
    tokens, padded = x.shape
    added = mm(terms, parts)
    added = added[:tokens] + added[tokens:2 * tokens] + added[2 * tokens:]
    return jnp.where(iota((tokens, padded), 1) < feats, x.astype(F32) + added, 0.0).astype(BF16)


def find_ready(cols, tokens, sections):
    per = cols.shape[0] // sections
    pick = (iota((cols.shape[0], tokens), 1).astype(F32) == cols[:, 0:1]).astype(F32)
    pending = cols[:, 4:5]
    layer = lambda v, l: v[l * per:(l + 1) * per]
    waits = [jnp.minimum(jnp.sum(layer(pick, l) * layer(pending, l), axis=0, keepdims=True), 1.0) for l in range(sections)]
    ahead, behind = [None] * sections, [None] * sections
    run_a = run_b = jnp.zeros((1, tokens), F32)
    for l in range(sections):
        ahead[l] = run_a
        run_a = run_a + waits[l]
        m = sections - 1 - l
        behind[m] = run_b
        run_b = run_b + waits[m]
    forward = iota((1, tokens), 1) < tokens // 2
    ready = []
    for l in range(sections):
        free = jnp.where(jnp.where(forward, ahead[l], behind[l]) == 0.0, waits[l], 0.0)
        ready.append(jnp.sum(layer(pick, l) * free, axis=-1, keepdims=True))
    return jnp.concatenate(ready, axis=0), pick, run_a


def values_of(cols, taken):
    lane = iota(cols.shape, 1)
    return jnp.where(taken & (lane < 4), jnp.where(lane == 0, cols + 1.0, cols), 0.0)


def select_steps(result, cols, tokens, kept, count, sections, slots):
    total = cols.shape[0]
    per = total // sections
    ready, pick, waits = find_ready(cols, tokens, sections)
    yield
    group_of = lambda v, size: jnp.floor((v.astype(F32) + 0.5) * (1.0 / size))
    row = iota((total, 1), 0)
    urgent = jnp.sum(pick * waits, axis=-1, keepdims=True) * slots + (slots - lax.rem(row, slots)).astype(F32)
    apart = 4.0 * slots * sections
    key = jnp.where(ready > 0.0, urgent, 0.0) + group_of(row, slots) * apart
    yield
    ahead = jnp.broadcast_to(key, (total, LANES)).T[0:1] - key
    rank = jnp.sum(jnp.where((ahead > 0.0) & (ahead < 0.5 * apart), 1.0, 0.0), axis=-1, keepdims=True)
    late = jnp.where(rank >= kept, ready, 0.0)
    yield
    held = []
    for l in range(sections):
        here = slice(l * per, (l + 1) * per)
        wait = jnp.sum(pick[here] * late[here], axis=0, keepdims=True)
        held.append(jnp.sum(pick[here] * wait, axis=-1, keepdims=True))
    yield
    taken = jnp.where(jnp.concatenate(held, axis=0) == 0.0, ready, 0.0)
    cols = jnp.where(iota((total, LANES), 1) == 4, cols - taken, cols)
    left = jnp.max(cols[:, 4:5], axis=0, keepdims=True)
    owner = (group_of(iota((count, total), 0), GROUP) == group_of(iota((count, total), 1), slots)).astype(BF16)
    yield
    tables = []
    for c in range(kept):
        mine = values_of(cols, (taken > 0.0) & (rank == c))
        tables.append(mm(owner, mine.astype(BF16)))
    table = jnp.concatenate(tables, axis=0)
    result[:] = cols, jnp.where(iota(table.shape, 1) == 4, left, table)


def select(*args):
    result = []
    for unused in select_steps(result, *args):
        pass
    return result


def row_picks(table, tokens):
    return (iota((table.shape[0], tokens), 1).astype(F32) + 1.0 == table[:, 0:1]).astype(BF16)


def pack_rows(picks, left, x, send_ref, wide_ref, feats, tiles):
    count, sub, lanes = send_ref.shape
    kept = sub // tiles
    rows = jnp.where(iota((kept * count, x.shape[1]), 1) == feats, left, mm(picks, x))
    for c in range(kept):
        for k in range(tiles):
            wide_ref[pl.ds(c * tiles + k, count, stride=sub), :] = rows[c * count:(c + 1) * count, k * lanes:(k + 1) * lanes]
    send_ref[...] = wide_ref[...].reshape(count, sub, lanes).astype(BF16)


def table_kernel(x_ref, in_ref, more, x_out, cols_out, send_out, table_out, done_hbm, wide_ref, *, sections, feats, tiles):
    more[0] = 1
    count, slots, padded = in_ref.shape
    tokens = x_ref.shape[0]
    groups = count // GROUP
    parts = in_ref[...].reshape(count * slots, padded)
    meta = [parts[g * GROUP * slots:(g * GROUP + 1) * slots, feats:feats + 4].astype(F32) for g in range(groups)]
    meta = jnp.concatenate(meta, axis=0)
    lane = iota((groups * slots, LANES), 1)
    cols = jnp.where(lane == 0, meta[:, 0:1], 0.0)
    for n in (1, 2, 3):
        cols = jnp.where(lane == n, meta[:, n:n + 1], cols)
    cols = jnp.where((lane == 4) & (meta[:, 0:1] >= 0.0), 1.0, cols)
    ready, *unused = find_ready(cols, tokens, sections)
    mine = values_of(cols, ready > 0.0)
    table = jnp.concatenate([mine[g * slots:(g + 1) * slots] for g in range(groups) for n in range(GROUP)], axis=0)
    x = add_parts(part_terms(table, tokens), parts, x_ref[...], feats)
    x_out[...] = x
    cols = jnp.where(lane == 4, cols - ready, cols)
    cols, table = select(cols, tokens, table_out.shape[0] // count, count, sections, slots)
    cols_out[...] = cols
    table_out[...] = table
    pack_rows(row_picks(table, tokens), table[:, 4:5], x, send_out, wide_ref, feats, tiles)


def update_kernel(
    more, x_ref, in_ref, terms_ref, picks_ref, next_ref, done_in,
    x_out, send_out, done_hbm, in_wide, out_wide, done_ref, sems, *, feats, tiles
):
    count, sub, lanes = in_ref.shape
    in_wide[...] = in_ref[...].astype(F32).reshape(count * sub, lanes)
    at = lambda c, k: pl.ds(c * tiles + k, count, stride=sub)
    parts = jnp.concatenate(
        [jnp.concatenate([in_wide[at(c, k), :] for k in range(tiles)], axis=1) for c in range(sub // tiles)], axis=0
    ).astype(BF16)
    x = add_parts(terms_ref[...], parts, x_ref[...], feats)
    x_out[...] = x

    @pl.when(more[0] > 0)
    def forward():
        pack_rows(picks_ref[...], next_ref[:, 4:5], x, send_out, out_wide, feats, tiles)

    @pl.when(more[0] <= 0)
    def finish():
        done_ref[...] = x[:, :feats]
        done, = start(pltpu.make_async_copy(done_ref, done_hbm, sems.at[0]))
        done.wait()


def call(kernel, out_shape, in_spaces, out_spaces, name, scratch=(), limit=24 * 2**20, aliases={}):
    spec = lambda space: pl.BlockSpec(memory_space=space)
    single = not isinstance(out_shape, (list, tuple))
    return pl.pallas_call(
        kernel,
        out_shape=out_shape,
        in_specs=[spec(s) for s in in_spaces],
        out_specs=spec(out_spaces[0]) if single else [spec(s) for s in out_spaces],
        scratch_shapes=list(scratch),
        input_output_aliases=aliases,
        compiler_params=pltpu.CompilerParams(vmem_limit_bytes=limit),
        name=name,
    )


def on_device(entering, norm_gain, w_gate, w_up, w_down, route_ids, route_scores):
    sections = lax.axis_size("section")
    spread = lax.axis_size("expert")
    window = spread // GROUP
    ways, micro, tokens, width = entering.shape
    everyone = ways * micro * tokens
    slots = ways * micro * CAP
    feats = width // sections
    tiles = feats // LANES + 1
    padded = tiles * LANES
    devices = sections * spread
    kept = max(1, 8 // tiles)
    by_token = lambda v: jnp.swapaxes(v[:, :, 0], 2, 3).reshape(ways * micro, v.shape[-1], tokens)
    in_hbm = lambda v: pltpu.with_memory_space_constraint(v, HBM)
    in_vmem = lambda v: pltpu.with_memory_space_constraint(v, VMEM)
    sds = jax.ShapeDtypeStruct
    dma = pltpu.SemaphoreType.DMA

    place = lax.axis_index(AXES).astype(jnp.int32).reshape(1)
    flat = in_hbm(entering.reshape(everyone, width))
    ids, scores = in_hbm(by_token(route_ids)), in_hbm(by_token(route_scores))
    wg, wu, wd = [in_hbm(v[0]) for v in (w_gate, w_up, w_down)]
    resident = lambda v: VMEM(v.shape, v.dtype)

    early = wd.shape[0] // EARLY
    *rows, begun = call(
        functools.partial(route_kernel, window=window, slots=slots, early=early),
        [sds((slots, width + LANES), BF16)] * spread + [resident(wd)],
        [SMEM] + [HBM] * 4,
        [VMEM] * (spread + 1),
        "route",
        scratch=[
            VMEM(ids.shape, ids.dtype),
            VMEM(scores.shape, scores.dtype),
            VMEM((everyone, width), BF16),
            VMEM((window, slots, width + LANES), BF16),
            dma((4,)),
        ],
    )(place, ids, scores, flat, wd)
    received = [rows[0]] + [
        lax.ppermute(rows[k], "expert", [(y, (y + k) % spread) for y in range(spread)]) for k in range(1, spread)
    ]
    reach = max(s * feats % LANES for s in range(sections)) + feats
    span = -(-reach // LANES) * LANES
    state = sds((everyone, padded), BF16)
    own, wg, wu = call(
        functools.partial(load_kernel, spread=spread, feats=feats),
        [state, resident(wg), resident(wu)],
        [SMEM] + [HBM] * 3,
        [VMEM] * 3,
        "load",
        scratch=[VMEM((everyone, span), BF16), dma((3,))],
    )(place, flat, wg, wu)
    wg, wu = in_vmem(wg), in_vmem(wu)
    message = sds((devices, slots, padded), BF16)
    compact = sds((devices, kept * tiles, LANES), BF16)
    swap = lambda v: lax.all_to_all(v, AXES, split_axis=0, concat_axis=0, tiled=True)
    parts, wd = call(
        functools.partial(first_kernel, sections=sections, feats=feats, early=early),
        [message, resident(wd)],
        [SMEM] + [VMEM] * 3 + [HBM] + [VMEM] * (1 + spread),
        [VMEM] * 2,
        "first",
        aliases={5: 1},
        scratch=[dma((1,))],
    )(place, norm_gain, wg, wu, wd, in_vmem(begun), *received)
    experts = (norm_gain, wg, wu, in_vmem(wd))
    parts, own = lax.optimization_barrier((parts, own))
    flag = SMEM((1,), jnp.int32)
    table_of = VMEM((devices * kept, LANES), F32)
    wide = VMEM((devices * kept * tiles, LANES), F32)
    cols_of = VMEM((devices // GROUP * slots, LANES), F32)
    whole = HBM((everyone, feats), BF16)
    sizes = dict(sections=sections, feats=feats, tiles=tiles)
    carry = call(
        functools.partial(table_kernel, **sizes),
        [flag, state, cols_of, compact, table_of, whole],
        [VMEM] * 2,
        [SMEM] + [VMEM] * 4 + [HBM],
        "table",
        scratch=[wide],
    )(own, swap(parts))

    def turn(carry):
        unused, x, cols, packed, table, done = lax.optimization_barrier(carry)
        parts, more, cols, table, terms, picks = call(
            functools.partial(round_kernel, tokens=everyone, slots=slots, **sizes),
            [compact, flag, cols_of, table_of, VMEM((3 * everyone, devices * kept), BF16), VMEM((devices * kept, everyone), BF16)],
            [VMEM] * 7,
            [VMEM, SMEM] + [VMEM] * 4,
            "round",
            aliases={5: 2, 6: 3},
            scratch=[wide],
        )(*experts, swap(packed), in_vmem(cols), in_vmem(table))
        x, packed, done = call(
            functools.partial(update_kernel, feats=feats, tiles=tiles),
            [state, compact, whole],
            [SMEM] + [VMEM] * 5 + [HBM],
            [VMEM] * 2 + [HBM],
            "update",
            aliases={1: 0, 6: 2},
            scratch=[wide, wide, VMEM((everyone, feats), BF16), dma((1,))],
        )(more, x, swap(parts), in_vmem(terms), in_vmem(picks), in_vmem(table), in_hbm(done))
        return more, x, cols, packed, table, done

    done = lax.while_loop(lambda c: c[0][0] > 0, turn, tuple(carry))[5]
    return done.reshape(ways, micro, tokens, feats)


def solution(mesh):
    return jax.shard_map(
        on_device,
        mesh=mesh,
        in_specs=(
            P(None, None, "expert", None),
            P("section", None),
            P("section", None, "expert"),
            P("section", None, "expert"),
            P("section", "expert", None),
            P(None, None, "section", "expert", None),
            P(None, None, "section", "expert", None),
        ),
        out_specs=P(None, None, "expert", "section"),
        check_vma=False,
    )
```

```python
import functools

import jax
import jax.numpy as jnp
from jax import lax
from jax.experimental import pallas as pl
from jax.experimental.pallas import tpu as pltpu
from jax.sharding import PartitionSpec as P

GROUP = 2
CAP = 2
EARLY = 2

norm_eps = 1e-06
route_scale = 2.5

F32 = jnp.float32
BF16 = jnp.bfloat16
LANES = 128
PLACES = ("section", "expert")
AXES = ("expert", "section")

VMEM = pltpu.VMEM
HBM = pltpu.HBM
SMEM = pltpu.SMEM


def iota(shape, dim):
    return lax.broadcasted_iota(jnp.int32, shape, dim)


def start(*copies):
    for copy in copies:
        copy.start()
    return copies


def mm(a, b):
    return jnp.dot(a, b, preferred_element_type=F32)


def route_kernel(place_ref, ids_hbm, scores_hbm, x_hbm, w_hbm, *refs, window, slots, early):
    spread = len(refs) - 6
    outs, w_ref = refs[:spread], refs[spread]
    ids_ref, scores_ref, x_ref, rows_ref, sems = refs[spread + 1:]
    pairs = ((ids_hbm, ids_ref), (scores_hbm, scores_ref), (x_hbm, x_ref))
    copies = start(*[pltpu.make_async_copy(a, b, sems.at[n]) for n, (a, b) in enumerate(pairs)])
    ahead, = start(pltpu.make_async_copy(w_hbm.at[:early], w_ref.at[:early], sems.at[3]))
    groups, topk, tokens = ids_ref.shape
    count, width = x_ref.shape
    block_of = lambda v: jnp.floor((v.astype(F32) + 0.5) * (1.0 / tokens))
    place_i = iota((count, count), 0)
    place_j = iota((count, count), 1)
    earlier = ((place_i < place_j) & (block_of(place_i) == block_of(place_j))).astype(BF16)
    token_lane = iota((slots, count), 1).astype(F32)
    slot_row = iota((slots, count), 0).astype(F32)
    base = block_of(iota((1, count), 1)) * CAP
    meta_lane = iota((slots, LANES), 1)
    copies[0].wait()
    copies[1].wait()
    across = lambda ref: jnp.concatenate([ref[g] for g in range(groups)], axis=1)
    ids = across(ids_ref)
    scores = across(scores_ref)
    weights = route_scale * scores / jnp.sum(scores, axis=0, keepdims=True)
    same = [ids == e for e in range(window)]
    hits = jnp.concatenate([jnp.sum(jnp.where(m, 1.0, 0.0), axis=0, keepdims=True) for m in same], axis=0)
    before = mm(hits.astype(BF16), earlier)
    picks = []
    for e in range(window):
        share = jnp.sum(jnp.where(same[e], weights, 0.0), axis=0, keepdims=True)
        pick = jnp.where(base + before[e:e + 1] == slot_row, hits[e:e + 1], 0.0)
        picks.append(pick.astype(BF16))
        token = jnp.sum(pick * token_lane + pick, axis=-1, keepdims=True) - 1.0
        w = jnp.sum(pick * share, axis=-1, keepdims=True)
        high = w.astype(BF16).astype(F32)
        mid = (w - high).astype(BF16).astype(F32)
        low = w - high - mid
        meta = jnp.where(meta_lane == 0, token, 0.0)
        meta = jnp.where(meta_lane == 1, high, meta)
        meta = jnp.where(meta_lane == 2, mid, meta)
        meta = jnp.where(meta_lane == 3, low, meta)
        rows_ref[e, :, width:] = meta.astype(BF16)
    copies[2].wait()
    x = x_ref[...]
    for e in range(window):
        rows_ref[e, :, :width] = mm(picks[e], x).astype(BF16)
    me = lax.rem(place_ref[0], spread)
    for k in range(spread):
        peer = lax.rem(me + k, spread)
        outs[k][...] = rows_ref[lax.div(peer, GROUP)]
    ahead.wait()


def load_kernel(place_ref, x_hbm, wg_hbm, wu_hbm, own_ref, wg_ref, wu_ref, piece_ref, sems, *, spread, feats):
    section = lax.div(place_ref[0], spread)
    tokens, padded = own_ref.shape
    span = piece_ref.shape[1]
    width = x_hbm.shape[1]
    first = jnp.minimum(lax.div(section * feats, LANES), (width - span) // LANES) * LANES
    piece, *weights = start(
        pltpu.make_async_copy(x_hbm.at[:, pl.ds(pl.multiple_of(first, LANES), span)], piece_ref, sems.at[0]),
        pltpu.make_async_copy(wg_hbm, wg_ref, sems.at[1]),
        pltpu.make_async_copy(wu_hbm, wu_ref, sems.at[2]),
    )
    piece.wait()
    moved = pltpu.roll(piece_ref[...].astype(F32), lax.rem(span - (section * feats - first), span), 1)[:, :padded]
    own_ref[...] = jnp.where(iota((tokens, padded), 1) < feats, moved, 0.0).astype(BF16)
    for weight in weights:
        weight.wait()


def silu_times(gate, up):
    return (gate / (1.0 + jnp.exp(-gate)) * up).astype(BF16)


def first_kernel(place_ref, gain_ref, wg_ref, wu_ref, wd_hbm, begun_ref, *refs, sections, feats, early):
    spread = len(refs) - 3
    ins, out_ref, wd_ref, sems = refs[:spread], refs[spread], refs[spread + 1], refs[spread + 2]
    copy, = start(pltpu.make_async_copy(wd_hbm.at[early:], wd_ref.at[early:], sems.at[0]))
    width = gain_ref.shape[1]
    slots = ins[0].shape[0]
    room = out_ref.shape[2] - feats
    x = jnp.concatenate([r[:, :width].astype(F32) for r in ins], axis=0)
    mean = jnp.mean(x * x, axis=-1, keepdims=True)
    h = (x * lax.rsqrt(mean + norm_eps) * gain_ref[...]).astype(BF16)
    act = silu_times(mm(h, wg_ref[...]), mm(h, wu_ref[...]))
    copy.wait()
    part = mm(act, wd_ref[...]).astype(BF16)
    me = lax.rem(place_ref[0], spread)
    for k in range(spread):
        block = lax.rem(me - k + spread, spread)
        meta = ins[k][:, width:width + room]
        for s in range(sections):
            out_ref[block * sections + s, :, :feats] = part[k * slots:(k + 1) * slots, s * feats:(s + 1) * feats]
            out_ref[block * sections + s, :, feats:] = meta


def all_layers(pieces, gain_ref, wg_ref, wu_ref, wd_ref, beside=None):
    rows, feats = pieces[0].shape
    total = jnp.zeros((rows, 1), F32)
    for piece in pieces:
        total = total + jnp.sum(piece * piece, axis=-1, keepdims=True)
    scale = lax.rsqrt(total * (1.0 / (feats * len(pieces))) + norm_eps)
    gate = jnp.zeros((rows, wg_ref.shape[1]), F32)
    up = jnp.zeros((rows, wg_ref.shape[1]), F32)
    for s, piece in enumerate(pieces):
        here = slice(s * feats, (s + 1) * feats)
        h = (piece * scale * gain_ref[:, here]).astype(BF16)
        gate = gate + mm(h, wg_ref[here, :])
        up = up + mm(h, wu_ref[here, :])
        if beside is not None:
            next(beside, None)
    return mm(silu_times(gate, up), wd_ref[...])


def round_kernel(
    gain_ref, wg_ref, wu_ref, wd_ref, in_ref, cols_ref, tab_ref,
    out_ref, more, cols_out, table_out, terms_out, picks_out, wide_ref, *,
    sections, feats, tiles, tokens, slots
):
    count, sub, lanes = in_ref.shape
    spread = count // sections
    rows = spread * (sub // tiles)
    span = spread * sub
    spots = [(y * sections + s, pl.ds((s * spread + y) * sub, sub)) for s in range(sections) for y in range(spread)]
    for n, spot in spots:
        wide_ref[spot, :] = in_ref[n].astype(F32)
    at = lambda s, k: pl.ds(s * span + k, rows, stride=tiles)
    spare = feats - (tiles - 1) * lanes
    more[0] = jnp.max(wide_ref[at(0, tiles - 1), :][:, spare:spare + 1]).astype(jnp.int32)
    pieces = []
    for s in range(sections):
        pieces.append(jnp.concatenate([wide_ref[at(s, k), :] for k in range(tiles)], axis=1)[:, :feats])
    chosen = []
    steps = select_steps(chosen, cols_ref[...], tokens, table_out.shape[0] // count, count, sections, slots)
    terms = part_terms(tab_ref[...], tokens)
    part = all_layers(pieces, gain_ref, wg_ref, wu_ref, wd_ref, steps)
    for unused in steps:
        pass
    cols, table = chosen
    terms_out[...] = terms
    picks_out[...] = row_picks(table, tokens)
    cols_out[...] = cols
    table_out[...] = table
    for s in range(sections):
        piece = part[:, s * feats:(s + 1) * feats]
        piece = jnp.concatenate([piece, jnp.zeros((rows, tiles * lanes - feats), F32)], axis=1)
        for k in range(tiles):
            wide_ref[at(s, k), :] = piece[:, k * lanes:(k + 1) * lanes]
    for n, spot in spots:
        out_ref[n] = wide_ref[spot, :].astype(BF16)


def part_terms(table, tokens):
    across = table.T[:8]
    chosen = iota((tokens, across.shape[1]), 0).astype(F32) + 1.0 == across[0:1]
    return jnp.concatenate([jnp.where(chosen, across[n:n + 1], 0.0) for n in (1, 2, 3)], axis=0).astype(BF16)


def add_parts(terms, parts, x, feats):
    tokens, padded = x.shape
    added = mm(terms, parts)
    added = added[:tokens] + added[tokens:2 * tokens] + added[2 * tokens:]
    return jnp.where(iota((tokens, padded), 1) < feats, x.astype(F32) + added, 0.0).astype(BF16)


def find_ready(cols, tokens, sections):
    per = cols.shape[0] // sections
    pick = (iota((cols.shape[0], tokens), 1).astype(F32) == cols[:, 0:1]).astype(F32)
    pending = cols[:, 4:5]
    layer = lambda v, l: v[l * per:(l + 1) * per]
    waits = [jnp.minimum(jnp.sum(layer(pick, l) * layer(pending, l), axis=0, keepdims=True), 1.0) for l in range(sections)]
    ahead, behind = [None] * sections, [None] * sections
    run_a = run_b = jnp.zeros((1, tokens), F32)
    for l in range(sections):
        ahead[l] = run_a
        run_a = run_a + waits[l]
        m = sections - 1 - l
        behind[m] = run_b
        run_b = run_b + waits[m]
    forward = iota((1, tokens), 1) < tokens // 2
    ready = []
    for l in range(sections):
        free = jnp.where(jnp.where(forward, ahead[l], behind[l]) == 0.0, waits[l], 0.0)
        ready.append(jnp.sum(layer(pick, l) * free, axis=-1, keepdims=True))
    return jnp.concatenate(ready, axis=0), pick, run_a


def values_of(cols, taken):
    lane = iota(cols.shape, 1)
    return jnp.where(taken & (lane < 4), jnp.where(lane == 0, cols + 1.0, cols), 0.0)


def select_steps(result, cols, tokens, kept, count, sections, slots):
    total = cols.shape[0]
    per = total // sections
    ready, pick, waits = find_ready(cols, tokens, sections)
    yield
    group_of = lambda v, size: jnp.floor((v.astype(F32) + 0.5) * (1.0 / size))
    row = iota((total, 1), 0)
    urgent = jnp.sum(pick * waits, axis=-1, keepdims=True) * slots + (slots - lax.rem(row, slots)).astype(F32)
    apart = 4.0 * slots * sections
    key = jnp.where(ready > 0.0, urgent, 0.0) + group_of(row, slots) * apart
    yield
    ahead = jnp.broadcast_to(key, (total, LANES)).T[0:1] - key
    rank = jnp.sum(jnp.where((ahead > 0.0) & (ahead < 0.5 * apart), 1.0, 0.0), axis=-1, keepdims=True)
    late = jnp.where(rank >= kept, ready, 0.0)
    yield
    held = []
    for l in range(sections):
        here = slice(l * per, (l + 1) * per)
        wait = jnp.sum(pick[here] * late[here], axis=0, keepdims=True)
        held.append(jnp.sum(pick[here] * wait, axis=-1, keepdims=True))
    yield
    taken = jnp.where(jnp.concatenate(held, axis=0) == 0.0, ready, 0.0)
    cols = jnp.where(iota((total, LANES), 1) == 4, cols - taken, cols)
    left = jnp.max(cols[:, 4:5], axis=0, keepdims=True)
    device = iota((count, total), 0)
    expert = group_of(device, GROUP * sections)
    layer = device.astype(F32) - sections * group_of(device, sections)
    window = count // (GROUP * sections)
    owner = (layer * window + expert == group_of(iota((count, total), 1), slots)).astype(BF16)
    yield
    tables = []
    for c in range(kept):
        mine = values_of(cols, (taken > 0.0) & (rank == c))
        tables.append(mm(owner, mine.astype(BF16)))
    table = jnp.concatenate(tables, axis=0)
    result[:] = cols, jnp.where(iota(table.shape, 1) == 4, left, table)


def select(*args):
    result = []
    for unused in select_steps(result, *args):
        pass
    return result


def row_picks(table, tokens):
    return (iota((table.shape[0], tokens), 1).astype(F32) + 1.0 == table[:, 0:1]).astype(BF16)


def pack_rows(picks, left, x, send_ref, wide_ref, feats, tiles):
    count, sub, lanes = send_ref.shape
    kept = sub // tiles
    rows = jnp.where(iota((kept * count, x.shape[1]), 1) == feats, left, mm(picks, x))
    for c in range(kept):
        for k in range(tiles):
            wide_ref[pl.ds(c * tiles + k, count, stride=sub), :] = rows[c * count:(c + 1) * count, k * lanes:(k + 1) * lanes]
    send_ref[...] = wide_ref[...].reshape(count, sub, lanes).astype(BF16)


def table_kernel(x_ref, in_ref, more, x_out, cols_out, send_out, table_out, done_hbm, wide_ref, *, sections, feats, tiles):
    more[0] = 1
    count, slots, padded = in_ref.shape
    tokens = x_ref.shape[0]
    groups = count // GROUP
    window = groups // sections
    parts = in_ref[...].reshape(count * slots, padded)
    firsts = [(e * GROUP * sections + l) * slots for l in range(sections) for e in range(window)]
    meta = [parts[n:n + slots, feats:feats + 4].astype(F32) for n in firsts]
    meta = jnp.concatenate(meta, axis=0)
    lane = iota((groups * slots, LANES), 1)
    cols = jnp.where(lane == 0, meta[:, 0:1], 0.0)
    for n in (1, 2, 3):
        cols = jnp.where(lane == n, meta[:, n:n + 1], cols)
    cols = jnp.where((lane == 4) & (meta[:, 0:1] >= 0.0), 1.0, cols)
    ready, *unused = find_ready(cols, tokens, sections)
    mine = values_of(cols, ready > 0.0)
    order = [l * window + e for e in range(window) for n in range(GROUP) for l in range(sections)]
    table = jnp.concatenate([mine[g * slots:(g + 1) * slots] for g in order], axis=0)
    x = add_parts(part_terms(table, tokens), parts, x_ref[...], feats)
    x_out[...] = x
    cols = jnp.where(lane == 4, cols - ready, cols)
    cols, table = select(cols, tokens, table_out.shape[0] // count, count, sections, slots)
    cols_out[...] = cols
    table_out[...] = table
    pack_rows(row_picks(table, tokens), table[:, 4:5], x, send_out, wide_ref, feats, tiles)


def update_kernel(
    more, x_ref, in_ref, terms_ref, picks_ref, next_ref, done_in,
    x_out, send_out, done_hbm, in_wide, out_wide, done_ref, sems, *, feats, tiles
):
    count, sub, lanes = in_ref.shape
    in_wide[...] = in_ref[...].astype(F32).reshape(count * sub, lanes)
    at = lambda c, k: pl.ds(c * tiles + k, count, stride=sub)
    parts = jnp.concatenate(
        [jnp.concatenate([in_wide[at(c, k), :] for k in range(tiles)], axis=1) for c in range(sub // tiles)], axis=0
    ).astype(BF16)
    x = add_parts(terms_ref[...], parts, x_ref[...], feats)
    x_out[...] = x

    @pl.when(more[0] > 0)
    def forward():
        pack_rows(picks_ref[...], next_ref[:, 4:5], x, send_out, out_wide, feats, tiles)

    @pl.when(more[0] <= 0)
    def finish():
        done_ref[...] = x[:, :feats]
        done, = start(pltpu.make_async_copy(done_ref, done_hbm, sems.at[0]))
        done.wait()


def call(kernel, out_shape, in_spaces, out_spaces, name, scratch=(), limit=24 * 2**20, aliases={}):
    spec = lambda space: pl.BlockSpec(memory_space=space)
    single = not isinstance(out_shape, (list, tuple))
    return pl.pallas_call(
        kernel,
        out_shape=out_shape,
        in_specs=[spec(s) for s in in_spaces],
        out_specs=spec(out_spaces[0]) if single else [spec(s) for s in out_spaces],
        scratch_shapes=list(scratch),
        input_output_aliases=aliases,
        compiler_params=pltpu.CompilerParams(vmem_limit_bytes=limit),
        name=name,
    )


def on_device(entering, norm_gain, w_gate, w_up, w_down, route_ids, route_scores):
    sections = lax.axis_size("section")
    spread = lax.axis_size("expert")
    window = spread // GROUP
    ways, micro, tokens, width = entering.shape
    everyone = ways * micro * tokens
    slots = ways * micro * CAP
    feats = width // sections
    tiles = feats // LANES + 1
    padded = tiles * LANES
    devices = sections * spread
    kept = max(1, 8 // tiles)
    by_token = lambda v: jnp.swapaxes(v[:, :, 0], 2, 3).reshape(ways * micro, v.shape[-1], tokens)
    in_hbm = lambda v: pltpu.with_memory_space_constraint(v, HBM)
    in_vmem = lambda v: pltpu.with_memory_space_constraint(v, VMEM)
    sds = jax.ShapeDtypeStruct
    dma = pltpu.SemaphoreType.DMA

    place = lax.axis_index(PLACES).astype(jnp.int32).reshape(1)
    flat = in_hbm(entering.reshape(everyone, width))
    ids, scores = in_hbm(by_token(route_ids)), in_hbm(by_token(route_scores))
    wg, wu, wd = [in_hbm(v[0]) for v in (w_gate, w_up, w_down)]
    resident = lambda v: VMEM(v.shape, v.dtype)

    early = wd.shape[0] // EARLY
    *rows, begun = call(
        functools.partial(route_kernel, window=window, slots=slots, early=early),
        [sds((slots, width + LANES), BF16)] * spread + [resident(wd)],
        [SMEM] + [HBM] * 4,
        [VMEM] * (spread + 1),
        "route",
        scratch=[
            VMEM(ids.shape, ids.dtype),
            VMEM(scores.shape, scores.dtype),
            VMEM((everyone, width), BF16),
            VMEM((window, slots, width + LANES), BF16),
            dma((4,)),
        ],
    )(place, ids, scores, flat, wd)
    received = [rows[0]] + [
        lax.ppermute(rows[k], "expert", [(y, (y + k) % spread) for y in range(spread)]) for k in range(1, spread)
    ]
    reach = max(s * feats % LANES for s in range(sections)) + feats
    span = -(-reach // LANES) * LANES
    state = sds((everyone, padded), BF16)
    own, wg, wu = call(
        functools.partial(load_kernel, spread=spread, feats=feats),
        [state, resident(wg), resident(wu)],
        [SMEM] + [HBM] * 3,
        [VMEM] * 3,
        "load",
        scratch=[VMEM((everyone, span), BF16), dma((3,))],
    )(place, flat, wg, wu)
    wg, wu = in_vmem(wg), in_vmem(wu)
    message = sds((devices, slots, padded), BF16)
    compact = sds((devices, kept * tiles, LANES), BF16)
    swap = lambda v: lax.all_to_all(v, AXES, split_axis=0, concat_axis=0, tiled=True)
    parts, wd = call(
        functools.partial(first_kernel, sections=sections, feats=feats, early=early),
        [message, resident(wd)],
        [SMEM] + [VMEM] * 3 + [HBM] + [VMEM] * (1 + spread),
        [VMEM] * 2,
        "first",
        aliases={5: 1},
        scratch=[dma((1,))],
    )(place, norm_gain, wg, wu, wd, in_vmem(begun), *received)
    experts = (norm_gain, wg, wu, in_vmem(wd))
    parts, own = lax.optimization_barrier((parts, own))
    flag = SMEM((1,), jnp.int32)
    table_of = VMEM((devices * kept, LANES), F32)
    wide = VMEM((devices * kept * tiles, LANES), F32)
    cols_of = VMEM((devices // GROUP * slots, LANES), F32)
    whole = HBM((everyone, feats), BF16)
    sizes = dict(sections=sections, feats=feats, tiles=tiles)
    carry = call(
        functools.partial(table_kernel, **sizes),
        [flag, state, cols_of, compact, table_of, whole],
        [VMEM] * 2,
        [SMEM] + [VMEM] * 4 + [HBM],
        "table",
        scratch=[wide],
    )(own, swap(parts))

    def turn(carry):
        unused, x, cols, packed, table, done = lax.optimization_barrier(carry)
        parts, more, cols, table, terms, picks = call(
            functools.partial(round_kernel, tokens=everyone, slots=slots, **sizes),
            [compact, flag, cols_of, table_of, VMEM((3 * everyone, devices * kept), BF16), VMEM((devices * kept, everyone), BF16)],
            [VMEM] * 7,
            [VMEM, SMEM] + [VMEM] * 4,
            "round",
            aliases={5: 2, 6: 3},
            scratch=[wide],
        )(*experts, swap(packed), in_vmem(cols), in_vmem(table))
        x, packed, done = call(
            functools.partial(update_kernel, feats=feats, tiles=tiles),
            [state, compact, whole],
            [SMEM] + [VMEM] * 5 + [HBM],
            [VMEM] * 2 + [HBM],
            "update",
            aliases={1: 0, 6: 2},
            scratch=[wide, wide, VMEM((everyone, feats), BF16), dma((1,))],
        )(more, x, swap(parts), in_vmem(terms), in_vmem(picks), in_vmem(table), in_hbm(done))
        return more, x, cols, packed, table, done

    done = lax.while_loop(lambda c: c[0][0] > 0, turn, tuple(carry))[5]
    return done.reshape(ways, micro, tokens, feats)


def solution(mesh):
    return jax.shard_map(
        on_device,
        mesh=mesh,
        in_specs=(
            P(None, None, "expert", None),
            P("section", None),
            P("section", None, "expert"),
            P("section", None, "expert"),
            P("section", "expert", None),
            P(None, None, "section", "expert", None),
            P(None, None, "section", "expert", None),
        ),
        out_specs=P(None, None, "expert", "section"),
        check_vma=False,
    )
```

```python
import functools

import jax
import jax.numpy as jnp
from jax import lax
from jax.experimental import pallas as pl
from jax.experimental.pallas import tpu as pltpu
from jax.sharding import PartitionSpec as P

GROUP = 2
CAP = 2
EARLY = 2

norm_eps = 1e-06
route_scale = 2.5

F32 = jnp.float32
BF16 = jnp.bfloat16
LANES = 128
PLACES = ("section", "expert")
AXES = ("expert", "section")

VMEM = pltpu.VMEM
HBM = pltpu.HBM
SMEM = pltpu.SMEM


def iota(shape, dim):
    return lax.broadcasted_iota(jnp.int32, shape, dim)


def start(*copies):
    for copy in copies:
        copy.start()
    return copies


def mm(a, b):
    return jnp.dot(a, b, preferred_element_type=F32)


def route_kernel(place_ref, ids_hbm, scores_hbm, x_hbm, w_hbm, *refs, window, slots, early):
    spread = len(refs) - 6
    outs, w_ref = refs[:spread], refs[spread]
    ids_ref, scores_ref, x_ref, rows_ref, sems = refs[spread + 1:]
    pairs = ((ids_hbm, ids_ref), (scores_hbm, scores_ref), (x_hbm, x_ref))
    copies = start(*[pltpu.make_async_copy(a, b, sems.at[n]) for n, (a, b) in enumerate(pairs)])
    ahead, = start(pltpu.make_async_copy(w_hbm.at[:early], w_ref.at[:early], sems.at[3]))
    groups, topk, tokens = ids_ref.shape
    count, width = x_ref.shape
    block_of = lambda v: jnp.floor((v.astype(F32) + 0.5) * (1.0 / tokens))
    place_i = iota((count, count), 0)
    place_j = iota((count, count), 1)
    earlier = ((place_i < place_j) & (block_of(place_i) == block_of(place_j))).astype(BF16)
    token_lane = iota((slots, count), 1).astype(F32)
    slot_row = iota((slots, count), 0).astype(F32)
    base = block_of(iota((1, count), 1)) * CAP
    meta_lane = iota((slots, LANES), 1)
    copies[0].wait()
    copies[1].wait()
    across = lambda ref: jnp.concatenate([ref[g] for g in range(groups)], axis=1)
    ids = across(ids_ref)
    scores = across(scores_ref)
    weights = route_scale * scores / jnp.sum(scores, axis=0, keepdims=True)
    same = [ids == e for e in range(window)]
    hits = jnp.concatenate([jnp.sum(jnp.where(m, 1.0, 0.0), axis=0, keepdims=True) for m in same], axis=0)
    before = mm(hits.astype(BF16), earlier)
    picks = []
    for e in range(window):
        share = jnp.sum(jnp.where(same[e], weights, 0.0), axis=0, keepdims=True)
        pick = jnp.where(base + before[e:e + 1] == slot_row, hits[e:e + 1], 0.0)
        picks.append(pick.astype(BF16))
        token = jnp.sum(pick * token_lane + pick, axis=-1, keepdims=True) - 1.0
        w = jnp.sum(pick * share, axis=-1, keepdims=True)
        high = w.astype(BF16).astype(F32)
        mid = (w - high).astype(BF16).astype(F32)
        low = w - high - mid
        meta = jnp.where(meta_lane == 0, token, 0.0)
        meta = jnp.where(meta_lane == 1, high, meta)
        meta = jnp.where(meta_lane == 2, mid, meta)
        meta = jnp.where(meta_lane == 3, low, meta)
        rows_ref[e, :, width:] = meta.astype(BF16)
    copies[2].wait()
    x = x_ref[...]
    for e in range(window):
        rows_ref[e, :, :width] = mm(picks[e], x).astype(BF16)
    me = lax.rem(place_ref[0], spread)
    for k in range(spread):
        peer = lax.bitwise_xor(me, k)
        outs[k][...] = rows_ref[lax.div(peer, GROUP)]
    ahead.wait()


def load_kernel(place_ref, x_hbm, wg_hbm, wu_hbm, own_ref, wg_ref, wu_ref, piece_ref, sems, *, spread, feats):
    section = lax.div(place_ref[0], spread)
    tokens, padded = own_ref.shape
    span = piece_ref.shape[1]
    width = x_hbm.shape[1]
    first = jnp.minimum(lax.div(section * feats, LANES), (width - span) // LANES) * LANES
    piece, *weights = start(
        pltpu.make_async_copy(x_hbm.at[:, pl.ds(pl.multiple_of(first, LANES), span)], piece_ref, sems.at[0]),
        pltpu.make_async_copy(wg_hbm, wg_ref, sems.at[1]),
        pltpu.make_async_copy(wu_hbm, wu_ref, sems.at[2]),
    )
    piece.wait()
    moved = pltpu.roll(piece_ref[...].astype(F32), lax.rem(span - (section * feats - first), span), 1)[:, :padded]
    own_ref[...] = jnp.where(iota((tokens, padded), 1) < feats, moved, 0.0).astype(BF16)
    for weight in weights:
        weight.wait()


def silu_times(gate, up):
    return (gate / (1.0 + jnp.exp(-gate)) * up).astype(BF16)


def first_kernel(place_ref, gain_ref, wg_ref, wu_ref, wd_hbm, begun_ref, *refs, sections, feats, early):
    spread = len(refs) - 3
    ins, out_ref, wd_ref, sems = refs[:spread], refs[spread], refs[spread + 1], refs[spread + 2]
    copy, = start(pltpu.make_async_copy(wd_hbm.at[early:], wd_ref.at[early:], sems.at[0]))
    width = gain_ref.shape[1]
    slots = ins[0].shape[0]
    room = out_ref.shape[2] - feats
    x = jnp.concatenate([r[:, :width].astype(F32) for r in ins], axis=0)
    mean = jnp.mean(x * x, axis=-1, keepdims=True)
    h = (x * lax.rsqrt(mean + norm_eps) * gain_ref[...]).astype(BF16)
    act = silu_times(mm(h, wg_ref[...]), mm(h, wu_ref[...]))
    copy.wait()
    part = mm(act, wd_ref[...]).astype(BF16)
    me = lax.rem(place_ref[0], spread)
    for k in range(spread):
        block = lax.bitwise_xor(me, k)
        meta = ins[k][:, width:width + room]
        for s in range(sections):
            out_ref[block * sections + s, :, :feats] = part[k * slots:(k + 1) * slots, s * feats:(s + 1) * feats]
            out_ref[block * sections + s, :, feats:] = meta


def all_layers(pieces, gain_ref, wg_ref, wu_ref, wd_ref, beside=None):
    rows, feats = pieces[0].shape
    total = jnp.zeros((rows, 1), F32)
    for piece in pieces:
        total = total + jnp.sum(piece * piece, axis=-1, keepdims=True)
    scale = lax.rsqrt(total * (1.0 / (feats * len(pieces))) + norm_eps)
    gate = jnp.zeros((rows, wg_ref.shape[1]), F32)
    up = jnp.zeros((rows, wg_ref.shape[1]), F32)
    for s, piece in enumerate(pieces):
        here = slice(s * feats, (s + 1) * feats)
        h = (piece * scale * gain_ref[:, here]).astype(BF16)
        gate = gate + mm(h, wg_ref[here, :])
        up = up + mm(h, wu_ref[here, :])
        if beside is not None:
            next(beside, None)
    return mm(silu_times(gate, up), wd_ref[...])


def round_kernel(
    gain_ref, wg_ref, wu_ref, wd_ref, in_ref, cols_ref, tab_ref,
    out_ref, more, cols_out, table_out, terms_out, picks_out, wide_ref, *,
    sections, feats, tiles, tokens, slots
):
    count, sub, lanes = in_ref.shape
    spread = count // sections
    rows = spread * (sub // tiles)
    span = spread * sub
    spots = [(y * sections + s, pl.ds((s * spread + y) * sub, sub)) for s in range(sections) for y in range(spread)]
    for n, spot in spots:
        wide_ref[spot, :] = in_ref[n].astype(F32)
    at = lambda s, k: pl.ds(s * span + k, rows, stride=tiles)
    spare = feats - (tiles - 1) * lanes
    more[0] = jnp.max(wide_ref[at(0, tiles - 1), :][:, spare:spare + 1]).astype(jnp.int32)
    pieces = []
    for s in range(sections):
        pieces.append(jnp.concatenate([wide_ref[at(s, k), :] for k in range(tiles)], axis=1)[:, :feats])
    chosen = []
    steps = select_steps(chosen, cols_ref[...], tokens, table_out.shape[0] // count, count, sections, slots)
    terms = part_terms(tab_ref[...], tokens)
    part = all_layers(pieces, gain_ref, wg_ref, wu_ref, wd_ref, steps)
    for unused in steps:
        pass
    cols, table = chosen
    terms_out[...] = terms
    picks_out[...] = row_picks(table, tokens)
    cols_out[...] = cols
    table_out[...] = table
    for s in range(sections):
        piece = part[:, s * feats:(s + 1) * feats]
        piece = jnp.concatenate([piece, jnp.zeros((rows, tiles * lanes - feats), F32)], axis=1)
        for k in range(tiles):
            wide_ref[at(s, k), :] = piece[:, k * lanes:(k + 1) * lanes]
    for n, spot in spots:
        out_ref[n] = wide_ref[spot, :].astype(BF16)


def part_terms(table, tokens):
    across = table.T[:8]
    chosen = iota((tokens, across.shape[1]), 0).astype(F32) + 1.0 == across[0:1]
    return jnp.concatenate([jnp.where(chosen, across[n:n + 1], 0.0) for n in (1, 2, 3)], axis=0).astype(BF16)


def add_parts(terms, parts, x, feats):
    tokens, padded = x.shape
    added = mm(terms, parts)
    added = added[:tokens] + added[tokens:2 * tokens] + added[2 * tokens:]
    return jnp.where(iota((tokens, padded), 1) < feats, x.astype(F32) + added, 0.0).astype(BF16)


def find_ready(cols, tokens, sections):
    per = cols.shape[0] // sections
    pick = (iota((cols.shape[0], tokens), 1).astype(F32) == cols[:, 0:1]).astype(F32)
    pending = cols[:, 4:5]
    layer = lambda v, l: v[l * per:(l + 1) * per]
    waits = [jnp.minimum(jnp.sum(layer(pick, l) * layer(pending, l), axis=0, keepdims=True), 1.0) for l in range(sections)]
    ahead, behind = [None] * sections, [None] * sections
    run_a = run_b = jnp.zeros((1, tokens), F32)
    for l in range(sections):
        ahead[l] = run_a
        run_a = run_a + waits[l]
        m = sections - 1 - l
        behind[m] = run_b
        run_b = run_b + waits[m]
    forward = iota((1, tokens), 1) < tokens // 2
    ready = []
    for l in range(sections):
        free = jnp.where(jnp.where(forward, ahead[l], behind[l]) == 0.0, waits[l], 0.0)
        ready.append(jnp.sum(layer(pick, l) * free, axis=-1, keepdims=True))
    return jnp.concatenate(ready, axis=0), pick, run_a


def values_of(cols, taken):
    lane = iota(cols.shape, 1)
    return jnp.where(taken & (lane < 4), jnp.where(lane == 0, cols + 1.0, cols), 0.0)


def select_steps(result, cols, tokens, kept, count, sections, slots):
    total = cols.shape[0]
    per = total // sections
    ready, pick, waits = find_ready(cols, tokens, sections)
    yield
    group_of = lambda v, size: jnp.floor((v.astype(F32) + 0.5) * (1.0 / size))
    row = iota((total, 1), 0)
    urgent = jnp.sum(pick * waits, axis=-1, keepdims=True) * slots + (slots - lax.rem(row, slots)).astype(F32)
    apart = 4.0 * slots * sections
    key = jnp.where(ready > 0.0, urgent, 0.0) + group_of(row, slots) * apart
    yield
    ahead = jnp.broadcast_to(key, (total, LANES)).T[0:1] - key
    rank = jnp.sum(jnp.where((ahead > 0.0) & (ahead < 0.5 * apart), 1.0, 0.0), axis=-1, keepdims=True)
    late = jnp.where(rank >= kept, ready, 0.0)
    yield
    held = []
    for l in range(sections):
        here = slice(l * per, (l + 1) * per)
        wait = jnp.sum(pick[here] * late[here], axis=0, keepdims=True)
        held.append(jnp.sum(pick[here] * wait, axis=-1, keepdims=True))
    yield
    taken = jnp.where(jnp.concatenate(held, axis=0) == 0.0, ready, 0.0)
    cols = jnp.where(iota((total, LANES), 1) == 4, cols - taken, cols)
    left = jnp.max(cols[:, 4:5], axis=0, keepdims=True)
    device = iota((count, total), 0)
    expert = group_of(device, GROUP * sections)
    layer = device.astype(F32) - sections * group_of(device, sections)
    window = count // (GROUP * sections)
    owner = (layer * window + expert == group_of(iota((count, total), 1), slots)).astype(BF16)
    yield
    tables = []
    for c in range(kept):
        mine = values_of(cols, (taken > 0.0) & (rank == c))
        tables.append(mm(owner, mine.astype(BF16)))
    table = jnp.concatenate(tables, axis=0)
    result[:] = cols, jnp.where(iota(table.shape, 1) == 4, left, table)


def select(*args):
    result = []
    for unused in select_steps(result, *args):
        pass
    return result


def row_picks(table, tokens):
    return (iota((table.shape[0], tokens), 1).astype(F32) + 1.0 == table[:, 0:1]).astype(BF16)


def pack_rows(picks, left, x, send_ref, wide_ref, feats, tiles):
    count, sub, lanes = send_ref.shape
    kept = sub // tiles
    rows = jnp.where(iota((kept * count, x.shape[1]), 1) == feats, left, mm(picks, x))
    for c in range(kept):
        for k in range(tiles):
            wide_ref[pl.ds(c * tiles + k, count, stride=sub), :] = rows[c * count:(c + 1) * count, k * lanes:(k + 1) * lanes]
    send_ref[...] = wide_ref[...].reshape(count, sub, lanes).astype(BF16)


def table_kernel(x_ref, in_ref, more, x_out, cols_out, send_out, table_out, done_hbm, wide_ref, *, sections, feats, tiles):
    more[0] = 1
    count, slots, padded = in_ref.shape
    tokens = x_ref.shape[0]
    groups = count // GROUP
    window = groups // sections
    parts = in_ref[...].reshape(count * slots, padded)
    firsts = [(e * GROUP * sections + l) * slots for l in range(sections) for e in range(window)]
    meta = [parts[n:n + slots, feats:feats + 4].astype(F32) for n in firsts]
    meta = jnp.concatenate(meta, axis=0)
    lane = iota((groups * slots, LANES), 1)
    cols = jnp.where(lane == 0, meta[:, 0:1], 0.0)
    for n in (1, 2, 3):
        cols = jnp.where(lane == n, meta[:, n:n + 1], cols)
    cols = jnp.where((lane == 4) & (meta[:, 0:1] >= 0.0), 1.0, cols)
    ready, *unused = find_ready(cols, tokens, sections)
    mine = values_of(cols, ready > 0.0)
    order = [l * window + e for e in range(window) for n in range(GROUP) for l in range(sections)]
    table = jnp.concatenate([mine[g * slots:(g + 1) * slots] for g in order], axis=0)
    x = add_parts(part_terms(table, tokens), parts, x_ref[...], feats)
    x_out[...] = x
    cols = jnp.where(lane == 4, cols - ready, cols)
    cols, table = select(cols, tokens, table_out.shape[0] // count, count, sections, slots)
    cols_out[...] = cols
    table_out[...] = table
    pack_rows(row_picks(table, tokens), table[:, 4:5], x, send_out, wide_ref, feats, tiles)


def update_kernel(
    more, x_ref, in_ref, terms_ref, picks_ref, next_ref, done_in,
    x_out, send_out, done_hbm, in_wide, out_wide, done_ref, sems, *, feats, tiles
):
    count, sub, lanes = in_ref.shape
    in_wide[...] = in_ref[...].astype(F32).reshape(count * sub, lanes)
    at = lambda c, k: pl.ds(c * tiles + k, count, stride=sub)
    parts = jnp.concatenate(
        [jnp.concatenate([in_wide[at(c, k), :] for k in range(tiles)], axis=1) for c in range(sub // tiles)], axis=0
    ).astype(BF16)
    x = add_parts(terms_ref[...], parts, x_ref[...], feats)
    x_out[...] = x

    @pl.when(more[0] > 0)
    def forward():
        pack_rows(picks_ref[...], next_ref[:, 4:5], x, send_out, out_wide, feats, tiles)

    @pl.when(more[0] <= 0)
    def finish():
        done_ref[...] = x[:, :feats]
        done, = start(pltpu.make_async_copy(done_ref, done_hbm, sems.at[0]))
        done.wait()


def call(kernel, out_shape, in_spaces, out_spaces, name, scratch=(), limit=24 * 2**20, aliases={}):
    spec = lambda space: pl.BlockSpec(memory_space=space)
    single = not isinstance(out_shape, (list, tuple))
    return pl.pallas_call(
        kernel,
        out_shape=out_shape,
        in_specs=[spec(s) for s in in_spaces],
        out_specs=spec(out_spaces[0]) if single else [spec(s) for s in out_spaces],
        scratch_shapes=list(scratch),
        input_output_aliases=aliases,
        compiler_params=pltpu.CompilerParams(vmem_limit_bytes=limit),
        name=name,
    )


def on_device(entering, norm_gain, w_gate, w_up, w_down, route_ids, route_scores):
    sections = lax.axis_size("section")
    spread = lax.axis_size("expert")
    window = spread // GROUP
    ways, micro, tokens, width = entering.shape
    everyone = ways * micro * tokens
    slots = ways * micro * CAP
    feats = width // sections
    tiles = feats // LANES + 1
    padded = tiles * LANES
    devices = sections * spread
    kept = max(1, 8 // tiles)
    by_token = lambda v: jnp.swapaxes(v[:, :, 0], 2, 3).reshape(ways * micro, v.shape[-1], tokens)
    in_hbm = lambda v: pltpu.with_memory_space_constraint(v, HBM)
    in_vmem = lambda v: pltpu.with_memory_space_constraint(v, VMEM)
    sds = jax.ShapeDtypeStruct
    dma = pltpu.SemaphoreType.DMA

    place = lax.axis_index(PLACES).astype(jnp.int32).reshape(1)
    flat = in_hbm(entering.reshape(everyone, width))
    ids, scores = in_hbm(by_token(route_ids)), in_hbm(by_token(route_scores))
    wg, wu, wd = [in_hbm(v[0]) for v in (w_gate, w_up, w_down)]
    resident = lambda v: VMEM(v.shape, v.dtype)

    early = wd.shape[0] // EARLY
    *rows, begun = call(
        functools.partial(route_kernel, window=window, slots=slots, early=early),
        [sds((slots, width + LANES), BF16)] * spread + [resident(wd)],
        [SMEM] + [HBM] * 4,
        [VMEM] * (spread + 1),
        "route",
        scratch=[
            VMEM(ids.shape, ids.dtype),
            VMEM(scores.shape, scores.dtype),
            VMEM((everyone, width), BF16),
            VMEM((window, slots, width + LANES), BF16),
            dma((4,)),
        ],
    )(place, ids, scores, flat, wd)
    received = [rows[0]] + [
        lax.ppermute(rows[k], "expert", [(y, y ^ k) for y in range(spread)]) for k in reversed(range(1, spread))
    ][::-1]
    reach = max(s * feats % LANES for s in range(sections)) + feats
    span = -(-reach // LANES) * LANES
    state = sds((everyone, padded), BF16)
    own, wg, wu = call(
        functools.partial(load_kernel, spread=spread, feats=feats),
        [state, resident(wg), resident(wu)],
        [SMEM] + [HBM] * 3,
        [VMEM] * 3,
        "load",
        scratch=[VMEM((everyone, span), BF16), dma((3,))],
    )(place, flat, wg, wu)
    wg, wu = in_vmem(wg), in_vmem(wu)
    message = sds((devices, slots, padded), BF16)
    compact = sds((devices, kept * tiles, LANES), BF16)
    swap = lambda v: lax.all_to_all(v, AXES, split_axis=0, concat_axis=0, tiled=True)
    parts, wd = call(
        functools.partial(first_kernel, sections=sections, feats=feats, early=early),
        [message, resident(wd)],
        [SMEM] + [VMEM] * 3 + [HBM] + [VMEM] * (1 + spread),
        [VMEM] * 2,
        "first",
        aliases={5: 1},
        scratch=[dma((1,))],
    )(place, norm_gain, wg, wu, wd, in_vmem(begun), *received)
    experts = (norm_gain, wg, wu, in_vmem(wd))
    parts, own = lax.optimization_barrier((parts, own))
    flag = SMEM((1,), jnp.int32)
    table_of = VMEM((devices * kept, LANES), F32)
    wide = VMEM((devices * kept * tiles, LANES), F32)
    cols_of = VMEM((devices // GROUP * slots, LANES), F32)
    whole = HBM((everyone, feats), BF16)
    sizes = dict(sections=sections, feats=feats, tiles=tiles)
    carry = call(
        functools.partial(table_kernel, **sizes),
        [flag, state, cols_of, compact, table_of, whole],
        [VMEM] * 2,
        [SMEM] + [VMEM] * 4 + [HBM],
        "table",
        scratch=[wide],
    )(own, swap(parts))

    def turn(carry):
        unused, x, cols, packed, table, done = lax.optimization_barrier(carry)
        parts, more, cols, table, terms, picks = call(
            functools.partial(round_kernel, tokens=everyone, slots=slots, **sizes),
            [compact, flag, cols_of, table_of, VMEM((3 * everyone, devices * kept), BF16), VMEM((devices * kept, everyone), BF16)],
            [VMEM] * 7,
            [VMEM, SMEM] + [VMEM] * 4,
            "round",
            aliases={5: 2, 6: 3},
            scratch=[wide],
        )(*experts, swap(packed), in_vmem(cols), in_vmem(table))
        x, packed, done = call(
            functools.partial(update_kernel, feats=feats, tiles=tiles),
            [state, compact, whole],
            [SMEM] + [VMEM] * 5 + [HBM],
            [VMEM] * 2 + [HBM],
            "update",
            aliases={1: 0, 6: 2},
            scratch=[wide, wide, VMEM((everyone, feats), BF16), dma((1,))],
        )(more, x, swap(parts), in_vmem(terms), in_vmem(picks), in_vmem(table), in_hbm(done))
        return more, x, cols, packed, table, done

    done = lax.while_loop(lambda c: c[0][0] > 0, turn, tuple(carry))[5]
    return done.reshape(ways, micro, tokens, feats)


def solution(mesh):
    return jax.shard_map(
        on_device,
        mesh=mesh,
        in_specs=(
            P(None, None, "expert", None),
            P("section", None),
            P("section", None, "expert"),
            P("section", None, "expert"),
            P("section", "expert", None),
            P(None, None, "section", "expert", None),
            P(None, None, "section", "expert", None),
        ),
        out_specs=P(None, None, "expert", "section"),
        check_vma=False,
    )
```
